32 devices in a mesh: groups: 2 (over y), tm: 4 (over z), chan: 2 (over x), sub: 2 (over core).
Axes of the slice: x: 2, y: 2, z: 4, core: 2. Of those that a mesh axis runs over, the one named last changes fastest.
Arguments:
- traces: bfloat16 [512, 8192], P(('chan', 'sub'), ('groups', 'tm')), parts along dimension 1, may hold values from -60 to 60
- templates: bfloat16 [32, 512, 256], P('tm', ('chan', 'sub')), may hold values from -6 to 6
- channel_mask: int32 [32, 512], P('tm', ('chan', 'sub')), may hold values from 0 to 1
Outputs:
- scores: float32 [32, 8192], P(('chan', 'sub'), ('groups', 'tm')), parts along dimension 1
The draws below stay inside these ranges and needn't reach their ends.
There are 2 independent parts, one for each index of `groups`. The reference program is written for one: setup_inputs(seed, part) draws one part's arguments, and reference() takes and returns one part's arrays. A program takes and returns all parts, laid end to end along the dimension named above; an argument that names none is the same for every part. Nothing has to cross between parts.
All inputs are finite; a program needn't handle non-finite values.
Results may differ from the reference program's by a relative error of at most 0.0003.
Values may be sent and summed in bfloat16 or wider, within the bound.
A program may use at most 64 MiB of HBM per device.

```python
import jax
import jax.numpy as jnp
from jax import lax

S = 256
TEMPLATES = 32
CHANNELS = 512
TIME = 4096


def draw_traces(key, part):
    scale_key, envelope_key, noise_key = jax.random.split(key, 3)
    chan_scale = jnp.exp(jax.random.uniform(scale_key, (CHANNELS, 1), jnp.float32, 0.0, 2.3))
    envelope = jnp.exp(jax.random.uniform(envelope_key, (1, TIME // 64), jnp.float32, -0.7, 0.7))
    envelope = jnp.repeat(envelope, 64, axis=1)
    noise = jax.random.normal(noise_key, (CHANNELS, TIME), jnp.float32)
    values = jnp.clip(noise * chan_scale * envelope, -60.0, 60.0)
    return values.astype(jnp.bfloat16)


def mask_pattern(key):
    mask_key, drop_key = jax.random.split(jax.random.fold_in(key, 7))
    used = jax.random.randint(mask_key, (TEMPLATES, CHANNELS), 0, 2, jnp.int32)
    dropped = jax.random.randint(drop_key, (TEMPLATES, CHANNELS), 0, 16, jnp.int32)
    silent = used * (dropped == 0).astype(jnp.int32)
    return (used, silent)


def draw_channel_mask(key, part):
    used, silent = mask_pattern(key)
    return used


def draw_templates(key, part):
    used, silent = mask_pattern(key)
    wave_key = jax.random.fold_in(key, 11)
    values = jnp.clip(jax.random.normal(wave_key, (TEMPLATES, CHANNELS, S), jnp.float32), -6.0, 6.0)
    keep = (1 - silent).astype(jnp.float32)[:, :, None]
    return (values * keep).astype(jnp.bfloat16)


def setup_inputs(seed: int = 0, part: int = 0) -> dict:
    arg_keys = jax.random.split(jax.random.key(seed), 4)
    part_splits = jax.random.split(jax.random.fold_in(arg_keys[3], part), 4)
    return {
        "traces": draw_traces(jax.random.fold_in(jax.random.fold_in(arg_keys[3], part), 71), part),
        "templates": draw_templates(jax.random.fold_in(arg_keys[3], 71), part),
        "channel_mask": draw_channel_mask(jax.random.fold_in(arg_keys[3], 71), part),
    }


EPSILON = 1e-06

def reference(traces, templates, channel_mask):
    signal = traces.astype(jnp.float32)
    wrapped = jnp.concatenate([signal, signal[:, :S]], 1)
    squares = wrapped * wrapped
    masked = templates * channel_mask.astype(jnp.bfloat16)[:, :, None]
    weights = masked.astype(jnp.float32)

    def advance(state_tuple, offset):
        correlation, chan_energy = state_tuple
        window = lax.dynamic_slice_in_dim(wrapped, offset, TIME, 1)
        lag_weights = lax.dynamic_index_in_dim(weights, offset, 2, keepdims=False)
        correlation = correlation + jnp.dot(lag_weights, window, precision=lax.Precision.HIGHEST, preferred_element_type=jnp.float32)
        chan_energy = chan_energy + lax.dynamic_slice_in_dim(squares, offset, TIME, 1)
        return ((correlation, chan_energy), None)
    initial = (jnp.zeros((TEMPLATES, TIME), jnp.float32), jnp.zeros((CHANNELS, TIME), jnp.float32))
    (correlation, chan_energy), _ = lax.scan(advance, initial, jnp.arange(S, dtype=jnp.int32))
    active = channel_mask.astype(jnp.float32)
    template_energy = lax.optimization_barrier(jnp.sum(weights * weights, axis=(1, 2)))
    active_count = lax.optimization_barrier(jnp.sum(active, axis=1))
    energy = jnp.dot(active, chan_energy, precision=lax.Precision.HIGHEST, preferred_element_type=jnp.float32)
    factor = jnp.sqrt(S * active_count)[:, None]
    return correlation * factor / jnp.sqrt(energy * template_energy[:, None] + EPSILON)
```

```python
import functools

import jax
import jax.numpy as jnp
from jax import lax
from jax.experimental import pallas as pl
from jax.experimental.pallas import tpu as pltpu
from jax.sharding import PartitionSpec as P

EPSILON = 1e-06
MESH = pl.DeviceIdType.MESH
LANES = 128
FINE = 32
NT = (((1,), (1,)), ((), ()))


def kernel(sizes, x_ref, w_ref, m_ref, o_ref, xt, af, ab, acc, rb, mk, pb, tp, fp, eh, es, ew,
           recv_sem, right_sem, left_sem, out_sem, in_sem, mask_sem, maskin_sem,
           pow_sem, powin_sem, te_sem, tein_sem, fac_sem, facin_sem, head_sem):
    tm, chan_n, sub_n = sizes
    cs_n = chan_n * sub_n
    me = lax.axis_index("tm")
    my_chan = lax.axis_index("chan")
    my_sub = lax.axis_index("sub")
    my_cs = my_chan * sub_n + my_sub
    chans, tile = x_ref.shape
    rows, _, span = w_ref.shape
    blocks = tm // cs_n
    coarse = span // FINE
    total = tm * tile
    n = tile // span
    owner = me // blocks
    first = me * n

    def remote(src, dst, send, recv, to):
        return pltpu.make_async_remote_copy(
            src_ref=src, dst_ref=dst, send_sem=send, recv_sem=recv,
            device_id=to, device_id_type=MESH)

    def peer(d):
        return {"tm": lax.rem(me + d, tm)}

    def cs_place(c):
        return {"chan": c // sub_n, "sub": c % sub_n}

    barrier = pltpu.get_barrier_semaphore()
    for d in range(1, tm):
        pl.semaphore_signal(barrier, inc=1, device_id=peer(d), device_id_type=MESH)
    for d in range(1, cs_n):
        pl.semaphore_signal(barrier, inc=1, device_id=cs_place(lax.rem(my_cs + d, cs_n)),
                            device_id_type=MESH)

    xt[pl.ds(me * tile, tile), :] = jnp.transpose(x_ref[...])
    mask = m_ref[...].astype(jnp.float32)
    mk[me] = mask
    pl.semaphore_wait(barrier, tm - 1 + cs_n - 1)

    def relay(c, to, sem):
        part = pl.ds(pl.multiple_of(c * span, span), span)
        return remote(xt.at[part, :], xt.at[part, :], sem.at[c], recv_sem.at[c], {"tm": to})

    for k in range(n):
        @pl.when(me < tm - 1)
        def _():
            relay(first + n - 1 - k, me + 1, right_sem).start()

        @pl.when(me > 0)
        def _():
            relay(first + k, me - 1, left_sem).start()

    def mask_copy(d):
        return remote(mk.at[me], mk.at[me], mask_sem.at[d], maskin_sem.at[me], peer(d))

    for d in range(1, tm):
        mask_copy(d).start()

    for k in range(rows):
        wave = jnp.transpose(w_ref[k].astype(jnp.float32)) * mask[k : k + 1, :]
        tp[my_cs, k : k + 1, 0:chans] = jnp.sum(wave * wave, axis=0, keepdims=True)
        for g in range(coarse):
            af[g, pl.ds(k, FINE, stride=rows), :] = wave[g * FINE : (g + 1) * FINE, :]
    for g in range(coarse):
        ab[:, g * chans : (g + 1) * chans] = af[g].astype(jnp.bfloat16)
    tp[my_cs, :, chans : 2 * chans] = mask

    def te_copy():
        return remote(tp.at[my_cs], tp.at[my_cs], te_sem, tein_sem.at[my_cs], cs_place(owner))

    @pl.when(my_cs != owner)
    def _():
        te_copy().start()

    acc[...] = jnp.zeros_like(acc)

    def add_products(right, start, before):
        p = lax.dot_general(ab[...], right, NT, preferred_element_type=jnp.float32)
        pad = jnp.zeros((rows, LANES), jnp.float32)
        out = jnp.concatenate([pad, p[:rows]], 1)
        for b in range(1, FINE):
            one = jnp.concatenate([pad, p[b * rows : (b + 1) * rows]], 1)
            out = out + pltpu.roll(one, span + LANES - b, 1)
        acc[:, pl.ds(before, LANES)] += out[:, :LANES]
        acc[:, pl.ds(start, span)] += out[:, LANES:]

    def process(c):
        start = pl.multiple_of(c * span, span)
        before = pl.multiple_of(lax.rem(start + total - LANES, total), LANES)
        right = jnp.concatenate(
            [xt[pl.ds(pl.multiple_of(start + FINE * g, FINE), span), :] for g in range(coarse)], 1)
        add_products(right, start, before)

    def close():
        start = total - span
        right = jnp.concatenate(
            [jnp.concatenate([xt[start + FINE * g : total, :], xt[0 : FINE * g, :]], 0)
             if g else xt[start:total, :] for g in range(coarse)], 1)
        add_products(right, start, start - LANES)

    def out_copy(c):
        at = pl.ds(pl.multiple_of(c * span, span), span)
        to = pl.ds(pl.multiple_of(lax.rem(c, n) * span, span), span)
        return remote(acc.at[:, at], rb.at[me % blocks, my_cs, :, to], out_sem.at[c],
                      in_sem.at[me % blocks, my_cs, lax.rem(c, n)],
                      {"tm": c // n, **cs_place(owner)})

    def is_local(c):
        return jnp.logical_and(c // n == me, my_cs == owner)

    def deliver(c):
        @pl.when(is_local(c))
        def _():
            at = pl.ds(pl.multiple_of(c * span, span), span)
            to = pl.ds(pl.multiple_of(lax.rem(c, n) * span, span), span)
            rb[me % blocks, my_cs, :, to] = acc[:, at]

        @pl.when(jnp.logical_not(is_local(c)))
        def _():
            out_copy(c).start()

    def pow_copy(d):
        to = lax.rem(my_cs + d, cs_n)
        return remote(es.at[to], pb.at[my_cs], pow_sem.at[d], powin_sem.at[my_cs], cs_place(to))

    def power():
        for d in range(1, tm):
            who = lax.rem(me + d, tm)
            remote(mk.at[who], mk.at[who], mask_sem.at[0], maskin_sem.at[who],
                   {"tm": who}).wait_recv()
        masks = jnp.concatenate([mk[i] for i in range(tm)], 0).astype(jnp.bfloat16)
        x32 = xt[pl.ds(me * tile, tile), :].astype(jnp.float32)
        square = x32 * x32
        high = square.astype(jnp.bfloat16)
        low = (square - high.astype(jnp.float32)).astype(jnp.bfloat16)
        p = lax.dot_general(jnp.concatenate([masks, masks], 1), jnp.concatenate([high, low], 1),
                            NT, preferred_element_type=jnp.float32)
        for c in range(cs_n):
            es[c] = p[c * blocks * rows : (c + 1) * blocks * rows, :]
        pb[my_cs] = es[my_cs]
        for d in range(1, cs_n):
            pow_copy(d).start()

    def fac_copy(d):
        return remote(fp.at[me % blocks], fp.at[me % blocks], fac_sem.at[d],
                      facin_sem.at[me % blocks], peer(d))

    def template_sums():
        @pl.when(my_cs == owner)
        def _():
            for d in range(1, cs_n):
                who = lax.rem(my_cs + d, cs_n)
                remote(tp.at[who], tp.at[who], te_sem, tein_sem.at[who], cs_place(who)).wait_recv()
            t = tp[0]
            for c in range(1, cs_n):
                t = t + tp[c]
            te = jnp.sum(t[:, :chans], axis=1, keepdims=True)
            active = jnp.sum(t[:, chans:], axis=1, keepdims=True)
            lane = lax.broadcasted_iota(jnp.int32, (rows, LANES), 1)
            fp[me % blocks] = jnp.where(lane < LANES // 2, te, active)
            for d in range(1, tm):
                fac_copy(d).start()

    def head_copy():
        return remote(eh.at[0], eh.at[1], head_sem.at[0], head_sem.at[1],
                      {"tm": lax.rem(me + tm - 1, tm)})

    def windows():
        for d in range(1, cs_n):
            who = lax.rem(my_cs + d, cs_n)
            remote(es.at[who], pb.at[who], pow_sem.at[0], powin_sem.at[who],
                   cs_place(who)).wait_recv()
        p = pb[0]
        for c in range(1, cs_n):
            p = p + pb[c]
        p = jnp.concatenate([jnp.zeros((blocks * rows, span), jnp.float32), p], 1)
        by = 1
        while by < span:
            p = p + pltpu.roll(p, tile + span - by, 1)
            by *= 2
        eh[0] = p[:, :span]
        head_copy().start()
        ew[0] = p[:, span:]

    def norms():
        head_copy().wait_recv()
        for q in range(blocks):
            j = my_cs * blocks + q

            @pl.when(me != j)
            def _():
                remote(fp.at[q], fp.at[q], fac_sem.at[0], facin_sem.at[q], {"tm": j}).wait_recv()

            at = slice(q * rows, (q + 1) * rows)
            factor = jnp.sqrt(span * fp[q, :, LANES - 1 : LANES])
            energy = jnp.concatenate(
                [ew[0, at, : tile - span], ew[0, at, tile - span :] + eh[1, at, :]], 1)
            ew[1, at, :] = factor / jnp.sqrt(energy * fp[q, :, 0:1] + EPSILON)

    for k in range(n - 1):
        process(first + n - 2 - k)
        if k:
            deliver(first + n - 2 - k)

    left_n = n * me
    right_n = n * (tm - 1 - me)
    short = jnp.minimum(left_n, right_n)
    left_short = left_n < right_n

    def step(u, carry):
        paired = u < 2 * short
        on_short = jnp.logical_and(paired, lax.rem(u, 2) == 0)
        k = jnp.where(paired, u // 2, u - short)
        from_left = on_short == left_short
        c = jnp.where(from_left, first - 1 - k, first + n + k)

        @pl.when(from_left)
        def _():
            relay(c, me, right_sem).wait_recv()

            @pl.when(me < tm - 1)
            def _():
                relay(c, me + 1, right_sem).start()

        @pl.when(jnp.logical_not(from_left))
        def _():
            relay(c, me, left_sem).wait_recv()

            @pl.when(me > 0)
            def _():
                relay(c, me - 1, left_sem).start()

        process(jnp.where(from_left, c, c - 1))
        deliver(jnp.where(from_left, c, c - 2))

        @pl.when(u == 0)
        def _():
            power()

        @pl.when(u == 1)
        def _():
            template_sums()

        @pl.when(u == n)
        def _():
            windows()

        @pl.when(u == 2 * n)
        def _():
            norms()

        return carry

    lax.fori_loop(0, n * (tm - 1), step, 0)
    close()
    deliver(total // span - 2)
    deliver(total // span - 1)

    for q in range(blocks):
        for d in range(cs_n):
            who = lax.rem(my_cs + d, cs_n)
            for k in range(n):
                def arrive():
                    remote(acc.at[:, pl.ds(0, span)], rb.at[q, who, :, pl.ds(k * span, span)],
                           out_sem.at[0], in_sem.at[q, who, k], {"tm": lax.rem(me + 1, tm)}).wait_recv()

                if d:
                    arrive()
                else:
                    pl.when(me != my_cs * blocks + q)(arrive)
        at = slice(q * rows, (q + 1) * rows)
        result = rb[q, 0]
        for c in range(1, cs_n):
            result = result + rb[q, c]
        o_ref[at, :] = result * ew[1, at, :]

    def finish(c, carry):
        @pl.when(jnp.logical_and(me < tm - 1, c // n <= me))
        def _():
            relay(c, me, right_sem).wait_send()

        @pl.when(jnp.logical_and(me > 0, c // n >= me))
        def _():
            relay(c, me, left_sem).wait_send()

        @pl.when(jnp.logical_not(is_local(c)))
        def _():
            out_copy(c).wait_send()

        return carry

    lax.fori_loop(0, n * tm, finish, 0)
    for d in range(1, tm):
        mask_copy(d).wait_send()
    for d in range(1, cs_n):
        pow_copy(d).wait_send()

    @pl.when(my_cs != owner)
    def _():
        te_copy().wait_send()

    @pl.when(my_cs == owner)
    def _():
        for d in range(1, tm):
            fac_copy(d).wait_send()

    head_copy().wait_send()


def solution(mesh):
    tm, chan_n, sub_n = (mesh.shape[a] for a in ("tm", "chan", "sub"))
    cs_n = chan_n * sub_n
    blocks = tm // cs_n

    def on_device(traces, templates, channel_mask):
        chans, tile = traces.shape
        rows, _, span = templates.shape
        coarse = span // FINE
        total = tm * tile
        n = tile // span
        out_rows = blocks * rows
        vmem = pl.BlockSpec(memory_space=pltpu.VMEM)
        f32, bf16 = jnp.float32, jnp.bfloat16
        dma = pltpu.SemaphoreType.DMA
        return pl.pallas_call(
            functools.partial(kernel, (tm, chan_n, sub_n)),
            out_shape=jax.ShapeDtypeStruct((out_rows, tile), f32),
            in_specs=[vmem] * 3,
            out_specs=vmem,
            scratch_shapes=[
                pltpu.VMEM((total, chans), bf16),
                pltpu.VMEM((coarse, FINE * rows, chans), f32),
                pltpu.VMEM((FINE * rows, coarse * chans), bf16),
                pltpu.VMEM((rows, total), f32),
                pltpu.VMEM((blocks, cs_n, rows, tile), f32),
                pltpu.VMEM((tm, rows, chans), f32),
                pltpu.VMEM((cs_n, out_rows, tile), f32),
                pltpu.VMEM((cs_n, rows, 2 * chans), f32),
                pltpu.VMEM((blocks, rows, LANES), f32),
                pltpu.VMEM((2, out_rows, span), f32),
                pltpu.VMEM((cs_n, out_rows, tile), f32),
                pltpu.VMEM((2, out_rows, tile), f32),
                dma((n * tm,)), dma((n * tm,)), dma((n * tm,)), dma((n * tm,)),
                dma((blocks, cs_n, n)),
                dma((tm,)), dma((tm,)),
                dma((cs_n,)), dma((cs_n,)),
                dma(()), dma((cs_n,)),
                dma((tm,)), dma((blocks,)),
                dma((2,)),
            ],
            compiler_params=pltpu.CompilerParams(collective_id=0, has_side_effects=True),
        )(traces, templates, channel_mask)

    placed = (
        P(("chan", "sub"), ("groups", "tm")),
        P("tm", ("chan", "sub"), None),
        P("tm", ("chan", "sub")),
    )
    return jax.shard_map(
        on_device,
        mesh=mesh,
        in_specs=placed,
        out_specs=P(("chan", "sub"), ("groups", "tm")),
        check_vma=False,
    )
```

```python
import functools

import jax
import jax.numpy as jnp
from jax import lax
from jax.experimental import pallas as pl
from jax.experimental.pallas import tpu as pltpu
from jax.sharding import PartitionSpec as P

EPSILON = 1e-06
MESH = pl.DeviceIdType.MESH
LANES = 128
FINE = 32
NT = (((1,), (1,)), ((), ()))
PIECES = 4
LAG = 2


def is_outer(z, half):
    return (z % 2 == 0) == (z < half)


def kernel(sizes, x_ref, w_ref, m_ref, o_ref, xt, af, ab, acc, px, rb, mk, pb, tp, fp, eh, es, ew,
           recv_sem, right_sem, left_sem, part_sem, partin_sem, out_sem, in_sem, wave_sem,
           wavein_sem, pass_sem, mask_sem, maskin_sem,
           pow_sem, powin_sem, te_sem, tein_sem, fac_sem, facin_sem, head_sem):
    group_n, tm, chan_n, sub_n = sizes
    cs_n = chan_n * sub_n
    me = lax.axis_index("tm")
    my_chan = lax.axis_index("chan")
    my_sub = lax.axis_index("sub")
    my_cs = my_chan * sub_n + my_sub
    chans, tile = x_ref.shape
    rows, _, span = w_ref.shape
    blocks = tm // cs_n
    coarse = span // FINE
    total = tm * tile
    n = tile // span
    owner = me // blocks
    first = me * n
    last = n * tm - 1
    my_group = lax.axis_index("groups")
    depth = FINE * rows
    piece = depth // (group_n * PIECES)
    half = tm // 2
    partner = me + 1 - 2 * lax.rem(me, 2)
    moves = my_sub == 0
    outer = is_outer(me, half)
    gives = jnp.logical_and(outer, moves)
    takes = jnp.logical_and(jnp.logical_not(outer), moves)
    works = jnp.logical_not(gives)
    low_end = jnp.where(moves, 1, 0)
    high_end = tm - 1 - low_end
    switch = n
    behind = n - 1 + switch

    def remote(src, dst, send, recv, to):
        return pltpu.make_async_remote_copy(
            src_ref=src, dst_ref=dst, send_sem=send, recv_sem=recv,
            device_id=to, device_id_type=MESH)

    def peer(d):
        return {"tm": lax.rem(me + d, tm)}

    def cs_place(c):
        return {"chan": c // sub_n, "sub": c % sub_n}

    barrier = pltpu.get_barrier_semaphore()
    for d in range(1, tm):
        pl.semaphore_signal(barrier, inc=1, device_id=peer(d), device_id_type=MESH)
    for d in range(1, cs_n):
        pl.semaphore_signal(barrier, inc=1, device_id=cs_place(lax.rem(my_cs + d, cs_n)),
                            device_id_type=MESH)

    for d in range(1, group_n):
        pl.semaphore_signal(barrier, inc=1, device_id={"groups": lax.rem(my_group + d, group_n)},
                            device_id_type=MESH)

    xt[pl.ds(me * tile, tile), :] = jnp.transpose(x_ref[...])
    mask = m_ref[...].astype(jnp.float32)
    mk[me] = mask
    for k in range(rows):
        wave = jnp.transpose(w_ref[k].astype(jnp.float32)) * mask[k : k + 1, :]
        tp[my_cs, k : k + 1, 0:chans] = jnp.sum(wave * wave, axis=0, keepdims=True)
        for g in range(coarse):
            af[g, pl.ds(k, FINE, stride=rows), :] = wave[g * FINE : (g + 1) * FINE, :]
    for g in range(coarse):
        ab[0:depth, g * chans : (g + 1) * chans] = af[g].astype(jnp.bfloat16)
    tp[my_cs, :, chans : 2 * chans] = mask

    pl.semaphore_wait(barrier, tm - 1 + cs_n - 1 + group_n - 1)

    def wave_copy(p, to):
        at = (my_group * PIECES + p) * piece
        return remote(ab.at[pl.ds(pl.multiple_of(at, piece), piece), :],
                      ab.at[pl.ds(pl.multiple_of(depth + at, piece), piece), :],
                      wave_sem.at[p], wavein_sem.at[my_group, p], {"tm": to})

    def pass_copy(p, d):
        at = pl.ds(pl.multiple_of(depth + (my_group * PIECES + p) * piece, piece), piece)
        return remote(ab.at[at, :], ab.at[at, :], pass_sem.at[d, p], wavein_sem.at[my_group, p],
                      {"groups": lax.rem(my_group + d, group_n)})

    @pl.when(gives)
    def _():
        for p in range(PIECES):
            wave_copy(p, partner).start()

    def relay(c, to, sem):
        part = pl.ds(pl.multiple_of(c * span, span), span)
        return remote(xt.at[part, :], xt.at[part, :], sem.at[c], recv_sem.at[c], {"tm": to})

    for k in range(n):
        @pl.when(me < high_end)
        def _():
            relay(first + n - 1 - k, me + 1, right_sem).start()

        @pl.when(me > low_end)
        def _():
            relay(first + k, me - 1, left_sem).start()

    def mask_copy(d):
        return remote(mk.at[me], mk.at[me], mask_sem.at[d], maskin_sem.at[me], peer(d))

    for d in range(1, tm):
        mask_copy(d).start()

    def te_copy():
        return remote(tp.at[my_cs], tp.at[my_cs], te_sem, tein_sem.at[my_cs], cs_place(owner))

    @pl.when(my_cs != owner)
    def _():
        te_copy().start()

    acc[...] = jnp.zeros_like(acc)

    def spread(p, slot, start, before):
        pad = jnp.zeros((rows, LANES), jnp.float32)
        out = jnp.concatenate([pad, p[:rows]], 1)
        for b in range(1, FINE):
            one = jnp.concatenate([pad, p[b * rows : (b + 1) * rows]], 1)
            out = out + pltpu.roll(one, span + LANES - b, 1)
        acc[slot, :, pl.ds(before, LANES)] += out[:, :LANES]
        acc[slot, :, pl.ds(start, span)] += out[:, LANES:]

    def add_products(slots, right, start, before):
        low, high = slots[0] * depth, (slots[-1] + 1) * depth
        p = lax.dot_general(ab[low:high, :], right, NT, preferred_element_type=jnp.float32)
        for i, slot in enumerate(slots):
            spread(p[i * depth : (i + 1) * depth], slot, start, before)

    def process(c, slots):
        start = pl.multiple_of(c * span, span)
        before = pl.multiple_of(lax.rem(start + total - LANES, total), LANES)
        right = jnp.concatenate(
            [xt[pl.ds(pl.multiple_of(start + FINE * g, FINE), span), :] for g in range(coarse)], 1)
        add_products(slots, right, start, before)

    def close(slots):
        start = total - span
        right = jnp.concatenate(
            [jnp.concatenate([xt[start + FINE * g : total, :], xt[0 : FINE * g, :]], 0)
             if g else xt[start:total, :] for g in range(coarse)], 1)
        add_products(slots, right, start, start - LANES)

    def block_of(slot):
        return partner if slot else me

    def holder(slot):
        return block_of(slot) // blocks

    def columns(c):
        return pl.ds(pl.multiple_of(c * span, span), span)

    def part_copy(c, slot):
        return remote(acc.at[slot, :, columns(c)], px.at[slot, my_chan, :, columns(c)],
                      part_sem.at[slot, c], partin_sem.at[slot, my_chan, c],
                      {"chan": holder(slot) // sub_n})

    def out_copy(c, slot):
        q = block_of(slot) % blocks
        return remote(acc.at[slot, :, columns(c)], rb.at[q, my_sub, :, columns(lax.rem(c, n))],
                      out_sem.at[slot, c], in_sem.at[q, my_sub, lax.rem(c, n)],
                      {"tm": c // n, **cs_place(holder(slot))})

    def is_summer(slot):
        return my_chan == holder(slot) // sub_n

    def is_local(c, slot):
        return jnp.logical_and(c // n == me, my_cs == holder(slot))

    def hand(c, slot):
        @pl.when(jnp.logical_not(is_summer(slot)))
        def _():
            part_copy(c, slot).start()

    def deliver(c, slot):
        @pl.when(is_summer(slot))
        def _():
            value = acc[slot, :, columns(c)]
            for d in range(1, chan_n):
                who = lax.rem(my_chan + d, chan_n)
                remote(acc.at[slot, :, columns(c)], px.at[slot, who, :, columns(c)],
                       part_sem.at[slot, c], partin_sem.at[slot, who, c],
                       {"chan": who}).wait_recv()
                value = value + px[slot, who, :, columns(c)]

            @pl.when(is_local(c, slot))
            def _():
                rb[block_of(slot) % blocks, my_sub, :, columns(lax.rem(c, n))] = value

            @pl.when(jnp.logical_not(is_local(c, slot)))
            def _():
                acc[slot, :, columns(c)] = value
                out_copy(c, slot).start()

    def pow_copy(d):
        to = lax.rem(my_cs + d, cs_n)
        return remote(es.at[to], pb.at[my_cs], pow_sem.at[d], powin_sem.at[my_cs], cs_place(to))

    def power():
        for d in range(1, tm):
            who = lax.rem(me + d, tm)
            remote(mk.at[who], mk.at[who], mask_sem.at[0], maskin_sem.at[who],
                   {"tm": who}).wait_recv()
        masks = jnp.concatenate([mk[i] for i in range(tm)], 0).astype(jnp.bfloat16)
        x32 = xt[pl.ds(me * tile, tile), :].astype(jnp.float32)
        square = x32 * x32
        high = square.astype(jnp.bfloat16)
        low = (square - high.astype(jnp.float32)).astype(jnp.bfloat16)
        p = lax.dot_general(jnp.concatenate([masks, masks], 1), jnp.concatenate([high, low], 1),
                            NT, preferred_element_type=jnp.float32)
        for c in range(cs_n):
            es[c] = p[c * blocks * rows : (c + 1) * blocks * rows, :]
        pb[my_cs] = es[my_cs]
        for d in range(1, cs_n):
            pow_copy(d).start()

    def fac_copy(d):
        return remote(fp.at[me % blocks], fp.at[me % blocks], fac_sem.at[d],
                      facin_sem.at[me % blocks], peer(d))

    def template_sums():
        @pl.when(my_cs == owner)
        def _():
            for d in range(1, cs_n):
                who = lax.rem(my_cs + d, cs_n)
                remote(tp.at[who], tp.at[who], te_sem, tein_sem.at[who], cs_place(who)).wait_recv()
            t = tp[0]
            for c in range(1, cs_n):
                t = t + tp[c]
            te = jnp.sum(t[:, :chans], axis=1, keepdims=True)
            active = jnp.sum(t[:, chans:], axis=1, keepdims=True)
            lane = lax.broadcasted_iota(jnp.int32, (rows, LANES), 1)
            fp[me % blocks] = jnp.where(lane < LANES // 2, te, active)
            for d in range(1, tm):
                fac_copy(d).start()

    def head_copy():
        return remote(eh.at[0], eh.at[1], head_sem.at[0], head_sem.at[1],
                      {"tm": lax.rem(me + tm - 1, tm)})

    def windows():
        for d in range(1, cs_n):
            who = lax.rem(my_cs + d, cs_n)
            remote(es.at[who], pb.at[who], pow_sem.at[0], powin_sem.at[who],
                   cs_place(who)).wait_recv()
        p = pb[0]
        for c in range(1, cs_n):
            p = p + pb[c]
        p = jnp.concatenate([jnp.zeros((blocks * rows, span), jnp.float32), p], 1)
        by = 1
        while by < span:
            p = p + pltpu.roll(p, tile + span - by, 1)
            by *= 2
        eh[0] = p[:, :span]
        head_copy().start()
        ew[0] = p[:, span:]

    def norms():
        head_copy().wait_recv()
        for q in range(blocks):
            j = my_cs * blocks + q

            @pl.when(me != j)
            def _():
                remote(fp.at[q], fp.at[q], fac_sem.at[0], facin_sem.at[q], {"tm": j}).wait_recv()

            at = slice(q * rows, (q + 1) * rows)
            factor = jnp.sqrt(span * fp[q, :, LANES - 1 : LANES])
            energy = jnp.concatenate(
                [ew[0, at, : tile - span], ew[0, at, tile - span :] + eh[1, at, :]], 1)
            ew[1, at, :] = factor / jnp.sqrt(energy * fp[q, :, 0:1] + EPSILON)

    left_n = jnp.where(me <= high_end, n * me, 0)
    right_n = jnp.where(me >= low_end, n * (tm - 1 - me), 0)
    short = jnp.minimum(left_n, right_n)
    left_short = left_n < right_n
    lead = jnp.where(takes, switch, 0)

    def arrival(u):
        v = u - lead
        paired = jnp.logical_and(v >= 0, v < 2 * short)
        on_short = jnp.logical_and(paired, lax.rem(jnp.maximum(v, 0), 2) == 0)
        k = jnp.where(v < 0, u, jnp.where(paired, v // 2 + jnp.where(on_short, 0, lead), u - short))
        from_left = on_short == left_short
        return from_left, jnp.where(from_left, first - 1 - k, first + n + k)

    def made(u):
        from_left, c = arrival(u)
        return jnp.where(from_left, c, c - 1)

    def ended(u):
        from_left, c = arrival(u)
        return jnp.where(from_left, c, c - 2)

    def earlier(i):
        own = i < n - 1
        u = jnp.maximum(i - (n - 1), 0)
        return jnp.where(own, first + n - 2 - i, made(u)), jnp.where(own, first + n - 2 - i, ended(u))

    @pl.when(works)
    def _():
        for k in range(n - 1):
            process(first + n - 2 - k, (0,))
            if k:
                hand(first + n - 2 - k, 0)

    def late(u):
        return jnp.logical_and(takes, u >= switch)

    def second(u, act):
        i = u - switch

        @pl.when(jnp.logical_and(late(u), jnp.logical_and(i >= 1, i < behind)))
        def _():
            act(earlier(i)[1], 1)

        @pl.when(jnp.logical_and(late(u), i >= 2))
        def _():
            act(ended(u), 1)

        @pl.when(jnp.logical_and(late(u), i == behind - 1))
        def _():
            act(ended(switch), 1)
            act(ended(switch + 1), 1)

    steps = n * (tm - 1)

    def step(u, carry):
        live = u < left_n + right_n
        from_left, c = arrival(u)

        @pl.when(jnp.logical_and(takes, u < PIECES))
        def _():
            remote(ab.at[pl.ds(0, piece), :], ab.at[pl.ds(0, piece), :], wave_sem.at[0],
                   wavein_sem.at[my_group, u], {"tm": partner}).wait_recv()
            for d in range(1, group_n):
                pass_copy(u, d).start()

        @pl.when(jnp.logical_and(live, from_left))
        def _():
            relay(c, me, right_sem).wait_recv()

            @pl.when(me < high_end)
            def _():
                relay(c, me + 1, right_sem).start()

        @pl.when(jnp.logical_and(live, jnp.logical_not(from_left)))
        def _():
            relay(c, me, left_sem).wait_recv()

            @pl.when(me > low_end)
            def _():
                relay(c, me - 1, left_sem).start()

        @pl.when(jnp.logical_and(takes, u == switch))
        def _():
            for d in range(1, group_n):
                who = lax.rem(my_group + d, group_n)
                for p in range(PIECES):
                    remote(ab.at[pl.ds(0, piece), :], ab.at[pl.ds(0, piece), :], wave_sem.at[0],
                           wavein_sem.at[who, p], {"groups": who}).wait_recv()

        @pl.when(jnp.logical_and(works, jnp.logical_not(late(u))))
        def _():
            process(made(u), (0,))

        @pl.when(jnp.logical_and(late(u), u < switch + behind))
        def _():
            process(made(u), (0, 1))
            process(earlier(u - switch)[0], (1,))

        @pl.when(jnp.logical_and(late(u), u >= switch + behind))
        def _():
            process(made(u), (0, 1))

        @pl.when(works)
        def _():
            hand(ended(u), 0)

            @pl.when(u < n - 2)
            def _():
                deliver(first + n - 3 - u, 0)

            @pl.when(u >= LAG)
            def _():
                deliver(ended(u - LAG), 0)

        second(u, hand)

        @pl.when(u >= LAG)
        def _():
            second(u - LAG, deliver)

        @pl.when(u == 0)
        def _():
            power()

        @pl.when(u == 1)
        def _():
            template_sums()

        @pl.when(u == n)
        def _():
            windows()

        @pl.when(u == 2 * n)
        def _():
            norms()

        return carry

    lax.fori_loop(0, steps, step, 0)

    @pl.when(takes)
    def _():
        close((0, 1))

    @pl.when(jnp.logical_and(works, jnp.logical_not(takes)))
    def _():
        close((0,))

    @pl.when(works)
    def _():
        hand(last - 1, 0)
        hand(last, 0)

    @pl.when(takes)
    def _():
        hand(last - 1, 1)
        hand(last, 1)

    @pl.when(works)
    def _():
        for u in range(steps - LAG, steps):
            deliver(ended(u), 0)

    for u in range(steps - LAG, steps):
        second(u, deliver)

    @pl.when(works)
    def _():
        deliver(last - 1, 0)
        deliver(last, 0)

    @pl.when(takes)
    def _():
        deliver(last - 1, 1)
        deliver(last, 1)

    for q in range(blocks):
        b = my_cs * blocks + q
        b_outer = is_outer(b, half)
        for slot in range(sub_n):
            source = jnp.where(b_outer, b + 1 - 2 * lax.rem(b, 2), b) if slot == 0 else b

            @pl.when(jnp.logical_not(jnp.logical_and(my_sub == slot, source == me)))
            def _():
                for k in range(n):
                    remote(acc.at[0, :, pl.ds(0, span)],
                           rb.at[q, slot, :, pl.ds(k * span, span)], out_sem.at[0, 0],
                           in_sem.at[q, slot, k], {"tm": lax.rem(me + 1, tm)}).wait_recv()

        at = slice(q * rows, (q + 1) * rows)
        result = rb[q, 0]
        for c in range(1, sub_n):
            result = result + rb[q, c]
        o_ref[at, :] = result * ew[1, at, :]

    def finish(c, carry):
        @pl.when(jnp.logical_and(me < high_end, c // n <= me))
        def _():
            relay(c, me, right_sem).wait_send()

        @pl.when(jnp.logical_and(me > low_end, c // n >= me))
        def _():
            relay(c, me, left_sem).wait_send()

        for slot in range(2):
            mine = takes if slot else works

            @pl.when(jnp.logical_and(mine, jnp.logical_not(is_summer(slot))))
            def _():
                part_copy(c, slot).wait_send()

            @pl.when(jnp.logical_and(jnp.logical_and(mine, is_summer(slot)),
                                     jnp.logical_not(is_local(c, slot))))
            def _():
                out_copy(c, slot).wait_send()

        return carry

    lax.fori_loop(0, n * tm, finish, 0)
    for p in range(PIECES):
        @pl.when(gives)
        def _():
            wave_copy(p, partner).wait_send()

        @pl.when(takes)
        def _():
            for d in range(1, group_n):
                pass_copy(p, d).wait_send()

    for d in range(1, tm):
        mask_copy(d).wait_send()
    for d in range(1, cs_n):
        pow_copy(d).wait_send()

    @pl.when(my_cs != owner)
    def _():
        te_copy().wait_send()

    @pl.when(my_cs == owner)
    def _():
        for d in range(1, tm):
            fac_copy(d).wait_send()

    head_copy().wait_send()


def solution(mesh):
    group_n, tm, chan_n, sub_n = (mesh.shape[a] for a in ("groups", "tm", "chan", "sub"))
    cs_n = chan_n * sub_n
    blocks = tm // cs_n

    def on_device(traces, templates, channel_mask):
        chans, tile = traces.shape
        rows, _, span = templates.shape
        coarse = span // FINE
        total = tm * tile
        n = tile // span
        out_rows = blocks * rows
        vmem = pl.BlockSpec(memory_space=pltpu.VMEM)
        f32, bf16 = jnp.float32, jnp.bfloat16
        dma = pltpu.SemaphoreType.DMA
        return pl.pallas_call(
            functools.partial(kernel, (group_n, tm, chan_n, sub_n)),
            out_shape=jax.ShapeDtypeStruct((out_rows, tile), f32),
            in_specs=[vmem] * 3,
            out_specs=vmem,
            scratch_shapes=[
                pltpu.VMEM((total, chans), bf16),
                pltpu.VMEM((coarse, FINE * rows, chans), f32),
                pltpu.VMEM((2 * FINE * rows, coarse * chans), bf16),
                pltpu.VMEM((2, rows, total), f32),
                pltpu.VMEM((2, chan_n, rows, total), f32),
                pltpu.VMEM((blocks, sub_n, rows, tile), f32),
                pltpu.VMEM((tm, rows, chans), f32),
                pltpu.VMEM((cs_n, out_rows, tile), f32),
                pltpu.VMEM((cs_n, rows, 2 * chans), f32),
                pltpu.VMEM((blocks, rows, LANES), f32),
                pltpu.VMEM((2, out_rows, span), f32),
                pltpu.VMEM((cs_n, out_rows, tile), f32),
                pltpu.VMEM((2, out_rows, tile), f32),
                dma((n * tm,)), dma((n * tm,)), dma((n * tm,)),
                dma((2, n * tm)), dma((2, chan_n, n * tm)),
                dma((2, n * tm)), dma((blocks, sub_n, n)),
                dma((PIECES,)), dma((group_n, PIECES)), dma((group_n, PIECES)),
                dma((tm,)), dma((tm,)),
                dma((cs_n,)), dma((cs_n,)),
                dma(()), dma((cs_n,)),
                dma((tm,)), dma((blocks,)),
                dma((2,)),
            ],
            compiler_params=pltpu.CompilerParams(collective_id=0, has_side_effects=True),
        )(traces, templates, channel_mask)

    placed = (
        P(("chan", "sub"), ("groups", "tm")),
        P("tm", ("chan", "sub"), None),
        P("tm", ("chan", "sub")),
    )
    return jax.shard_map(
        on_device,
        mesh=mesh,
        in_specs=placed,
        out_specs=P(("chan", "sub"), ("groups", "tm")),
        check_vma=False,
    )
```

```python
import functools

import jax
import jax.numpy as jnp
from jax import lax
from jax.experimental import pallas as pl
from jax.experimental.pallas import tpu as pltpu
from jax.sharding import PartitionSpec as P

EPSILON = 1e-06
MESH = pl.DeviceIdType.MESH
LANES = 128
FINE = 32
NT = (((1,), (1,)), ((), ()))
PIECES = 4
POWER_AT = 1


def is_outer(z, half):
    return (z % 2 == 0) == (z < half)


def kernel(sizes, x_ref, w_ref, m_ref, o_ref, xt, af, ab, acc, rb, mk, pb, tp, fp, eh, es, ew,
           recv_sem, right_sem, left_sem, out_sem, in_sem, wave_sem,
           wavein_sem, pass_sem, mask_sem, maskin_sem,
           pow_sem, powin_sem, te_sem, tein_sem, fac_sem, facin_sem, head_sem):
    group_n, tm, chan_n, sub_n = sizes
    cs_n = chan_n * sub_n
    me = lax.axis_index("tm")
    my_chan = lax.axis_index("chan")
    my_sub = lax.axis_index("sub")
    my_cs = my_chan * sub_n + my_sub
    chans, tile = x_ref.shape
    rows, _, span = w_ref.shape
    blocks = tm // cs_n
    coarse = span // FINE
    total = tm * tile
    n = tile // span
    owner = me // blocks
    first = me * n
    my_group = lax.axis_index("groups")
    depth = FINE * rows
    piece = depth // (group_n * PIECES)
    half = tm // 2
    partner = me + 1 - 2 * lax.rem(me, 2)
    moves = my_sub == 0
    outer = is_outer(me, half)
    gives = jnp.logical_and(outer, moves)
    takes = jnp.logical_and(jnp.logical_not(outer), moves)
    works = jnp.logical_not(gives)
    low_end = jnp.where(moves, 1, 0)
    high_end = tm - 1 - low_end
    pair = 2 * span
    pairs = tile // pair
    switch = pairs
    behind = 1 + switch

    def remote(src, dst, send, recv, to):
        return pltpu.make_async_remote_copy(
            src_ref=src, dst_ref=dst, send_sem=send, recv_sem=recv,
            device_id=to, device_id_type=MESH)

    def peer(d):
        return {"tm": lax.rem(me + d, tm)}

    def cs_place(c):
        return {"chan": c // sub_n, "sub": c % sub_n}

    barrier = pltpu.get_barrier_semaphore()
    for d in range(1, tm):
        pl.semaphore_signal(barrier, inc=1, device_id=peer(d), device_id_type=MESH)
    for d in range(1, cs_n):
        pl.semaphore_signal(barrier, inc=1, device_id=cs_place(lax.rem(my_cs + d, cs_n)),
                            device_id_type=MESH)

    for d in range(1, group_n):
        pl.semaphore_signal(barrier, inc=1, device_id={"groups": lax.rem(my_group + d, group_n)},
                            device_id_type=MESH)

    xt[pl.ds(me * tile, tile), :] = jnp.transpose(x_ref[...])
    mask = m_ref[...].astype(jnp.float32)
    mk[me] = mask
    for k in range(rows):
        wave = jnp.transpose(w_ref[k].astype(jnp.float32)) * mask[k : k + 1, :]
        tp[my_cs, k : k + 1, 0:chans] = jnp.sum(wave * wave, axis=0, keepdims=True)
        for g in range(coarse):
            af[g, pl.ds(k, FINE, stride=rows), :] = wave[g * FINE : (g + 1) * FINE, :]
    for g in range(coarse):
        ab[0:depth, g * chans : (g + 1) * chans] = af[g].astype(jnp.bfloat16)
    tp[my_cs, :, chans : 2 * chans] = mask

    pl.semaphore_wait(barrier, tm - 1 + cs_n - 1 + group_n - 1)

    def mask_copy(d):
        return remote(mk.at[me], mk.at[me], mask_sem.at[d], maskin_sem.at[me], peer(d))

    for d in range(1, tm):
        mask_copy(d).start()

    def wave_copy(p, to):
        at = (my_group * PIECES + p) * piece
        return remote(ab.at[pl.ds(pl.multiple_of(at, piece), piece), :],
                      ab.at[pl.ds(pl.multiple_of(depth + at, piece), piece), :],
                      wave_sem.at[p], wavein_sem.at[my_group, p], {"tm": to})

    def pass_copy(p, d):
        at = pl.ds(pl.multiple_of(depth + (my_group * PIECES + p) * piece, piece), piece)
        return remote(ab.at[at, :], ab.at[at, :], pass_sem.at[d, p], wavein_sem.at[my_group, p],
                      {"groups": lax.rem(my_group + d, group_n)})

    @pl.when(gives)
    def _():
        for p in range(PIECES):
            wave_copy(p, partner).start()

    def relay(c, to, sem):
        part = pl.ds(pl.multiple_of(c * span, span), span)
        return remote(xt.at[part, :], xt.at[part, :], sem.at[c], recv_sem.at[c], {"tm": to})

    def send_own():
        for k in range(n):
            @pl.when(me < high_end)
            def _():
                relay(first + n - 1 - k, me + 1, right_sem).start()

            @pl.when(me > low_end)
            def _():
                relay(first + k, me - 1, left_sem).start()


    send_own()

    def te_copy():
        return remote(tp.at[my_cs], tp.at[my_cs], te_sem, tein_sem.at[my_cs], cs_place(owner))

    @pl.when(my_cs != owner)
    def _():
        te_copy().start()

    acc[...] = jnp.zeros_like(acc)

    def spread(p, slot, start, before):
        width = p.shape[1]
        pad = jnp.zeros((rows, LANES), jnp.float32)
        out = jnp.concatenate([pad, p[:rows]], 1)
        for b in range(1, FINE):
            one = jnp.concatenate([pad, p[b * rows : (b + 1) * rows]], 1)
            out = out + pltpu.roll(one, width + LANES - b, 1)
        acc[slot, :, pl.ds(before, LANES)] += out[:, :LANES]
        acc[slot, :, pl.ds(start, width)] += out[:, LANES:]

    def add_products(slots, right, start, before):
        low, high = slots[0] * depth, (slots[-1] + 1) * depth
        p = lax.dot_general(ab[low:high, :], right, NT, preferred_element_type=jnp.float32)
        for i, slot in enumerate(slots):
            spread(p[i * depth : (i + 1) * depth], slot, start, before)

    def process(c, width, slots):
        start = pl.multiple_of(c * span, span)
        before = pl.multiple_of(lax.rem(start + total - LANES, total), LANES)
        right = jnp.concatenate(
            [xt[pl.ds(pl.multiple_of(start + FINE * g, FINE), width), :] for g in range(coarse)],
            1)
        add_products(slots, right, start, before)

    def own(slots):
        process(first, tile - span, slots)

    def close(slots):
        start = total - span
        right = jnp.concatenate(
            [jnp.concatenate([xt[start + FINE * g : total, :], xt[0 : FINE * g, :]], 0)
             if g else xt[start:total, :] for g in range(coarse)], 1)
        add_products(slots, right, start, start - LANES)

    def block_of(slot):
        return partner if slot else me

    def holder(slot):
        return block_of(slot) // blocks

    def columns(o):
        return pl.ds(pl.multiple_of(o * pair, pair), pair)

    def out_copy(o, slot):
        q = block_of(slot) % blocks
        return remote(acc.at[slot, :, columns(o)], rb.at[q, my_cs, :, columns(lax.rem(o, pairs))],
                      out_sem.at[slot, o], in_sem.at[q, my_cs, lax.rem(o, pairs)],
                      {"tm": o // pairs, **cs_place(holder(slot))})

    def is_local(o, slot):
        return jnp.logical_and(o // pairs == me, my_cs == holder(slot))

    def hand(o, slot):
        @pl.when(is_local(o, slot))
        def _():
            rb[block_of(slot) % blocks, my_cs, :, columns(lax.rem(o, pairs))] = (
                acc[slot, :, columns(o)])

        @pl.when(jnp.logical_not(is_local(o, slot)))
        def _():
            out_copy(o, slot).start()

    def pow_copy(d):
        to = lax.rem(my_cs + d, cs_n)
        return remote(es.at[to], pb.at[my_cs], pow_sem.at[d], powin_sem.at[my_cs], cs_place(to))

    def power():
        for d in range(1, tm):
            who = lax.rem(me + d, tm)
            remote(mk.at[who], mk.at[who], mask_sem.at[0], maskin_sem.at[who],
                   {"tm": who}).wait_recv()
        masks = jnp.concatenate([mk[i] for i in range(tm)], 0).astype(jnp.bfloat16)
        x32 = xt[pl.ds(me * tile, tile), :].astype(jnp.float32)
        square = x32 * x32
        high = square.astype(jnp.bfloat16)
        low = (square - high.astype(jnp.float32)).astype(jnp.bfloat16)
        p = lax.dot_general(jnp.concatenate([masks, masks], 1), jnp.concatenate([high, low], 1),
                            NT, preferred_element_type=jnp.float32)
        for c in range(cs_n):
            es[c] = p[c * blocks * rows : (c + 1) * blocks * rows, :]
        pb[my_cs] = es[my_cs]
        for d in range(1, cs_n):
            pow_copy(d).start()

    def fac_copy(d):
        return remote(fp.at[me % blocks], fp.at[me % blocks], fac_sem.at[d],
                      facin_sem.at[me % blocks], peer(d))

    def template_sums():
        @pl.when(my_cs == owner)
        def _():
            for d in range(1, cs_n):
                who = lax.rem(my_cs + d, cs_n)
                remote(tp.at[who], tp.at[who], te_sem, tein_sem.at[who], cs_place(who)).wait_recv()
            t = tp[0]
            for c in range(1, cs_n):
                t = t + tp[c]
            te = jnp.sum(t[:, :chans], axis=1, keepdims=True)
            active = jnp.sum(t[:, chans:], axis=1, keepdims=True)
            lane = lax.broadcasted_iota(jnp.int32, (rows, LANES), 1)
            fp[me % blocks] = jnp.where(lane < LANES // 2, te, active)
            for d in range(1, tm):
                fac_copy(d).start()

    def head_copy():
        return remote(eh.at[0], eh.at[1], head_sem.at[0], head_sem.at[1],
                      {"tm": lax.rem(me + tm - 1, tm)})

    def windows():
        for d in range(1, cs_n):
            who = lax.rem(my_cs + d, cs_n)
            remote(es.at[who], pb.at[who], pow_sem.at[0], powin_sem.at[who],
                   cs_place(who)).wait_recv()
        p = pb[0]
        for c in range(1, cs_n):
            p = p + pb[c]
        p = jnp.concatenate([jnp.zeros((blocks * rows, span), jnp.float32), p], 1)
        by = 1
        while by < span:
            p = p + pltpu.roll(p, tile + span - by, 1)
            by *= 2
        eh[0] = p[:, :span]
        head_copy().start()
        ew[0] = p[:, span:]

    def norms():
        head_copy().wait_recv()
        for q in range(blocks):
            j = my_cs * blocks + q

            @pl.when(me != j)
            def _():
                remote(fp.at[q], fp.at[q], fac_sem.at[0], facin_sem.at[q], {"tm": j}).wait_recv()

            at = slice(q * rows, (q + 1) * rows)
            factor = jnp.sqrt(span * fp[q, :, LANES - 1 : LANES])
            energy = jnp.concatenate(
                [ew[0, at, : tile - span], ew[0, at, tile - span :] + eh[1, at, :]], 1)
            ew[1, at, :] = factor / jnp.sqrt(energy * fp[q, :, 0:1] + EPSILON)

    left_n = jnp.where(me <= high_end, pairs * me, 0)
    right_n = jnp.where(me >= low_end, pairs * (tm - 1 - me), 0)
    short = jnp.minimum(left_n, right_n)
    left_short = left_n < right_n
    home = me * pairs
    steps = pairs * (tm - 1)

    def arrival(u):
        v = u - switch
        paired = u < 2 * short
        on_short = jnp.where(takes, jnp.logical_and(v >= 0, v < short),
                             jnp.logical_and(paired, lax.rem(u, 2) == 0))
        k = jnp.where(takes, jnp.where(v < 0, u, jnp.where(on_short, v, u - short)),
                      jnp.where(paired, u // 2, u - short))
        from_left = on_short == left_short
        return from_left, jnp.where(from_left, home - 1 - k, home + pairs + k)

    def made(u):
        from_left, o = arrival(u)
        return jnp.where(from_left, 2 * o, 2 * o - 1)

    def ended(u):
        from_left, o = arrival(u)
        return jnp.where(from_left, o, o - 1)

    @pl.when(works)
    def _():
        own((0,))
        for o in range(pairs - 1):
            hand(home + o, 0)


    def step(u, final):
        live = u < left_n + right_n
        from_left, o = arrival(u)
        per = PIECES // switch

        @pl.when(jnp.logical_and(takes, u < switch))
        def _():
            for i in range(per):
                p = jnp.minimum(u, switch - 1) * per + i
                remote(ab.at[pl.ds(0, piece), :], ab.at[pl.ds(0, piece), :], wave_sem.at[0],
                       wavein_sem.at[my_group, p], {"tm": partner}).wait_recv()
                for d in range(1, group_n):
                    pass_copy(p, d).start()

        @pl.when(jnp.logical_and(live, from_left))
        def _():
            for i in (1, 0):
                relay(2 * o + i, me, right_sem).wait_recv()

                @pl.when(me < high_end)
                def _():
                    relay(2 * o + i, me + 1, right_sem).start()

        @pl.when(jnp.logical_and(live, jnp.logical_not(from_left)))
        def _():
            for i in (0, 1):
                relay(2 * o + i, me, left_sem).wait_recv()

                @pl.when(me > low_end)
                def _():
                    relay(2 * o + i, me - 1, left_sem).start()

        @pl.when(jnp.logical_and(takes, u == switch))
        def _():
            for d in range(1, group_n):
                who = lax.rem(my_group + d, group_n)
                for p in range(PIECES):
                    remote(ab.at[pl.ds(0, piece), :], ab.at[pl.ds(0, piece), :], wave_sem.at[0],
                           wavein_sem.at[who, p], {"groups": who}).wait_recv()

        if final:
            @pl.when(takes)
            def _():
                process(made(u), pair, (0, 1))
                close((0, 1))
                for slot in (0, 1):
                    hand(ended(u), slot)
                    hand(tm * pairs - 1, slot)

            @pl.when(jnp.logical_and(works, jnp.logical_not(takes)))
            def _():
                process(made(u), pair, (0,))
                close((0,))
                hand(ended(u), 0)
                hand(tm * pairs - 1, 0)

            return

        late = jnp.logical_and(takes, u >= switch)

        @pl.when(jnp.logical_and(works, jnp.logical_not(late)))
        def _():
            process(made(u), pair, (0,))

        @pl.when(jnp.logical_and(late, u == switch))
        def _():
            process(made(u), pair, (0, 1))
            own((1,))
            for o in range(pairs - 1):
                hand(home + o, 1)

        @pl.when(jnp.logical_and(late, jnp.logical_and(u > switch, u < switch + behind)))
        def _():
            process(made(u), pair, (0, 1))
            process(made(u - switch - 1), pair, (1,))
            hand(ended(u - switch - 1), 1)

        @pl.when(jnp.logical_and(late, u >= switch + behind))
        def _():
            process(made(u), pair, (0, 1))

        @pl.when(works)
        def _():
            hand(ended(u), 0)

        @pl.when(late)
        def _():
            hand(ended(u), 1)

        @pl.when(u == POWER_AT)
        def _():
            power()

        @pl.when(u == POWER_AT + 1)
        def _():
            template_sums()

        @pl.when(u == POWER_AT + 3)
        def _():
            windows()

    def loop(u, carry):
        step(u, False)
        return carry

    lax.fori_loop(0, steps - 1, loop, 0)
    step(steps - 1, True)

    norms()

    def finish(c, carry):
        @pl.when(jnp.logical_and(me < high_end, c // n <= me))
        def _():
            relay(c, me, right_sem).wait_send()

        @pl.when(jnp.logical_and(me > low_end, c // n >= me))
        def _():
            relay(c, me, left_sem).wait_send()

        return carry

    lax.fori_loop(0, n * tm, finish, 0)

    def finish_out(o, carry):
        for slot in range(2):
            @pl.when(jnp.logical_and(takes if slot else works,
                                     jnp.logical_not(is_local(o, slot))))
            def _():
                out_copy(o, slot).wait_send()

        return carry

    lax.fori_loop(0, pairs * tm, finish_out, 0)
    for p in range(PIECES):
        @pl.when(gives)
        def _():
            wave_copy(p, partner).wait_send()

        @pl.when(takes)
        def _():
            for d in range(1, group_n):
                pass_copy(p, d).wait_send()

    for d in range(1, tm):
        mask_copy(d).wait_send()
    for d in range(1, cs_n):
        pow_copy(d).wait_send()

    @pl.when(my_cs != owner)
    def _():
        te_copy().wait_send()

    @pl.when(my_cs == owner)
    def _():
        for d in range(1, tm):
            fac_copy(d).wait_send()

    head_copy().wait_send()

    for q in range(blocks):
        b = my_cs * blocks + q
        b_outer = is_outer(b, half)
        for slot in range(cs_n):
            moved = slot % sub_n == 0
            source = jnp.where(b_outer, b + 1 - 2 * lax.rem(b, 2), b) if moved else b

            @pl.when(jnp.logical_not(jnp.logical_and(my_cs == slot, source == me)))
            def _():
                for k in range(pairs):
                    remote(acc.at[0, :, pl.ds(0, pair)],
                           rb.at[q, slot, :, pl.ds(k * pair, pair)], out_sem.at[0, 0],
                           in_sem.at[q, slot, k], {"tm": lax.rem(me + 1, tm)}).wait_recv()

        at = slice(q * rows, (q + 1) * rows)
        result = rb[q, 0]
        for c in range(1, cs_n):
            result = result + rb[q, c]
        o_ref[at, :] = result * ew[1, at, :]


def solution(mesh):
    group_n, tm, chan_n, sub_n = (mesh.shape[a] for a in ("groups", "tm", "chan", "sub"))
    cs_n = chan_n * sub_n
    blocks = tm // cs_n

    def on_device(traces, templates, channel_mask):
        chans, tile = traces.shape
        rows, _, span = templates.shape
        coarse = span // FINE
        total = tm * tile
        n = tile // span
        out_rows = blocks * rows
        vmem = pl.BlockSpec(memory_space=pltpu.VMEM)
        f32, bf16 = jnp.float32, jnp.bfloat16
        dma = pltpu.SemaphoreType.DMA
        return pl.pallas_call(
            functools.partial(kernel, (group_n, tm, chan_n, sub_n)),
            out_shape=jax.ShapeDtypeStruct((out_rows, tile), f32),
            in_specs=[vmem] * 3,
            out_specs=vmem,
            scratch_shapes=[
                pltpu.VMEM((total, chans), bf16),
                pltpu.VMEM((coarse, FINE * rows, chans), f32),
                pltpu.VMEM((2 * FINE * rows, coarse * chans), bf16),
                pltpu.VMEM((2, rows, total), f32),
                pltpu.VMEM((blocks, cs_n, rows, tile), f32),
                pltpu.VMEM((tm, rows, chans), f32),
                pltpu.VMEM((cs_n, out_rows, tile), f32),
                pltpu.VMEM((cs_n, rows, 2 * chans), f32),
                pltpu.VMEM((blocks, rows, LANES), f32),
                pltpu.VMEM((2, out_rows, span), f32),
                pltpu.VMEM((cs_n, out_rows, tile), f32),
                pltpu.VMEM((2, out_rows, tile), f32),
                dma((n * tm,)), dma((n * tm,)), dma((n * tm,)),
                dma((2, n * tm // 2)), dma((blocks, cs_n, n // 2)),
                dma((PIECES,)), dma((group_n, PIECES)), dma((group_n, PIECES)),
                dma((tm,)), dma((tm,)),
                dma((cs_n,)), dma((cs_n,)),
                dma(()), dma((cs_n,)),
                dma((tm,)), dma((blocks,)),
                dma((2,)),
            ],
            compiler_params=pltpu.CompilerParams(collective_id=0, has_side_effects=True),
        )(traces, templates, channel_mask)

    placed = (
        P(("chan", "sub"), ("groups", "tm")),
        P("tm", ("chan", "sub"), None),
        P("tm", ("chan", "sub")),
    )
    return jax.shard_map(
        on_device,
        mesh=mesh,
        in_specs=placed,
        out_specs=P(("chan", "sub"), ("groups", "tm")),
        check_vma=False,
    )
```

```python
import functools

import jax
import jax.numpy as jnp
from jax import lax
from jax.experimental import pallas as pl
from jax.experimental.pallas import tpu as pltpu
from jax.sharding import PartitionSpec as P

EPSILON = 1e-06
MESH = pl.DeviceIdType.MESH
LANES = 128
FINE = 32
NT = (((1,), (1,)), ((), ()))
PIECES = 4
POWER_AT = 1


def is_outer(z, half):
    return (z % 2 == 0) == (z < half)


def kernel(sizes, x_ref, w_ref, m_ref, o_ref, xt, af, ab, acc, rb, rx, mk, pb, tp, fp, eh, es, ew,
           recv_sem, right_sem, left_sem, out_sem, in_sem, extra_sem,
           extrain_sem, wave_sem,
           wavein_sem, pass_sem, mask_sem, maskin_sem,
           pow_sem, powin_sem, te_sem, tein_sem, fac_sem, facin_sem, head_sem):
    group_n, tm, chan_n, sub_n = sizes
    cs_n = chan_n * sub_n
    me = lax.axis_index("tm")
    my_chan = lax.axis_index("chan")
    my_sub = lax.axis_index("sub")
    my_cs = my_chan * sub_n + my_sub
    chans, tile = x_ref.shape
    rows, _, span = w_ref.shape
    blocks = tm // cs_n
    coarse = span // FINE
    total = tm * tile
    n = tile // span
    owner = me // blocks
    first = me * n
    my_group = lax.axis_index("groups")
    depth = FINE * rows
    piece = depth // (group_n * PIECES)
    half = tm // 2
    partner = me + 1 - 2 * lax.rem(me, 2)
    moves = my_sub == 0
    outer = is_outer(me, half)
    gives = jnp.logical_and(outer, moves)
    takes = jnp.logical_and(jnp.logical_not(outer), moves)
    low_end = jnp.where(moves, 1, 0)
    high_end = tm - 1 - low_end
    pair = 2 * span
    pairs = tile // pair
    switch = pairs

    def remote(src, dst, send, recv, to):
        return pltpu.make_async_remote_copy(
            src_ref=src, dst_ref=dst, send_sem=send, recv_sem=recv,
            device_id=to, device_id_type=MESH)

    def peer(d):
        return {"tm": lax.rem(me + d, tm)}

    def cs_place(c):
        return {"chan": c // sub_n, "sub": c % sub_n}

    barrier = pltpu.get_barrier_semaphore()
    for d in range(1, tm):
        pl.semaphore_signal(barrier, inc=1, device_id=peer(d), device_id_type=MESH)
    for d in range(1, cs_n):
        pl.semaphore_signal(barrier, inc=1, device_id=cs_place(lax.rem(my_cs + d, cs_n)),
                            device_id_type=MESH)

    for d in range(1, group_n):
        pl.semaphore_signal(barrier, inc=1, device_id={"groups": lax.rem(my_group + d, group_n)},
                            device_id_type=MESH)

    xt[pl.ds(me * tile, tile), :] = jnp.transpose(x_ref[...])
    mask = m_ref[...].astype(jnp.float32)
    mk[me] = mask
    for k in range(rows):
        wave = jnp.transpose(w_ref[k].astype(jnp.float32)) * mask[k : k + 1, :]
        tp[my_cs, k : k + 1, 0:chans] = jnp.sum(wave * wave, axis=0, keepdims=True)
        for g in range(coarse):
            af[g, pl.ds(k, FINE, stride=rows), :] = wave[g * FINE : (g + 1) * FINE, :]
    for g in range(coarse):
        ab[0:depth, g * chans : (g + 1) * chans] = af[g].astype(jnp.bfloat16)
    tp[my_cs, :, chans : 2 * chans] = mask

    pl.semaphore_wait(barrier, tm - 1 + cs_n - 1 + group_n - 1)

    def mask_copy(d):
        return remote(mk.at[me], mk.at[me], mask_sem.at[d], maskin_sem.at[me], peer(d))

    for d in range(1, tm):
        mask_copy(d).start()

    def wave_copy(p, to):
        at = (my_group * PIECES + p) * piece
        return remote(ab.at[pl.ds(pl.multiple_of(at, piece), piece), :],
                      ab.at[pl.ds(pl.multiple_of(depth + at, piece), piece), :],
                      wave_sem.at[p], wavein_sem.at[my_group, p], {"tm": to})

    def pass_copy(p, d):
        at = pl.ds(pl.multiple_of(depth + (my_group * PIECES + p) * piece, piece), piece)
        return remote(ab.at[at, :], ab.at[at, :], pass_sem.at[d, p], wavein_sem.at[my_group, p],
                      {"groups": lax.rem(my_group + d, group_n)})

    @pl.when(gives)
    def _():
        for p in range(PIECES):
            wave_copy(p, partner).start()

    def relay(c, to, sem):
        part = pl.ds(pl.multiple_of(c * span, span), span)
        return remote(xt.at[part, :], xt.at[part, :], sem.at[c], recv_sem.at[c], {"tm": to})

    def send_own():
        for k in range(n):
            @pl.when(me < tm - 1)
            def _():
                relay(first + n - 1 - k, me + 1, right_sem).start()

            @pl.when(me > 0)
            def _():
                relay(first + k, me - 1, left_sem).start()

    send_own()

    def te_copy():
        return remote(tp.at[my_cs], tp.at[my_cs], te_sem, tein_sem.at[my_cs], cs_place(owner))

    @pl.when(my_cs != owner)
    def _():
        te_copy().start()

    acc[...] = jnp.zeros_like(acc)

    def spread(p, slot, start, before):
        width = p.shape[1]
        pad = jnp.zeros((rows, LANES), jnp.float32)
        out = jnp.concatenate([pad, p[:rows]], 1)
        for b in range(1, FINE):
            one = jnp.concatenate([pad, p[b * rows : (b + 1) * rows]], 1)
            out = out + pltpu.roll(one, width + LANES - b, 1)
        acc[slot, :, pl.ds(before, LANES)] += out[:, :LANES]
        acc[slot, :, pl.ds(start, width)] += out[:, LANES:]

    def add_products(slots, right, start, before):
        low, high = slots[0] * depth, (slots[-1] + 1) * depth
        p = lax.dot_general(ab[low:high, :], right, NT, preferred_element_type=jnp.float32)
        for i, slot in enumerate(slots):
            spread(p[i * depth : (i + 1) * depth], slot, start, before)

    def process(c, width, slots):
        start = pl.multiple_of(c * span, span)
        before = pl.multiple_of(lax.rem(start + total - LANES, total), LANES)
        right = jnp.concatenate(
            [xt[pl.ds(pl.multiple_of(start + FINE * g, FINE), width), :] for g in range(coarse)],
            1)
        add_products(slots, right, start, before)

    def own(slots):
        process(first, tile - span, slots)

    def close(slots):
        start = total - span
        right = jnp.concatenate(
            [jnp.concatenate([xt[start + FINE * g : total, :], xt[0 : FINE * g, :]], 0)
             if g else xt[start:total, :] for g in range(coarse)], 1)
        add_products(slots, right, start, start - LANES)

    def block_of(slot):
        return partner if slot else me

    def holder(slot):
        return block_of(slot) // blocks

    def columns(o):
        return pl.ds(pl.multiple_of(o * pair, pair), pair)

    def out_copy(o, slot):
        q = block_of(slot) % blocks
        return remote(acc.at[slot, :, columns(o)], rb.at[q, my_cs, :, columns(lax.rem(o, pairs))],
                      out_sem.at[slot, o], in_sem.at[q, my_cs, lax.rem(o, pairs)],
                      {"tm": o // pairs, **cs_place(holder(slot))})

    def extra_copy(o, slot):
        q = block_of(slot) % blocks
        return remote(acc.at[slot, :, columns(o)], rx.at[q, my_chan],
                      extra_sem, extrain_sem.at[q, my_chan],
                      {"tm": o // pairs, **cs_place(holder(slot))})

    def is_local(o, slot):
        return jnp.logical_and(o // pairs == me, my_cs == holder(slot))

    def hand(o, slot):
        @pl.when(is_local(o, slot))
        def _():
            rb[block_of(slot) % blocks, my_cs, :, columns(lax.rem(o, pairs))] = (
                acc[slot, :, columns(o)])

        @pl.when(jnp.logical_not(is_local(o, slot)))
        def _():
            out_copy(o, slot).start()

    def hand_extra(o, slot):
        @pl.when(is_local(o, slot))
        def _():
            rx[block_of(slot) % blocks, my_chan] = acc[slot, :, columns(o)]

        @pl.when(jnp.logical_not(is_local(o, slot)))
        def _():
            extra_copy(o, slot).start()

    home = me * pairs
    low = me - lax.rem(me, 2)
    pair_last = (low + 2) * pairs - 1
    before_pair = lax.rem(low * pairs + tm * pairs - 1, tm * pairs)

    def hand_second(o):
        @pl.when(o == pair_last)
        def _():
            hand_extra(o, 1)

        @pl.when(o != pair_last)
        def _():
            hand(o, 1)

    def pow_copy(d):
        to = lax.rem(my_cs + d, cs_n)
        return remote(es.at[to], pb.at[my_cs], pow_sem.at[d], powin_sem.at[my_cs], cs_place(to))

    def power():
        for d in range(1, tm):
            who = lax.rem(me + d, tm)
            remote(mk.at[who], mk.at[who], mask_sem.at[0], maskin_sem.at[who],
                   {"tm": who}).wait_recv()
        masks = jnp.concatenate([mk[i] for i in range(tm)], 0).astype(jnp.bfloat16)
        x32 = xt[pl.ds(me * tile, tile), :].astype(jnp.float32)
        square = x32 * x32
        high = square.astype(jnp.bfloat16)
        low = (square - high.astype(jnp.float32)).astype(jnp.bfloat16)
        p = lax.dot_general(jnp.concatenate([masks, masks], 1), jnp.concatenate([high, low], 1),
                            NT, preferred_element_type=jnp.float32)
        for c in range(cs_n):
            es[c] = p[c * blocks * rows : (c + 1) * blocks * rows, :]
        pb[my_cs] = es[my_cs]
        for d in range(1, cs_n):
            pow_copy(d).start()

    def fac_copy(d):
        return remote(fp.at[me % blocks], fp.at[me % blocks], fac_sem.at[d],
                      facin_sem.at[me % blocks], peer(d))

    def template_sums():
        @pl.when(my_cs == owner)
        def _():
            for d in range(1, cs_n):
                who = lax.rem(my_cs + d, cs_n)
                remote(tp.at[who], tp.at[who], te_sem, tein_sem.at[who], cs_place(who)).wait_recv()
            t = tp[0]
            for c in range(1, cs_n):
                t = t + tp[c]
            te = jnp.sum(t[:, :chans], axis=1, keepdims=True)
            active = jnp.sum(t[:, chans:], axis=1, keepdims=True)
            lane = lax.broadcasted_iota(jnp.int32, (rows, LANES), 1)
            fp[me % blocks] = jnp.where(lane < LANES // 2, te, active)
            for d in range(1, tm):
                fac_copy(d).start()

    def head_copy():
        return remote(eh.at[0], eh.at[1], head_sem.at[0], head_sem.at[1],
                      {"tm": lax.rem(me + tm - 1, tm)})

    def windows():
        for d in range(1, cs_n):
            who = lax.rem(my_cs + d, cs_n)
            remote(es.at[who], pb.at[who], pow_sem.at[0], powin_sem.at[who],
                   cs_place(who)).wait_recv()
        p = pb[0]
        for c in range(1, cs_n):
            p = p + pb[c]
        p = jnp.concatenate([jnp.zeros((blocks * rows, span), jnp.float32), p], 1)
        by = 1
        while by < span:
            p = p + pltpu.roll(p, tile + span - by, 1)
            by *= 2
        eh[0] = p[:, :span]
        head_copy().start()
        ew[0] = p[:, span:]

    def norms():
        head_copy().wait_recv()
        for q in range(blocks):
            j = my_cs * blocks + q

            @pl.when(me != j)
            def _():
                remote(fp.at[q], fp.at[q], fac_sem.at[0], facin_sem.at[q], {"tm": j}).wait_recv()

            at = slice(q * rows, (q + 1) * rows)
            factor = jnp.sqrt(span * fp[q, :, LANES - 1 : LANES])
            energy = jnp.concatenate(
                [ew[0, at, : tile - span], ew[0, at, tile - span :] + eh[1, at, :]], 1)
            ew[1, at, :] = factor / jnp.sqrt(energy * fp[q, :, 0:1] + EPSILON)

    left_n = pairs * jnp.where(jnp.logical_and(moves, me == tm - 1), 1, me)
    right_n = pairs * jnp.where(jnp.logical_and(moves, me == 0), 1, tm - 1 - me)
    short = jnp.minimum(left_n, right_n)
    left_short = left_n < right_n
    steps = pairs * (tm - 1)

    def arrival(u):
        v = u - switch
        paired = u < 2 * short
        on_short = jnp.where(takes, jnp.logical_and(v >= 0, v < short),
                             jnp.logical_and(paired, lax.rem(u, 2) == 0))
        k = jnp.where(takes, jnp.where(v < 0, u, jnp.where(on_short, v, u - short)),
                      jnp.where(paired, u // 2, u - short))
        from_left = on_short == left_short
        return from_left, jnp.where(from_left, home - 1 - k, home + pairs + k)

    def made(u):
        from_left, o = arrival(u)
        return jnp.where(from_left, 2 * o, 2 * o - 1)

    def ended(u):
        from_left, o = arrival(u)
        return jnp.where(from_left, o, o - 1)

    own((0,))
    for o in range(pairs - 1):
        @pl.when(jnp.logical_not(jnp.logical_and(gives, lax.rem(me, 2) == 1)))
        def _():
            hand(home + o, 0)

    def step(u, final):
        live = u < left_n + right_n
        from_left, o = arrival(u)
        per = PIECES // switch

        @pl.when(jnp.logical_and(takes, u < switch))
        def _():
            for i in range(per):
                p = jnp.minimum(u, switch - 1) * per + i
                remote(ab.at[pl.ds(0, piece), :], ab.at[pl.ds(0, piece), :], wave_sem.at[0],
                       wavein_sem.at[my_group, p], {"tm": partner}).wait_recv()
                for d in range(1, group_n):
                    pass_copy(p, d).start()

        @pl.when(jnp.logical_and(live, from_left))
        def _():
            for i in (1, 0):
                relay(2 * o + i, me, right_sem).wait_recv()

                @pl.when(me < high_end)
                def _():
                    relay(2 * o + i, me + 1, right_sem).start()

        @pl.when(jnp.logical_and(live, jnp.logical_not(from_left)))
        def _():
            for i in (0, 1):
                relay(2 * o + i, me, left_sem).wait_recv()

                @pl.when(me > low_end)
                def _():
                    relay(2 * o + i, me - 1, left_sem).start()

        @pl.when(jnp.logical_and(takes, u == switch + 1))
        def _():
            for d in range(1, group_n):
                who = lax.rem(my_group + d, group_n)
                for p in range(PIECES):
                    remote(ab.at[pl.ds(0, piece), :], ab.at[pl.ds(0, piece), :], wave_sem.at[0],
                           wavein_sem.at[who, p], {"groups": who}).wait_recv()

        both = jnp.logical_and(takes, u >= switch + pairs)
        if final:
            @pl.when(takes)
            def _():
                process(made(u), pair, (0, 1))
                close((0, 1))
                hand(ended(u), 0)
                hand_second(ended(u))
                hand(tm * pairs - 1, 0)
                hand_second(tm * pairs - 1)

            @pl.when(jnp.logical_not(moves))
            def _():
                process(made(u), pair, (0,))
                close((0,))
                hand(ended(u), 0)
                hand(tm * pairs - 1, 0)

            @pl.when(gives)
            def _():
                for o in range(2 * pairs):
                    at = low * pairs + o

                    @pl.when(jnp.logical_or(lax.rem(me, 2) == 1, o >= pairs - 1))
                    def _():
                        hand(at, 0)
                hand_extra(before_pair, 0)

            return

        @pl.when(jnp.logical_or(
            jnp.logical_and(gives, jnp.logical_and(live, o // pairs == partner)),
            jnp.logical_and(jnp.logical_not(gives), jnp.logical_not(jnp.logical_or(
                both, jnp.logical_and(takes, u == switch + 1))))))
        def _():
            process(made(u), pair, (0,))

        @pl.when(jnp.logical_and(takes, u == switch + 1))
        def _():
            process(made(u), pair, (0,))
            process(jnp.minimum(made(0), made(switch - 1)), switch * pair, (1,))
            for v in range(switch):
                hand_second(ended(v))

        @pl.when(both)
        def _():
            process(made(u), pair, (0, 1))
            hand_second(ended(u))

        @pl.when(jnp.logical_not(gives))
        def _():
            hand(ended(u), 0)

        @pl.when(u == POWER_AT)
        def _():
            power()

        @pl.when(u == POWER_AT + 1)
        def _():
            template_sums()

        @pl.when(u == POWER_AT + 3)
        def _():
            windows()

    def loop(u, carry):
        step(u, False)
        return carry

    lax.fori_loop(0, steps - 1, loop, 0)
    step(steps - 1, True)

    norms()

    def finish(c, carry):
        @pl.when(jnp.logical_or(jnp.logical_and(me < high_end, c // n < me),
                                jnp.logical_and(me < tm - 1, c // n == me)))
        def _():
            relay(c, me, right_sem).wait_send()

        @pl.when(jnp.logical_or(jnp.logical_and(me > low_end, c // n > me),
                                jnp.logical_and(me > 0, c // n == me)))
        def _():
            relay(c, me, left_sem).wait_send()

        return carry

    lax.fori_loop(0, n * tm, finish, 0)

    def finish_out(o, carry):
        in_pair = o // (2 * pairs) == me // 2

        @pl.when(jnp.logical_and(jnp.logical_or(jnp.logical_not(gives), in_pair),
                                 jnp.logical_not(is_local(o, 0))))
        def _():
            out_copy(o, 0).wait_send()

        @pl.when(jnp.logical_and(jnp.logical_and(takes, jnp.logical_not(in_pair)),
                                 jnp.logical_not(is_local(o, 1))))
        def _():
            out_copy(o, 1).wait_send()

        return carry

    lax.fori_loop(0, pairs * tm, finish_out, 0)

    @pl.when(jnp.logical_and(gives, jnp.logical_not(is_local(before_pair, 0))))
    def _():
        extra_copy(before_pair, 0).wait_send()

    @pl.when(jnp.logical_and(takes, jnp.logical_not(is_local(pair_last, 1))))
    def _():
        extra_copy(pair_last, 1).wait_send()
    for p in range(PIECES):
        @pl.when(gives)
        def _():
            wave_copy(p, partner).wait_send()

        @pl.when(takes)
        def _():
            for d in range(1, group_n):
                pass_copy(p, d).wait_send()

    for d in range(1, tm):
        mask_copy(d).wait_send()
    for d in range(1, cs_n):
        pow_copy(d).wait_send()

    @pl.when(my_cs != owner)
    def _():
        te_copy().wait_send()

    @pl.when(my_cs == owner)
    def _():
        for d in range(1, tm):
            fac_copy(d).wait_send()

    head_copy().wait_send()

    for q in range(blocks):
        b = my_cs * blocks + q
        b_outer = is_outer(b, half)
        for slot in range(cs_n):
            moved = slot % sub_n == 0
            inner = b + 1 - 2 * lax.rem(b, 2)
            apart = jnp.logical_and(b_outer, me // 2 != b // 2)
            source = jnp.where(apart, inner, b) if moved else b

            @pl.when(jnp.logical_not(jnp.logical_and(my_cs == slot, source == me)))
            def _():
                for k in range(pairs):
                    remote(acc.at[0, :, pl.ds(0, pair)],
                           rb.at[q, slot, :, pl.ds(k * pair, pair)], out_sem.at[0, 0],
                           in_sem.at[q, slot, k], {"tm": lax.rem(me + 1, tm)}).wait_recv()

        at = slice(q * rows, (q + 1) * rows)
        result = rb[q, 0]
        for c in range(1, cs_n):
            result = result + rb[q, c]
        b_low = b - lax.rem(b, 2)
        tail = jnp.logical_and(b_outer, me == b_low + 1)
        ahead = jnp.logical_and(b_outer, me == lax.rem(b_low + tm - 1, tm))
        for c in range(chan_n):
            source = jnp.where(me == b_low + 1, inner, b)
            near_me = jnp.logical_and(jnp.logical_and(my_sub == 0, my_chan == c), source == me)

            @pl.when(jnp.logical_and(jnp.logical_or(tail, ahead), jnp.logical_not(near_me)))
            def _():
                remote(acc.at[0, :, pl.ds(0, pair)], rx.at[q, c], out_sem.at[0, 0],
                       extrain_sem.at[q, c], {"tm": lax.rem(me + 1, tm)}).wait_recv()

        o_ref[at, :] = result * ew[1, at, :]

        @pl.when(jnp.logical_or(tail, ahead))
        def _():
            more = rx[q, 0]
            for c in range(1, chan_n):
                more = more + rx[q, c]
            whole = slice(tile - pair, tile)
            o_ref[at, whole] = (result[:, whole] + more) * ew[1, at, whole]


def solution(mesh):
    group_n, tm, chan_n, sub_n = (mesh.shape[a] for a in ("groups", "tm", "chan", "sub"))
    cs_n = chan_n * sub_n
    blocks = tm // cs_n

    def on_device(traces, templates, channel_mask):
        chans, tile = traces.shape
        rows, _, span = templates.shape
        coarse = span // FINE
        total = tm * tile
        n = tile // span
        out_rows = blocks * rows
        vmem = pl.BlockSpec(memory_space=pltpu.VMEM)
        f32, bf16 = jnp.float32, jnp.bfloat16
        dma = pltpu.SemaphoreType.DMA
        return pl.pallas_call(
            functools.partial(kernel, (group_n, tm, chan_n, sub_n)),
            out_shape=jax.ShapeDtypeStruct((out_rows, tile), f32),
            in_specs=[vmem] * 3,
            out_specs=vmem,
            scratch_shapes=[
                pltpu.VMEM((total, chans), bf16),
                pltpu.VMEM((coarse, FINE * rows, chans), f32),
                pltpu.VMEM((2 * FINE * rows, coarse * chans), bf16),
                pltpu.VMEM((2, rows, total), f32),
                pltpu.VMEM((blocks, cs_n, rows, tile), f32),
                pltpu.VMEM((blocks, chan_n, rows, 2 * span), f32),
                pltpu.VMEM((tm, rows, chans), f32),
                pltpu.VMEM((cs_n, out_rows, tile), f32),
                pltpu.VMEM((cs_n, rows, 2 * chans), f32),
                pltpu.VMEM((blocks, rows, LANES), f32),
                pltpu.VMEM((2, out_rows, span), f32),
                pltpu.VMEM((cs_n, out_rows, tile), f32),
                pltpu.VMEM((2, out_rows, tile), f32),
                dma((n * tm,)), dma((n * tm,)), dma((n * tm,)),
                dma((2, n * tm // 2)), dma((blocks, cs_n, n // 2)),
                dma(()), dma((blocks, chan_n)),
                dma((PIECES,)), dma((group_n, PIECES)), dma((group_n, PIECES)),
                dma((tm,)), dma((tm,)),
                dma((cs_n,)), dma((cs_n,)),
                dma(()), dma((cs_n,)),
                dma((tm,)), dma((blocks,)),
                dma((2,)),
            ],
            compiler_params=pltpu.CompilerParams(collective_id=0, has_side_effects=True),
        )(traces, templates, channel_mask)

    placed = (
        P(("chan", "sub"), ("groups", "tm")),
        P("tm", ("chan", "sub"), None),
        P("tm", ("chan", "sub")),
    )
    return jax.shard_map(
        on_device,
        mesh=mesh,
        in_specs=placed,
        out_specs=P(("chan", "sub"), ("groups", "tm")),
        check_vma=False,
    )
```

```python
import functools

import jax
import jax.numpy as jnp
from jax import lax
from jax.experimental import pallas as pl
from jax.experimental.pallas import tpu as pltpu
from jax.sharding import PartitionSpec as P

EPSILON = 1e-06
MESH = pl.DeviceIdType.MESH
LANES = 128
FINE = 32
NT = (((1,), (1,)), ((), ()))
PIECES = 4
VMEM_LIMIT = 32 * 1024 * 1024
POWER_AT = 1


def is_outer(z, half):
    return (z % 2 == 0) == (z < half)


def kernel(sizes, x_hbm, w_hbm, m_hbm, o_ref, x_ref, w_ref, m_ref, xt, af, ab, acc, rb, rx, mk, pb, tp, fp, eh, es, ew,
           recv_sem, right_sem, left_sem, out_sem, in_sem, extra_sem,
           extrain_sem, wave_sem,
           wavein_sem, pass_sem, mask_sem, maskin_sem,
           pow_sem, powin_sem, te_sem, tein_sem, fac_sem, facin_sem, head_sem, load_sem):
    group_n, tm, chan_n, sub_n = sizes
    cs_n = chan_n * sub_n
    me = lax.axis_index("tm")
    my_chan = lax.axis_index("chan")
    my_sub = lax.axis_index("sub")
    my_cs = my_chan * sub_n + my_sub
    chans, tile = x_ref.shape
    rows, _, span = w_ref.shape
    blocks = tm // cs_n
    coarse = span // FINE
    total = tm * tile
    n = tile // span
    owner = me // blocks
    first = me * n
    my_group = lax.axis_index("groups")
    depth = FINE * rows
    piece = depth // (group_n * PIECES)
    half = tm // 2
    partner = me + 1 - 2 * lax.rem(me, 2)
    moves = my_sub == 0
    outer = is_outer(me, half)
    gives = jnp.logical_and(outer, moves)
    takes = jnp.logical_and(jnp.logical_not(outer), moves)
    low_end = jnp.where(moves, 1, 0)
    high_end = tm - 1 - low_end
    pair = 2 * span
    pairs = tile // pair
    switch = pairs

    def remote(src, dst, send, recv, to):
        return pltpu.make_async_remote_copy(
            src_ref=src, dst_ref=dst, send_sem=send, recv_sem=recv,
            device_id=to, device_id_type=MESH)

    def peer(d):
        return {"tm": lax.rem(me + d, tm)}

    def cs_place(c):
        return {"chan": c // sub_n, "sub": c % sub_n}

    loads = [pltpu.make_async_copy(src, dst, load_sem.at[i]) for i, (src, dst) in enumerate(
        ((m_hbm, m_ref), (x_hbm, x_ref), (w_hbm, w_ref)))]
    for load in loads:
        load.start()

    barrier = pltpu.get_barrier_semaphore()
    for d in range(1, tm):
        pl.semaphore_signal(barrier, inc=1, device_id=peer(d), device_id_type=MESH)
    for d in range(1, cs_n):
        pl.semaphore_signal(barrier, inc=1, device_id=cs_place(lax.rem(my_cs + d, cs_n)),
                            device_id_type=MESH)

    for d in range(1, group_n):
        pl.semaphore_signal(barrier, inc=1, device_id={"groups": lax.rem(my_group + d, group_n)},
                            device_id_type=MESH)

    loads[0].wait()
    mask = m_ref[...].astype(jnp.float32)
    mk[me] = mask
    loads[1].wait()
    xt[pl.ds(me * tile, tile), :] = jnp.transpose(x_ref[...])
    loads[2].wait()
    for k in range(rows):
        wave = jnp.transpose(w_ref[k].astype(jnp.float32)) * mask[k : k + 1, :]
        tp[my_cs, k : k + 1, 0:chans] = jnp.sum(wave * wave, axis=0, keepdims=True)
        for g in range(coarse):
            af[g, pl.ds(k, FINE, stride=rows), :] = wave[g * FINE : (g + 1) * FINE, :]
    for g in range(coarse):
        ab[0:depth, g * chans : (g + 1) * chans] = af[g].astype(jnp.bfloat16)
    tp[my_cs, :, chans : 2 * chans] = mask

    pl.semaphore_wait(barrier, tm - 1 + cs_n - 1 + group_n - 1)

    def mask_copy(d):
        return remote(mk.at[me], mk.at[me], mask_sem.at[d], maskin_sem.at[me], peer(d))

    for d in range(1, tm):
        mask_copy(d).start()

    def wave_copy(p, to):
        at = (my_group * PIECES + p) * piece
        return remote(ab.at[pl.ds(pl.multiple_of(at, piece), piece), :],
                      ab.at[pl.ds(pl.multiple_of(depth + at, piece), piece), :],
                      wave_sem.at[p], wavein_sem.at[my_group, p], {"tm": to})

    def pass_copy(p, d):
        at = pl.ds(pl.multiple_of(depth + (my_group * PIECES + p) * piece, piece), piece)
        return remote(ab.at[at, :], ab.at[at, :], pass_sem.at[d, p], wavein_sem.at[my_group, p],
                      {"groups": lax.rem(my_group + d, group_n)})

    @pl.when(gives)
    def _():
        for p in range(PIECES):
            wave_copy(p, partner).start()

    def relay(c, to, sem):
        part = pl.ds(pl.multiple_of(c * span, span), span)
        return remote(xt.at[part, :], xt.at[part, :], sem.at[c], recv_sem.at[c], {"tm": to})

    def send_own():
        for k in range(n):
            @pl.when(me < tm - 1)
            def _():
                relay(first + n - 1 - k, me + 1, right_sem).start()

            @pl.when(me > 0)
            def _():
                relay(first + k, me - 1, left_sem).start()

    send_own()

    def te_copy():
        return remote(tp.at[my_cs], tp.at[my_cs], te_sem, tein_sem.at[my_cs], cs_place(owner))

    @pl.when(my_cs != owner)
    def _():
        te_copy().start()

    acc[...] = jnp.zeros_like(acc)

    def spread(p, slot, start, before):
        width = p.shape[1]
        pad = jnp.zeros((rows, LANES), jnp.float32)
        out = jnp.concatenate([pad, p[:rows]], 1)
        for b in range(1, FINE):
            one = jnp.concatenate([pad, p[b * rows : (b + 1) * rows]], 1)
            out = out + pltpu.roll(one, width + LANES - b, 1)
        acc[slot, :, pl.ds(before, LANES)] += out[:, :LANES]
        acc[slot, :, pl.ds(start, width)] += out[:, LANES:]

    def add_products(slots, right, start, before):
        low, high = slots[0] * depth, (slots[-1] + 1) * depth
        p = lax.dot_general(ab[low:high, :], right, NT, preferred_element_type=jnp.float32)
        for i, slot in enumerate(slots):
            spread(p[i * depth : (i + 1) * depth], slot, start, before)

    def process(c, width, slots):
        start = pl.multiple_of(c * span, span)
        before = pl.multiple_of(lax.rem(start + total - LANES, total), LANES)
        right = jnp.concatenate(
            [xt[pl.ds(pl.multiple_of(start + FINE * g, FINE), width), :] for g in range(coarse)],
            1)
        add_products(slots, right, start, before)

    def own(slots):
        process(first, tile - span, slots)

    def close(slots):
        start = total - span
        right = jnp.concatenate(
            [jnp.concatenate([xt[start + FINE * g : total, :], xt[0 : FINE * g, :]], 0)
             if g else xt[start:total, :] for g in range(coarse)], 1)
        add_products(slots, right, start, start - LANES)

    def block_of(slot):
        return partner if slot else me

    def holder(slot):
        return block_of(slot) // blocks

    def columns(o):
        return pl.ds(pl.multiple_of(o * pair, pair), pair)

    def out_copy(o, slot):
        q = block_of(slot) % blocks
        return remote(acc.at[slot, :, columns(o)], rb.at[q, my_cs, :, columns(lax.rem(o, pairs))],
                      out_sem.at[slot, o], in_sem.at[q, my_cs, lax.rem(o, pairs)],
                      {"tm": o // pairs, **cs_place(holder(slot))})

    def extra_copy(o, slot):
        q = block_of(slot) % blocks
        return remote(acc.at[slot, :, columns(o)], rx.at[q, my_chan],
                      extra_sem, extrain_sem.at[q, my_chan],
                      {"tm": o // pairs, **cs_place(holder(slot))})

    def is_local(o, slot):
        return jnp.logical_and(o // pairs == me, my_cs == holder(slot))

    def hand(o, slot):
        @pl.when(is_local(o, slot))
        def _():
            rb[block_of(slot) % blocks, my_cs, :, columns(lax.rem(o, pairs))] = (
                acc[slot, :, columns(o)])

        @pl.when(jnp.logical_not(is_local(o, slot)))
        def _():
            out_copy(o, slot).start()

    def hand_extra(o, slot):
        @pl.when(is_local(o, slot))
        def _():
            rx[block_of(slot) % blocks, my_chan] = acc[slot, :, columns(o)]

        @pl.when(jnp.logical_not(is_local(o, slot)))
        def _():
            extra_copy(o, slot).start()

    home = me * pairs
    low = me - lax.rem(me, 2)
    pair_last = (low + 2) * pairs - 1
    before_pair = lax.rem(low * pairs + tm * pairs - 1, tm * pairs)

    def hand_second(o):
        @pl.when(o == pair_last)
        def _():
            hand_extra(o, 1)

        @pl.when(o != pair_last)
        def _():
            hand(o, 1)

    def pow_copy(d):
        to = lax.rem(my_cs + d, cs_n)
        return remote(es.at[to], pb.at[my_cs], pow_sem.at[d], powin_sem.at[my_cs], cs_place(to))

    def power():
        for d in range(1, tm):
            who = lax.rem(me + d, tm)
            remote(mk.at[who], mk.at[who], mask_sem.at[0], maskin_sem.at[who],
                   {"tm": who}).wait_recv()
        masks = jnp.concatenate([mk[i] for i in range(tm)], 0).astype(jnp.bfloat16)
        x32 = xt[pl.ds(me * tile, tile), :].astype(jnp.float32)
        square = x32 * x32
        high = square.astype(jnp.bfloat16)
        low = (square - high.astype(jnp.float32)).astype(jnp.bfloat16)
        p = lax.dot_general(jnp.concatenate([masks, masks], 1), jnp.concatenate([high, low], 1),
                            NT, preferred_element_type=jnp.float32)
        for c in range(cs_n):
            es[c] = p[c * blocks * rows : (c + 1) * blocks * rows, :]
        pb[my_cs] = es[my_cs]
        for d in range(1, cs_n):
            pow_copy(d).start()

    def fac_copy(d):
        return remote(fp.at[me % blocks], fp.at[me % blocks], fac_sem.at[d],
                      facin_sem.at[me % blocks], peer(d))

    def template_sums():
        @pl.when(my_cs == owner)
        def _():
            for d in range(1, cs_n):
                who = lax.rem(my_cs + d, cs_n)
                remote(tp.at[who], tp.at[who], te_sem, tein_sem.at[who], cs_place(who)).wait_recv()
            t = tp[0]
            for c in range(1, cs_n):
                t = t + tp[c]
            te = jnp.sum(t[:, :chans], axis=1, keepdims=True)
            active = jnp.sum(t[:, chans:], axis=1, keepdims=True)
            lane = lax.broadcasted_iota(jnp.int32, (rows, LANES), 1)
            fp[me % blocks] = jnp.where(lane < LANES // 2, te, active)
            for d in range(1, tm):
                fac_copy(d).start()

    def head_copy():
        return remote(eh.at[0], eh.at[1], head_sem.at[0], head_sem.at[1],
                      {"tm": lax.rem(me + tm - 1, tm)})

    def windows():
        for d in range(1, cs_n):
            who = lax.rem(my_cs + d, cs_n)
            remote(es.at[who], pb.at[who], pow_sem.at[0], powin_sem.at[who],
                   cs_place(who)).wait_recv()
        p = pb[0]
        for c in range(1, cs_n):
            p = p + pb[c]
        p = jnp.concatenate([jnp.zeros((blocks * rows, span), jnp.float32), p], 1)
        by = 1
        while by < span:
            p = p + pltpu.roll(p, tile + span - by, 1)
            by *= 2
        eh[0] = p[:, :span]
        head_copy().start()
        ew[0] = p[:, span:]

    def norms():
        head_copy().wait_recv()
        for q in range(blocks):
            j = my_cs * blocks + q

            @pl.when(me != j)
            def _():
                remote(fp.at[q], fp.at[q], fac_sem.at[0], facin_sem.at[q], {"tm": j}).wait_recv()

            at = slice(q * rows, (q + 1) * rows)
            factor = jnp.sqrt(span * fp[q, :, LANES - 1 : LANES])
            energy = jnp.concatenate(
                [ew[0, at, : tile - span], ew[0, at, tile - span :] + eh[1, at, :]], 1)
            ew[1, at, :] = factor / jnp.sqrt(energy * fp[q, :, 0:1] + EPSILON)

    left_n = pairs * jnp.where(jnp.logical_and(moves, me == tm - 1), 1, me)
    right_n = pairs * jnp.where(jnp.logical_and(moves, me == 0), 1, tm - 1 - me)
    short = jnp.minimum(left_n, right_n)
    left_short = left_n < right_n
    steps = pairs * (tm - 1)

    def arrival(u):
        v = u - switch
        paired = u < 2 * short
        on_short = jnp.where(takes, jnp.logical_and(v >= 0, v < short),
                             jnp.logical_and(paired, lax.rem(u, 2) == 0))
        k = jnp.where(takes, jnp.where(v < 0, u, jnp.where(on_short, v, u - short)),
                      jnp.where(paired, u // 2, u - short))
        from_left = on_short == left_short
        return from_left, jnp.where(from_left, home - 1 - k, home + pairs + k)

    def made(u):
        from_left, o = arrival(u)
        return jnp.where(from_left, 2 * o, 2 * o - 1)

    def ended(u):
        from_left, o = arrival(u)
        return jnp.where(from_left, o, o - 1)

    own((0,))
    for o in range(pairs - 1):
        @pl.when(jnp.logical_not(jnp.logical_and(gives, lax.rem(me, 2) == 1)))
        def _():
            hand(home + o, 0)

    def step(u, final):
        live = u < left_n + right_n
        from_left, o = arrival(u)
        per = PIECES // switch

        @pl.when(jnp.logical_and(takes, u < switch))
        def _():
            for i in range(per):
                p = jnp.minimum(u, switch - 1) * per + i
                remote(ab.at[pl.ds(0, piece), :], ab.at[pl.ds(0, piece), :], wave_sem.at[0],
                       wavein_sem.at[my_group, p], {"tm": partner}).wait_recv()
                for d in range(1, group_n):
                    pass_copy(p, d).start()

        @pl.when(jnp.logical_and(live, from_left))
        def _():
            for i in (1, 0):
                relay(2 * o + i, me, right_sem).wait_recv()

                @pl.when(me < high_end)
                def _():
                    relay(2 * o + i, me + 1, right_sem).start()

        @pl.when(jnp.logical_and(live, jnp.logical_not(from_left)))
        def _():
            for i in (0, 1):
                relay(2 * o + i, me, left_sem).wait_recv()

                @pl.when(me > low_end)
                def _():
                    relay(2 * o + i, me - 1, left_sem).start()

        @pl.when(jnp.logical_and(takes, u == switch + 1))
        def _():
            for d in range(1, group_n):
                who = lax.rem(my_group + d, group_n)
                for p in range(PIECES):
                    remote(ab.at[pl.ds(0, piece), :], ab.at[pl.ds(0, piece), :], wave_sem.at[0],
                           wavein_sem.at[who, p], {"groups": who}).wait_recv()

        both = jnp.logical_and(takes, u >= switch + pairs)
        if final:
            @pl.when(takes)
            def _():
                process(made(u), pair, (0, 1))
                close((0, 1))
                hand(ended(u), 0)
                hand_second(ended(u))
                hand(tm * pairs - 1, 0)
                hand_second(tm * pairs - 1)

            @pl.when(jnp.logical_not(moves))
            def _():
                process(made(u), pair, (0,))
                close((0,))
                hand(ended(u), 0)
                hand(tm * pairs - 1, 0)

            @pl.when(gives)
            def _():
                for o in range(2 * pairs):
                    at = low * pairs + o

                    @pl.when(jnp.logical_or(lax.rem(me, 2) == 1, o >= pairs - 1))
                    def _():
                        hand(at, 0)
                hand_extra(before_pair, 0)

            return

        @pl.when(jnp.logical_or(
            jnp.logical_and(gives, jnp.logical_and(live, o // pairs == partner)),
            jnp.logical_and(jnp.logical_not(gives), jnp.logical_not(jnp.logical_or(
                both, jnp.logical_and(takes, u == switch + 1))))))
        def _():
            process(made(u), pair, (0,))

        @pl.when(jnp.logical_and(takes, u == switch + 1))
        def _():
            process(made(u), pair, (0,))
            process(jnp.minimum(made(0), made(switch - 1)), switch * pair, (1,))
            for v in range(switch):
                hand_second(ended(v))

        @pl.when(both)
        def _():
            process(made(u), pair, (0, 1))
            hand_second(ended(u))

        @pl.when(jnp.logical_not(gives))
        def _():
            hand(ended(u), 0)

        @pl.when(u == POWER_AT)
        def _():
            power()

        @pl.when(u == POWER_AT + 1)
        def _():
            template_sums()

        @pl.when(u == POWER_AT + 3)
        def _():
            windows()

    def loop(u, carry):
        step(u, False)
        return carry

    lax.fori_loop(0, steps - 1, loop, 0)
    step(steps - 1, True)

    norms()

    def finish(c, carry):
        @pl.when(jnp.logical_or(jnp.logical_and(me < high_end, c // n < me),
                                jnp.logical_and(me < tm - 1, c // n == me)))
        def _():
            relay(c, me, right_sem).wait_send()

        @pl.when(jnp.logical_or(jnp.logical_and(me > low_end, c // n > me),
                                jnp.logical_and(me > 0, c // n == me)))
        def _():
            relay(c, me, left_sem).wait_send()

        return carry

    lax.fori_loop(0, n * tm, finish, 0)

    def finish_out(o, carry):
        in_pair = o // (2 * pairs) == me // 2

        @pl.when(jnp.logical_and(jnp.logical_or(jnp.logical_not(gives), in_pair),
                                 jnp.logical_not(is_local(o, 0))))
        def _():
            out_copy(o, 0).wait_send()

        @pl.when(jnp.logical_and(jnp.logical_and(takes, jnp.logical_not(in_pair)),
                                 jnp.logical_not(is_local(o, 1))))
        def _():
            out_copy(o, 1).wait_send()

        return carry

    lax.fori_loop(0, pairs * tm, finish_out, 0)

    @pl.when(jnp.logical_and(gives, jnp.logical_not(is_local(before_pair, 0))))
    def _():
        extra_copy(before_pair, 0).wait_send()

    @pl.when(jnp.logical_and(takes, jnp.logical_not(is_local(pair_last, 1))))
    def _():
        extra_copy(pair_last, 1).wait_send()
    for p in range(PIECES):
        @pl.when(gives)
        def _():
            wave_copy(p, partner).wait_send()

        @pl.when(takes)
        def _():
            for d in range(1, group_n):
                pass_copy(p, d).wait_send()

    for d in range(1, tm):
        mask_copy(d).wait_send()
    for d in range(1, cs_n):
        pow_copy(d).wait_send()

    @pl.when(my_cs != owner)
    def _():
        te_copy().wait_send()

    @pl.when(my_cs == owner)
    def _():
        for d in range(1, tm):
            fac_copy(d).wait_send()

    head_copy().wait_send()

    for q in range(blocks):
        b = my_cs * blocks + q
        b_outer = is_outer(b, half)
        for slot in range(cs_n):
            moved = slot % sub_n == 0
            inner = b + 1 - 2 * lax.rem(b, 2)
            apart = jnp.logical_and(b_outer, me // 2 != b // 2)
            source = jnp.where(apart, inner, b) if moved else b

            @pl.when(jnp.logical_not(jnp.logical_and(my_cs == slot, source == me)))
            def _():
                for k in range(pairs):
                    remote(acc.at[0, :, pl.ds(0, pair)],
                           rb.at[q, slot, :, pl.ds(k * pair, pair)], out_sem.at[0, 0],
                           in_sem.at[q, slot, k], {"tm": lax.rem(me + 1, tm)}).wait_recv()

        at = slice(q * rows, (q + 1) * rows)
        result = rb[q, 0]
        for c in range(1, cs_n):
            result = result + rb[q, c]
        b_low = b - lax.rem(b, 2)
        tail = jnp.logical_and(b_outer, me == b_low + 1)
        ahead = jnp.logical_and(b_outer, me == lax.rem(b_low + tm - 1, tm))
        for c in range(chan_n):
            source = jnp.where(me == b_low + 1, inner, b)
            near_me = jnp.logical_and(jnp.logical_and(my_sub == 0, my_chan == c), source == me)

            @pl.when(jnp.logical_and(jnp.logical_or(tail, ahead), jnp.logical_not(near_me)))
            def _():
                remote(acc.at[0, :, pl.ds(0, pair)], rx.at[q, c], out_sem.at[0, 0],
                       extrain_sem.at[q, c], {"tm": lax.rem(me + 1, tm)}).wait_recv()

        o_ref[at, :] = result * ew[1, at, :]

        @pl.when(jnp.logical_or(tail, ahead))
        def _():
            more = rx[q, 0]
            for c in range(1, chan_n):
                more = more + rx[q, c]
            whole = slice(tile - pair, tile)
            o_ref[at, whole] = (result[:, whole] + more) * ew[1, at, whole]


def solution(mesh):
    group_n, tm, chan_n, sub_n = (mesh.shape[a] for a in ("groups", "tm", "chan", "sub"))
    cs_n = chan_n * sub_n
    blocks = tm // cs_n

    def on_device(traces, templates, channel_mask):
        chans, tile = traces.shape
        rows, _, span = templates.shape
        coarse = span // FINE
        total = tm * tile
        n = tile // span
        out_rows = blocks * rows
        vmem = pl.BlockSpec(memory_space=pltpu.VMEM)
        f32, bf16 = jnp.float32, jnp.bfloat16
        dma = pltpu.SemaphoreType.DMA
        return pl.pallas_call(
            functools.partial(kernel, (group_n, tm, chan_n, sub_n)),
            out_shape=jax.ShapeDtypeStruct((out_rows, tile), f32),
            in_specs=[pl.BlockSpec(memory_space=pltpu.HBM)] * 3,
            out_specs=vmem,
            scratch_shapes=[
                pltpu.VMEM((chans, tile), bf16),
                pltpu.VMEM((rows, chans, span), bf16),
                pltpu.VMEM((rows, chans), jnp.int32),
                pltpu.VMEM((total, chans), bf16),
                pltpu.VMEM((coarse, FINE * rows, chans), f32),
                pltpu.VMEM((2 * FINE * rows, coarse * chans), bf16),
                pltpu.VMEM((2, rows, total), f32),
                pltpu.VMEM((blocks, cs_n, rows, tile), f32),
                pltpu.VMEM((blocks, chan_n, rows, 2 * span), f32),
                pltpu.VMEM((tm, rows, chans), f32),
                pltpu.VMEM((cs_n, out_rows, tile), f32),
                pltpu.VMEM((cs_n, rows, 2 * chans), f32),
                pltpu.VMEM((blocks, rows, LANES), f32),
                pltpu.VMEM((2, out_rows, span), f32),
                pltpu.VMEM((cs_n, out_rows, tile), f32),
                pltpu.VMEM((2, out_rows, tile), f32),
                dma((n * tm,)), dma((n * tm,)), dma((n * tm,)),
                dma((2, n * tm // 2)), dma((blocks, cs_n, n // 2)),
                dma(()), dma((blocks, chan_n)),
                dma((PIECES,)), dma((group_n, PIECES)), dma((group_n, PIECES)),
                dma((tm,)), dma((tm,)),
                dma((cs_n,)), dma((cs_n,)),
                dma(()), dma((cs_n,)),
                dma((tm,)), dma((blocks,)),
                dma((2,)),
                dma((3,)),
            ],
            compiler_params=pltpu.CompilerParams(collective_id=0, has_side_effects=True, vmem_limit_bytes=VMEM_LIMIT),
        )(*(pltpu.with_memory_space_constraint(a, pltpu.HBM)
            for a in (traces, templates, channel_mask)))

    placed = (
        P(("chan", "sub"), ("groups", "tm")),
        P("tm", ("chan", "sub"), None),
        P("tm", ("chan", "sub")),
    )
    return jax.shard_map(
        on_device,
        mesh=mesh,
        in_specs=placed,
        out_specs=P(("chan", "sub"), ("groups", "tm")),
        check_vma=False,
    )
```

```python
import functools

import jax
import jax.numpy as jnp
from jax import lax
from jax.experimental import pallas as pl
from jax.experimental.pallas import tpu as pltpu
from jax.sharding import PartitionSpec as P

EPSILON = 1e-06
MESH = pl.DeviceIdType.MESH
LANES = 128
FINE = 32
NT = (((1,), (1,)), ((), ()))
PIECES = 4
VMEM_LIMIT = 32 * 1024 * 1024


def is_outer(z, half):
    return (z % 2 == 0) == (z < half)


def kernel(sizes, x_hbm, w_hbm, m_hbm, o_ref, x_ref, w_ref, m_ref, xt, af, ab, acc, rb, rx, mk, pb, tp, fp, eh, es, ew,
           recv_sem, right_sem, left_sem, out_sem, in_sem, extra_sem,
           extrain_sem, wave_sem,
           wavein_sem, pass_sem, mask_sem, maskin_sem,
           pow_sem, powin_sem, te_sem, tein_sem, fac_sem, facin_sem, head_sem, load_sem):
    group_n, tm, chan_n, sub_n = sizes
    cs_n = chan_n * sub_n
    me = lax.axis_index("tm")
    my_chan = lax.axis_index("chan")
    my_sub = lax.axis_index("sub")
    my_cs = my_chan * sub_n + my_sub
    chans, tile = x_ref.shape
    rows, _, span = w_ref.shape
    blocks = tm // cs_n
    coarse = span // FINE
    total = tm * tile
    n = tile // span
    owner = me // blocks
    first = me * n
    my_group = lax.axis_index("groups")
    depth = FINE * rows
    piece = depth // (group_n * PIECES)
    half = tm // 2
    partner = me + 1 - 2 * lax.rem(me, 2)
    moves = my_sub == 0
    outer = is_outer(me, half)
    gives = jnp.logical_and(outer, moves)
    takes = jnp.logical_and(jnp.logical_not(outer), moves)
    low_end = jnp.where(moves, 1, 0)
    high_end = tm - 1 - low_end
    pair = 2 * span
    pairs = tile // pair
    switch = pairs

    def remote(src, dst, send, recv, to):
        return pltpu.make_async_remote_copy(
            src_ref=src, dst_ref=dst, send_sem=send, recv_sem=recv,
            device_id=to, device_id_type=MESH)

    def peer(d):
        return {"tm": lax.rem(me + d, tm)}

    def cs_place(c):
        return {"chan": c // sub_n, "sub": c % sub_n}

    loads = [pltpu.make_async_copy(src, dst, load_sem.at[i]) for i, (src, dst) in enumerate(
        ((m_hbm, m_ref), (x_hbm, x_ref), (w_hbm, w_ref)))]
    for load in loads:
        load.start()

    barrier = pltpu.get_barrier_semaphore()
    for d in range(1, tm):
        pl.semaphore_signal(barrier, inc=1, device_id=peer(d), device_id_type=MESH)
    for d in range(1, cs_n):
        pl.semaphore_signal(barrier, inc=1, device_id=cs_place(lax.rem(my_cs + d, cs_n)),
                            device_id_type=MESH)

    for d in range(1, group_n):
        pl.semaphore_signal(barrier, inc=1, device_id={"groups": lax.rem(my_group + d, group_n)},
                            device_id_type=MESH)

    loads[0].wait()
    mask = m_ref[...].astype(jnp.float32)
    mk[me] = mask
    loads[1].wait()
    xt[pl.ds(me * tile, tile), :] = jnp.transpose(x_ref[...])
    loads[2].wait()
    for k in range(rows):
        wave = jnp.transpose(w_ref[k].astype(jnp.float32)) * mask[k : k + 1, :]
        tp[my_cs, k : k + 1, 0:chans] = jnp.sum(wave * wave, axis=0, keepdims=True)
        for g in range(coarse):
            af[g, pl.ds(k, FINE, stride=rows), :] = wave[g * FINE : (g + 1) * FINE, :]
    for g in range(coarse):
        ab[0:depth, g * chans : (g + 1) * chans] = af[g].astype(jnp.bfloat16)
    tp[my_cs, :, chans : 2 * chans] = mask

    pl.semaphore_wait(barrier, tm - 1 + cs_n - 1 + group_n - 1)

    def mask_copy(d):
        return remote(mk.at[me], mk.at[me], mask_sem.at[d], maskin_sem.at[me], peer(d))

    for d in range(1, tm):
        mask_copy(d).start()

    def wave_copy(p, to):
        at = (my_group * PIECES + p) * piece
        return remote(ab.at[pl.ds(pl.multiple_of(at, piece), piece), :],
                      ab.at[pl.ds(pl.multiple_of(depth + at, piece), piece), :],
                      wave_sem.at[p], wavein_sem.at[my_group, p], {"tm": to})

    def pass_copy(p, d):
        at = pl.ds(pl.multiple_of(depth + (my_group * PIECES + p) * piece, piece), piece)
        return remote(ab.at[at, :], ab.at[at, :], pass_sem.at[d, p], wavein_sem.at[my_group, p],
                      {"groups": lax.rem(my_group + d, group_n)})

    @pl.when(gives)
    def _():
        for p in range(PIECES):
            wave_copy(p, partner).start()

    def relay(c, to, sem):
        part = pl.ds(pl.multiple_of(c * span, span), span)
        return remote(xt.at[part, :], xt.at[part, :], sem.at[c], recv_sem.at[c], {"tm": to})

    def send_own():
        for k in range(n):
            @pl.when(me < tm - 1)
            def _():
                relay(first + n - 1 - k, me + 1, right_sem).start()

            @pl.when(me > 0)
            def _():
                relay(first + k, me - 1, left_sem).start()

    send_own()

    def te_copy():
        return remote(tp.at[my_cs], tp.at[my_cs], te_sem, tein_sem.at[my_cs], cs_place(owner))

    @pl.when(my_cs != owner)
    def _():
        te_copy().start()

    acc[...] = jnp.zeros_like(acc)

    def spread(p):
        width = p.shape[1]
        pad = jnp.zeros((rows, LANES), jnp.float32)
        out = jnp.concatenate([pad, p[:rows]], 1)
        for b in range(1, FINE):
            one = jnp.concatenate([pad, p[b * rows : (b + 1) * rows]], 1)
            out = out + pltpu.roll(one, width + LANES - b, 1)
        return out

    def add_products(slots, right, start, before):
        low, high = slots[0] * depth, (slots[-1] + 1) * depth
        p = lax.dot_general(ab[low:high, :], right, NT, preferred_element_type=jnp.float32)
        for i, slot in enumerate(slots):
            out = spread(p[i * depth : (i + 1) * depth])
            acc[slot, :, pl.ds(before, LANES)] += out[:, :LANES]
            acc[slot, :, pl.ds(start, right.shape[0])] += out[:, LANES:]

    def process(c, width, slots):
        start = pl.multiple_of(c * span, span)
        before = pl.multiple_of(lax.rem(start + total - LANES, total), LANES)
        right = jnp.concatenate(
            [xt[pl.ds(pl.multiple_of(start + FINE * g, FINE), width), :] for g in range(coarse)],
            1)
        add_products(slots, right, start, before)

    def own(slots):
        process(first, tile - span, slots)

    def close(from_left, slots):
        wide = pair + span
        xt[total : total + wide, :] = xt[0:wide, :]
        start = pl.multiple_of(jnp.where(from_left, total - span, total - wide), span)
        right = jnp.concatenate(
            [xt[pl.ds(pl.multiple_of(start + FINE * g, FINE), wide), :] for g in range(coarse)], 1)
        p = lax.dot_general(ab[slots[0] * depth : (slots[-1] + 1) * depth, :], right, NT,
                            preferred_element_type=jnp.float32)
        for i, slot in enumerate(slots):
            out = spread(p[i * depth : (i + 1) * depth])
            acc[slot, :, pl.ds(pl.multiple_of(start - LANES, LANES), LANES)] += out[:, :LANES]
            for k in range(3):
                at = pl.multiple_of(lax.rem(start + k * span, total), span)
                low = LANES + k * span
                acc[slot, :, pl.ds(at, span)] += out[:, low : low + span]

    def block_of(slot):
        return partner if slot else me

    def holder(slot):
        return block_of(slot) // blocks

    def columns(o):
        return pl.ds(pl.multiple_of(o * pair, pair), pair)

    def out_copy(o, slot):
        q = block_of(slot) % blocks
        return remote(acc.at[slot, :, columns(o)], rb.at[q, my_cs, :, columns(lax.rem(o, pairs))],
                      out_sem.at[slot, o], in_sem.at[q, my_cs, lax.rem(o, pairs)],
                      {"tm": o // pairs, **cs_place(holder(slot))})

    def extra_copy(o, slot):
        q = block_of(slot) % blocks
        return remote(acc.at[slot, :, columns(o)], rx.at[q, my_chan],
                      extra_sem, extrain_sem.at[q, my_chan],
                      {"tm": o // pairs, **cs_place(holder(slot))})

    def is_local(o, slot):
        return jnp.logical_and(o // pairs == me, my_cs == holder(slot))

    def hand(o, slot):
        @pl.when(is_local(o, slot))
        def _():
            rb[block_of(slot) % blocks, my_cs, :, columns(lax.rem(o, pairs))] = (
                acc[slot, :, columns(o)])

        @pl.when(jnp.logical_not(is_local(o, slot)))
        def _():
            out_copy(o, slot).start()

    def hand_extra(o, slot):
        @pl.when(is_local(o, slot))
        def _():
            rx[block_of(slot) % blocks, my_chan] = acc[slot, :, columns(o)]

        @pl.when(jnp.logical_not(is_local(o, slot)))
        def _():
            extra_copy(o, slot).start()

    home = me * pairs
    low = me - lax.rem(me, 2)
    pair_last = (low + 2) * pairs - 1
    before_pair = lax.rem(low * pairs + tm * pairs - 1, tm * pairs)

    def hand_second(o):
        @pl.when(o == pair_last)
        def _():
            hand_extra(o, 1)

        @pl.when(o != pair_last)
        def _():
            hand(o, 1)

    def pow_copy(d):
        to = lax.rem(my_cs + d, cs_n)
        return remote(es.at[to], pb.at[my_cs], pow_sem.at[d], powin_sem.at[my_cs], cs_place(to))

    def power():
        for d in range(1, tm):
            who = lax.rem(me + d, tm)
            remote(mk.at[who], mk.at[who], mask_sem.at[0], maskin_sem.at[who],
                   {"tm": who}).wait_recv()
        masks = jnp.concatenate([mk[i] for i in range(tm)], 0).astype(jnp.bfloat16)
        x32 = xt[pl.ds(me * tile, tile), :].astype(jnp.float32)
        square = x32 * x32
        high = square.astype(jnp.bfloat16)
        low = (square - high.astype(jnp.float32)).astype(jnp.bfloat16)
        p = lax.dot_general(jnp.concatenate([masks, masks], 1), jnp.concatenate([high, low], 1),
                            NT, preferred_element_type=jnp.float32)
        for c in range(cs_n):
            es[c] = p[c * blocks * rows : (c + 1) * blocks * rows, :]
        pb[my_cs] = es[my_cs]
        for d in range(1, cs_n):
            pow_copy(d).start()

    def fac_copy(d):
        return remote(fp.at[me % blocks], fp.at[me % blocks], fac_sem.at[d],
                      facin_sem.at[me % blocks], peer(d))

    def template_sums():
        @pl.when(my_cs == owner)
        def _():
            for d in range(1, cs_n):
                who = lax.rem(my_cs + d, cs_n)
                remote(tp.at[who], tp.at[who], te_sem, tein_sem.at[who], cs_place(who)).wait_recv()
            t = tp[0]
            for c in range(1, cs_n):
                t = t + tp[c]
            te = jnp.sum(t[:, :chans], axis=1, keepdims=True)
            active = jnp.sum(t[:, chans:], axis=1, keepdims=True)
            lane = lax.broadcasted_iota(jnp.int32, (rows, LANES), 1)
            fp[me % blocks] = jnp.where(lane < LANES // 2, te, active)
            for d in range(1, tm):
                fac_copy(d).start()

    def head_copy():
        return remote(eh.at[0], eh.at[1], head_sem.at[0], head_sem.at[1],
                      {"tm": lax.rem(me + tm - 1, tm)})

    def windows():
        for d in range(1, cs_n):
            who = lax.rem(my_cs + d, cs_n)
            remote(es.at[who], pb.at[who], pow_sem.at[0], powin_sem.at[who],
                   cs_place(who)).wait_recv()
        p = pb[0]
        for c in range(1, cs_n):
            p = p + pb[c]
        p = jnp.concatenate([jnp.zeros((blocks * rows, span), jnp.float32), p], 1)
        by = 1
        while by < span:
            p = p + pltpu.roll(p, tile + span - by, 1)
            by *= 2
        eh[0] = p[:, :span]
        head_copy().start()
        ew[0] = p[:, span:]

    def norms():
        head_copy().wait_recv()
        for q in range(blocks):
            j = my_cs * blocks + q

            @pl.when(me != j)
            def _():
                remote(fp.at[q], fp.at[q], fac_sem.at[0], facin_sem.at[q], {"tm": j}).wait_recv()

            at = slice(q * rows, (q + 1) * rows)
            factor = jnp.sqrt(span * fp[q, :, LANES - 1 : LANES])
            energy = jnp.concatenate(
                [ew[0, at, : tile - span], ew[0, at, tile - span :] + eh[1, at, :]], 1)
            ew[1, at, :] = factor / jnp.sqrt(energy * fp[q, :, 0:1] + EPSILON)

    left_n = pairs * jnp.where(jnp.logical_and(moves, me == tm - 1), 1, me)
    right_n = pairs * jnp.where(jnp.logical_and(moves, me == 0), 1, tm - 1 - me)
    short = jnp.minimum(left_n, right_n)
    left_short = left_n < right_n
    steps = pairs * (tm - 1)

    def arrival(u):
        v = u - switch
        paired = u < 2 * short
        on_short = jnp.where(takes, jnp.logical_and(v >= 0, v < short),
                             jnp.logical_and(paired, lax.rem(u, 2) == 0))
        k = jnp.where(takes, jnp.where(v < 0, u, jnp.where(on_short, v, u - short)),
                      jnp.where(paired, u // 2, u - short))
        from_left = on_short == left_short
        return from_left, jnp.where(from_left, home - 1 - k, home + pairs + k)

    def made(u):
        from_left, o = arrival(u)
        return jnp.where(from_left, 2 * o, 2 * o - 1)

    def ended(u):
        from_left, o = arrival(u)
        return jnp.where(from_left, o, o - 1)

    own((0,))
    for o in range(pairs - 1):
        @pl.when(jnp.logical_not(jnp.logical_and(gives, lax.rem(me, 2) == 1)))
        def _():
            hand(home + o, 0)

    power()

    def step(u, final):
        live = u < left_n + right_n
        from_left, o = arrival(u)
        per = PIECES // switch

        @pl.when(jnp.logical_and(takes, u < switch))
        def _():
            for i in range(per):
                p = jnp.minimum(u, switch - 1) * per + i
                remote(ab.at[pl.ds(0, piece), :], ab.at[pl.ds(0, piece), :], wave_sem.at[0],
                       wavein_sem.at[my_group, p], {"tm": partner}).wait_recv()
                for d in range(1, group_n):
                    pass_copy(p, d).start()

        @pl.when(jnp.logical_and(live, from_left))
        def _():
            for i in (1, 0):
                relay(2 * o + i, me, right_sem).wait_recv()

                @pl.when(me < high_end)
                def _():
                    relay(2 * o + i, me + 1, right_sem).start()

        @pl.when(jnp.logical_and(live, jnp.logical_not(from_left)))
        def _():
            for i in (0, 1):
                relay(2 * o + i, me, left_sem).wait_recv()

                @pl.when(me > low_end)
                def _():
                    relay(2 * o + i, me - 1, left_sem).start()

        @pl.when(jnp.logical_and(takes, u == switch + 1))
        def _():
            for d in range(1, group_n):
                who = lax.rem(my_group + d, group_n)
                for p in range(PIECES):
                    remote(ab.at[pl.ds(0, piece), :], ab.at[pl.ds(0, piece), :], wave_sem.at[0],
                           wavein_sem.at[who, p], {"groups": who}).wait_recv()

        both = jnp.logical_and(takes, u >= switch + pairs)
        if final:
            @pl.when(takes)
            def _():
                close(from_left, (0, 1))
                hand(ended(u), 0)
                hand_second(ended(u))
                hand(tm * pairs - 1, 0)
                hand_second(tm * pairs - 1)

            @pl.when(jnp.logical_not(moves))
            def _():
                close(from_left, (0,))
                hand(ended(u), 0)
                hand(tm * pairs - 1, 0)

            @pl.when(gives)
            def _():
                for o in range(2 * pairs):
                    at = low * pairs + o

                    @pl.when(jnp.logical_or(lax.rem(me, 2) == 1, o >= pairs - 1))
                    def _():
                        hand(at, 0)
                hand_extra(before_pair, 0)

            return

        @pl.when(jnp.logical_or(
            jnp.logical_and(gives, jnp.logical_and(live, o // pairs == partner)),
            jnp.logical_and(jnp.logical_not(gives), jnp.logical_not(jnp.logical_or(
                both, jnp.logical_and(takes, u == switch + 1))))))
        def _():
            process(made(u), pair, (0,))

        @pl.when(jnp.logical_and(takes, u == switch + 1))
        def _():
            process(made(u), pair, (0,))
            process(jnp.minimum(made(0), made(switch - 1)), switch * pair, (1,))
            for v in range(switch):
                hand_second(ended(v))

        @pl.when(both)
        def _():
            process(made(u), pair, (0, 1))
            hand_second(ended(u))

        @pl.when(jnp.logical_not(gives))
        def _():
            hand(ended(u), 0)

        @pl.when(u == 0)
        def _():
            template_sums()

        @pl.when(u == 2)
        def _():
            windows()

    def loop(u, carry):
        step(u, False)
        return carry

    lax.fori_loop(0, steps - 1, loop, 0)
    step(steps - 1, True)

    norms()

    def finish(c, carry):
        @pl.when(jnp.logical_or(jnp.logical_and(me < high_end, c // n < me),
                                jnp.logical_and(me < tm - 1, c // n == me)))
        def _():
            relay(c, me, right_sem).wait_send()

        @pl.when(jnp.logical_or(jnp.logical_and(me > low_end, c // n > me),
                                jnp.logical_and(me > 0, c // n == me)))
        def _():
            relay(c, me, left_sem).wait_send()

        return carry

    lax.fori_loop(0, n * tm, finish, 0)

    def finish_out(o, carry):
        in_pair = o // (2 * pairs) == me // 2

        @pl.when(jnp.logical_and(jnp.logical_or(jnp.logical_not(gives), in_pair),
                                 jnp.logical_not(is_local(o, 0))))
        def _():
            out_copy(o, 0).wait_send()

        @pl.when(jnp.logical_and(jnp.logical_and(takes, jnp.logical_not(in_pair)),
                                 jnp.logical_not(is_local(o, 1))))
        def _():
            out_copy(o, 1).wait_send()

        return carry

    lax.fori_loop(0, pairs * tm, finish_out, 0)

    @pl.when(jnp.logical_and(gives, jnp.logical_not(is_local(before_pair, 0))))
    def _():
        extra_copy(before_pair, 0).wait_send()

    @pl.when(jnp.logical_and(takes, jnp.logical_not(is_local(pair_last, 1))))
    def _():
        extra_copy(pair_last, 1).wait_send()
    for p in range(PIECES):
        @pl.when(gives)
        def _():
            wave_copy(p, partner).wait_send()

        @pl.when(takes)
        def _():
            for d in range(1, group_n):
                pass_copy(p, d).wait_send()

    for d in range(1, tm):
        mask_copy(d).wait_send()
    for d in range(1, cs_n):
        pow_copy(d).wait_send()

    @pl.when(my_cs != owner)
    def _():
        te_copy().wait_send()

    @pl.when(my_cs == owner)
    def _():
        for d in range(1, tm):
            fac_copy(d).wait_send()

    head_copy().wait_send()

    for q in range(blocks):
        b = my_cs * blocks + q
        b_outer = is_outer(b, half)
        for slot in range(cs_n):
            moved = slot % sub_n == 0
            inner = b + 1 - 2 * lax.rem(b, 2)
            apart = jnp.logical_and(b_outer, me // 2 != b // 2)
            source = jnp.where(apart, inner, b) if moved else b

            @pl.when(jnp.logical_not(jnp.logical_and(my_cs == slot, source == me)))
            def _():
                for k in range(pairs):
                    remote(acc.at[0, :, pl.ds(0, pair)],
                           rb.at[q, slot, :, pl.ds(k * pair, pair)], out_sem.at[0, 0],
                           in_sem.at[q, slot, k], {"tm": lax.rem(me + 1, tm)}).wait_recv()

        at = slice(q * rows, (q + 1) * rows)
        result = rb[q, 0]
        for c in range(1, cs_n):
            result = result + rb[q, c]
        b_low = b - lax.rem(b, 2)
        tail = jnp.logical_and(b_outer, me == b_low + 1)
        ahead = jnp.logical_and(b_outer, me == lax.rem(b_low + tm - 1, tm))
        for c in range(chan_n):
            source = jnp.where(me == b_low + 1, inner, b)
            near_me = jnp.logical_and(jnp.logical_and(my_sub == 0, my_chan == c), source == me)

            @pl.when(jnp.logical_and(jnp.logical_or(tail, ahead), jnp.logical_not(near_me)))
            def _():
                remote(acc.at[0, :, pl.ds(0, pair)], rx.at[q, c], out_sem.at[0, 0],
                       extrain_sem.at[q, c], {"tm": lax.rem(me + 1, tm)}).wait_recv()

        o_ref[at, :] = result * ew[1, at, :]

        @pl.when(jnp.logical_or(tail, ahead))
        def _():
            more = rx[q, 0]
            for c in range(1, chan_n):
                more = more + rx[q, c]
            whole = slice(tile - pair, tile)
            o_ref[at, whole] = (result[:, whole] + more) * ew[1, at, whole]


def solution(mesh):
    group_n, tm, chan_n, sub_n = (mesh.shape[a] for a in ("groups", "tm", "chan", "sub"))
    cs_n = chan_n * sub_n
    blocks = tm // cs_n

    def on_device(traces, templates, channel_mask):
        chans, tile = traces.shape
        rows, _, span = templates.shape
        coarse = span // FINE
        total = tm * tile
        n = tile // span
        out_rows = blocks * rows
        vmem = pl.BlockSpec(memory_space=pltpu.VMEM)
        f32, bf16 = jnp.float32, jnp.bfloat16
        dma = pltpu.SemaphoreType.DMA
        return pl.pallas_call(
            functools.partial(kernel, (group_n, tm, chan_n, sub_n)),
            out_shape=jax.ShapeDtypeStruct((out_rows, tile), f32),
            in_specs=[pl.BlockSpec(memory_space=pltpu.HBM)] * 3,
            out_specs=vmem,
            scratch_shapes=[
                pltpu.VMEM((chans, tile), bf16),
                pltpu.VMEM((rows, chans, span), bf16),
                pltpu.VMEM((rows, chans), jnp.int32),
                pltpu.VMEM((total + 3 * span, chans), bf16),
                pltpu.VMEM((coarse, FINE * rows, chans), f32),
                pltpu.VMEM((2 * FINE * rows, coarse * chans), bf16),
                pltpu.VMEM((2, rows, total), f32),
                pltpu.VMEM((blocks, cs_n, rows, tile), f32),
                pltpu.VMEM((blocks, chan_n, rows, 2 * span), f32),
                pltpu.VMEM((tm, rows, chans), f32),
                pltpu.VMEM((cs_n, out_rows, tile), f32),
                pltpu.VMEM((cs_n, rows, 2 * chans), f32),
                pltpu.VMEM((blocks, rows, LANES), f32),
                pltpu.VMEM((2, out_rows, span), f32),
                pltpu.VMEM((cs_n, out_rows, tile), f32),
                pltpu.VMEM((2, out_rows, tile), f32),
                dma((n * tm,)), dma((n * tm,)), dma((n * tm,)),
                dma((2, n * tm // 2)), dma((blocks, cs_n, n // 2)),
                dma(()), dma((blocks, chan_n)),
                dma((PIECES,)), dma((group_n, PIECES)), dma((group_n, PIECES)),
                dma((tm,)), dma((tm,)),
                dma((cs_n,)), dma((cs_n,)),
                dma(()), dma((cs_n,)),
                dma((tm,)), dma((blocks,)),
                dma((2,)),
                dma((3,)),
            ],
            compiler_params=pltpu.CompilerParams(collective_id=0, has_side_effects=True, vmem_limit_bytes=VMEM_LIMIT),
        )(*(pltpu.with_memory_space_constraint(a, pltpu.HBM)
            for a in (traces, templates, channel_mask)))

    placed = (
        P(("chan", "sub"), ("groups", "tm")),
        P("tm", ("chan", "sub"), None),
        P("tm", ("chan", "sub")),
    )
    return jax.shard_map(
        on_device,
        mesh=mesh,
        in_specs=placed,
        out_specs=P(("chan", "sub"), ("groups", "tm")),
        check_vma=False,
    )
```

```python
import functools

import jax
import jax.numpy as jnp
from jax import lax
from jax.experimental import pallas as pl
from jax.experimental.pallas import tpu as pltpu
from jax.sharding import PartitionSpec as P

EPSILON = 1e-06
MESH = pl.DeviceIdType.MESH
LANES = 128
FINE = 32
NT = (((1,), (1,)), ((), ()))
PIECES = 2
VMEM_LIMIT = 32 * 1024 * 1024


def is_outer(z, half):
    return (z % 2 == 0) == (z < half)


def kernel(sizes, x_hbm, w_hbm, m_hbm, o_ref, x_ref, w_ref, m_ref, xt, af, ab, acc, rb, rx, mk, pb, tp, fp, eh, es, ew,
           recv_sem, right_sem, left_sem, out_sem, in_sem, extra_sem,
           extrain_sem, wave_sem,
           wavein_sem, pass_sem, mask_sem, maskin_sem,
           pow_sem, powin_sem, te_sem, tein_sem, fac_sem, facin_sem, head_sem, load_sem):
    group_n, tm, chan_n, sub_n = sizes
    cs_n = chan_n * sub_n
    me = lax.axis_index("tm")
    my_chan = lax.axis_index("chan")
    my_sub = lax.axis_index("sub")
    my_cs = my_chan * sub_n + my_sub
    chans, tile = x_ref.shape
    rows, _, span = w_ref.shape
    blocks = tm // cs_n
    coarse = span // FINE
    total = tm * tile
    n = tile // span
    owner = me // blocks
    first = me * n
    my_group = lax.axis_index("groups")
    depth = FINE * rows
    piece = depth // (group_n * PIECES)
    half = tm // 2
    partner = me + 1 - 2 * lax.rem(me, 2)
    moves = my_sub == 0
    outer = is_outer(me, half)
    gives = jnp.logical_and(outer, moves)
    takes = jnp.logical_and(jnp.logical_not(outer), moves)
    low_end = jnp.where(moves, 1, 0)
    high_end = tm - 1 - low_end
    pair = 2 * span
    pairs = tile // pair
    switch = pairs

    def remote(src, dst, send, recv, to):
        return pltpu.make_async_remote_copy(
            src_ref=src, dst_ref=dst, send_sem=send, recv_sem=recv,
            device_id=to, device_id_type=MESH)

    def peer(d):
        return {"tm": lax.rem(me + d, tm)}

    def cs_place(c):
        return {"chan": c // sub_n, "sub": c % sub_n}

    loads = [pltpu.make_async_copy(src, dst, load_sem.at[i]) for i, (src, dst) in enumerate(
        ((m_hbm, m_ref), (x_hbm, x_ref), (w_hbm, w_ref)))]
    for load in loads:
        load.start()

    barrier = pltpu.get_barrier_semaphore()
    for d in range(1, tm):
        pl.semaphore_signal(barrier, inc=1, device_id=peer(d), device_id_type=MESH)
    for d in range(1, cs_n):
        pl.semaphore_signal(barrier, inc=1, device_id=cs_place(lax.rem(my_cs + d, cs_n)),
                            device_id_type=MESH)

    for d in range(1, group_n):
        pl.semaphore_signal(barrier, inc=1, device_id={"groups": lax.rem(my_group + d, group_n)},
                            device_id_type=MESH)

    loads[0].wait()
    mask = m_ref[...].astype(jnp.float32)
    mk[me] = mask
    loads[1].wait()
    xt[pl.ds(me * tile, tile), :] = jnp.transpose(x_ref[...])
    loads[2].wait()
    for k in range(rows):
        wave = jnp.transpose(w_ref[k].astype(jnp.float32)) * mask[k : k + 1, :]
        tp[my_cs, k : k + 1, 0:chans] = jnp.sum(wave * wave, axis=0, keepdims=True)
        for g in range(coarse):
            af[g, pl.ds(k, FINE, stride=rows), :] = wave[g * FINE : (g + 1) * FINE, :]
    for g in range(coarse):
        ab[0:depth, g * chans : (g + 1) * chans] = af[g].astype(jnp.bfloat16)
    tp[my_cs, :, chans : 2 * chans] = mask

    pl.semaphore_wait(barrier, tm - 1 + cs_n - 1 + group_n - 1)

    def mask_copy(d):
        return remote(mk.at[me], mk.at[me], mask_sem.at[d], maskin_sem.at[me], peer(d))

    for d in range(1, tm):
        mask_copy(d).start()

    def wave_copy(p, to):
        at = (my_group * PIECES + p) * piece
        return remote(ab.at[pl.ds(pl.multiple_of(at, piece), piece), :],
                      ab.at[pl.ds(pl.multiple_of(depth + at, piece), piece), :],
                      wave_sem.at[p], wavein_sem.at[my_group, p], {"tm": to})

    def pass_copy(p, d):
        at = pl.ds(pl.multiple_of(depth + (my_group * PIECES + p) * piece, piece), piece)
        return remote(ab.at[at, :], ab.at[at, :], pass_sem.at[d, p], wavein_sem.at[my_group, p],
                      {"groups": lax.rem(my_group + d, group_n)})

    @pl.when(gives)
    def _():
        for p in range(PIECES):
            wave_copy(p, partner).start()

    def relay(c, to, sem):
        part = pl.ds(pl.multiple_of(c * span, span), span)
        return remote(xt.at[part, :], xt.at[part, :], sem.at[c], recv_sem.at[c], {"tm": to})

    def send_own():
        for k in range(n):
            @pl.when(me < tm - 1)
            def _():
                relay(first + n - 1 - k, me + 1, right_sem).start()

            @pl.when(me > 0)
            def _():
                relay(first + k, me - 1, left_sem).start()

    send_own()

    def te_copy():
        return remote(tp.at[my_cs], tp.at[my_cs], te_sem, tein_sem.at[my_cs], cs_place(owner))

    @pl.when(my_cs != owner)
    def _():
        te_copy().start()

    acc[...] = jnp.zeros_like(acc)

    def spread(p):
        width = p.shape[1]
        pad = jnp.zeros((rows, LANES), jnp.float32)
        out = jnp.concatenate([pad, p[:rows]], 1)
        for b in range(1, FINE):
            one = jnp.concatenate([pad, p[b * rows : (b + 1) * rows]], 1)
            out = out + pltpu.roll(one, width + LANES - b, 1)
        return out

    def add_products(slots, right, start, before):
        for slot in slots:
            out = spread(lax.dot_general(ab[slot * depth : (slot + 1) * depth, :], right, NT,
                                         preferred_element_type=jnp.float32))
            acc[slot, :, pl.ds(before, LANES)] += out[:, :LANES]
            acc[slot, :, pl.ds(start, right.shape[0])] += out[:, LANES:]

    def process(c, width, slots):
        start = pl.multiple_of(c * span, span)
        before = pl.multiple_of(lax.rem(start + total - LANES, total), LANES)
        right = jnp.concatenate(
            [xt[pl.ds(pl.multiple_of(start + FINE * g, FINE), width), :] for g in range(coarse)],
            1)
        add_products(slots, right, start, before)

    def own(slots):
        process(first, tile - span, slots)

    def close(from_left, slots):
        wide = pair + span
        xt[total : total + wide, :] = xt[0:wide, :]
        start = pl.multiple_of(jnp.where(from_left, total - span, total - wide), span)
        right = jnp.concatenate(
            [xt[pl.ds(pl.multiple_of(start + FINE * g, FINE), wide), :] for g in range(coarse)], 1)
        for slot in slots:
            out = spread(lax.dot_general(ab[slot * depth : (slot + 1) * depth, :], right, NT,
                                         preferred_element_type=jnp.float32))
            acc[slot, :, pl.ds(pl.multiple_of(start - LANES, LANES), LANES)] += out[:, :LANES]
            for k in range(3):
                at = pl.multiple_of(lax.rem(start + k * span, total), span)
                low = LANES + k * span
                acc[slot, :, pl.ds(at, span)] += out[:, low : low + span]

    def block_of(slot):
        return partner if slot else me

    def holder(slot):
        return block_of(slot) // blocks

    def columns(o):
        return pl.ds(pl.multiple_of(o * pair, pair), pair)

    def out_copy(o, slot):
        q = block_of(slot) % blocks
        return remote(acc.at[slot, :, columns(o)], rb.at[q, my_cs, :, columns(lax.rem(o, pairs))],
                      out_sem.at[slot, o], in_sem.at[q, my_cs, lax.rem(o, pairs)],
                      {"tm": o // pairs, **cs_place(holder(slot))})

    def extra_copy(o, slot):
        q = block_of(slot) % blocks
        return remote(acc.at[slot, :, columns(o)], rx.at[q, my_chan],
                      extra_sem, extrain_sem.at[q, my_chan],
                      {"tm": o // pairs, **cs_place(holder(slot))})

    def is_local(o, slot):
        return jnp.logical_and(o // pairs == me, my_cs == holder(slot))

    def hand(o, slot):
        @pl.when(is_local(o, slot))
        def _():
            rb[block_of(slot) % blocks, my_cs, :, columns(lax.rem(o, pairs))] = (
                acc[slot, :, columns(o)])

        @pl.when(jnp.logical_not(is_local(o, slot)))
        def _():
            out_copy(o, slot).start()

    def hand_extra(o, slot):
        @pl.when(is_local(o, slot))
        def _():
            rx[block_of(slot) % blocks, my_chan] = acc[slot, :, columns(o)]

        @pl.when(jnp.logical_not(is_local(o, slot)))
        def _():
            extra_copy(o, slot).start()

    home = me * pairs
    low = me - lax.rem(me, 2)
    pair_last = (low + 2) * pairs - 1
    before_pair = lax.rem(low * pairs + tm * pairs - 1, tm * pairs)

    def hand_second(o):
        @pl.when(o == pair_last)
        def _():
            hand_extra(o, 1)

        @pl.when(o != pair_last)
        def _():
            hand(o, 1)

    def pow_copy(d):
        to = lax.rem(my_cs + d, cs_n)
        return remote(es.at[to], pb.at[my_cs], pow_sem.at[d], powin_sem.at[my_cs], cs_place(to))

    def power():
        for d in range(1, tm):
            who = lax.rem(me + d, tm)
            remote(mk.at[who], mk.at[who], mask_sem.at[0], maskin_sem.at[who],
                   {"tm": who}).wait_recv()
        masks = jnp.concatenate([mk[i] for i in range(tm)], 0).astype(jnp.bfloat16)
        x32 = xt[pl.ds(me * tile, tile), :].astype(jnp.float32)
        square = x32 * x32
        high = square.astype(jnp.bfloat16)
        low = (square - high.astype(jnp.float32)).astype(jnp.bfloat16)
        p = lax.dot_general(jnp.concatenate([masks, masks], 1), jnp.concatenate([high, low], 1),
                            NT, preferred_element_type=jnp.float32)
        for c in range(cs_n):
            es[c] = p[c * blocks * rows : (c + 1) * blocks * rows, :]
        pb[my_cs] = es[my_cs]
        for d in range(1, cs_n):
            pow_copy(d).start()

    def fac_copy(d):
        return remote(fp.at[me % blocks], fp.at[me % blocks], fac_sem.at[d],
                      facin_sem.at[me % blocks], peer(d))

    def template_sums():
        @pl.when(my_cs == owner)
        def _():
            for d in range(1, cs_n):
                who = lax.rem(my_cs + d, cs_n)
                remote(tp.at[who], tp.at[who], te_sem, tein_sem.at[who], cs_place(who)).wait_recv()
            t = tp[0]
            for c in range(1, cs_n):
                t = t + tp[c]
            te = jnp.sum(t[:, :chans], axis=1, keepdims=True)
            active = jnp.sum(t[:, chans:], axis=1, keepdims=True)
            lane = lax.broadcasted_iota(jnp.int32, (rows, LANES), 1)
            fp[me % blocks] = jnp.where(lane < LANES // 2, te, active)
            for d in range(1, tm):
                fac_copy(d).start()

    def head_copy():
        return remote(eh.at[0], eh.at[1], head_sem.at[0], head_sem.at[1],
                      {"tm": lax.rem(me + tm - 1, tm)})

    def windows():
        for d in range(1, cs_n):
            who = lax.rem(my_cs + d, cs_n)
            remote(es.at[who], pb.at[who], pow_sem.at[0], powin_sem.at[who],
                   cs_place(who)).wait_recv()
        p = pb[0]
        for c in range(1, cs_n):
            p = p + pb[c]
        p = jnp.concatenate([jnp.zeros((blocks * rows, span), jnp.float32), p], 1)
        by = 1
        while by < span:
            p = p + pltpu.roll(p, tile + span - by, 1)
            by *= 2
        eh[0] = p[:, :span]
        head_copy().start()
        ew[0] = p[:, span:]

    def norms():
        head_copy().wait_recv()
        for q in range(blocks):
            j = my_cs * blocks + q

            @pl.when(me != j)
            def _():
                remote(fp.at[q], fp.at[q], fac_sem.at[0], facin_sem.at[q], {"tm": j}).wait_recv()

            at = slice(q * rows, (q + 1) * rows)
            factor = jnp.sqrt(span * fp[q, :, LANES - 1 : LANES])
            energy = jnp.concatenate(
                [ew[0, at, : tile - span], ew[0, at, tile - span :] + eh[1, at, :]], 1)
            ew[1, at, :] = factor / jnp.sqrt(energy * fp[q, :, 0:1] + EPSILON)

    left_n = pairs * jnp.where(jnp.logical_and(moves, me == tm - 1), 1, me)
    right_n = pairs * jnp.where(jnp.logical_and(moves, me == 0), 1, tm - 1 - me)
    short = jnp.minimum(left_n, right_n)
    left_short = left_n < right_n
    steps = pairs * (tm - 1)

    def arrival(u):
        v = u - switch
        paired = u < 2 * short
        on_short = jnp.where(takes, jnp.logical_and(v >= 0, v < short),
                             jnp.logical_and(paired, lax.rem(u, 2) == 0))
        k = jnp.where(takes, jnp.where(v < 0, u, jnp.where(on_short, v, u - short)),
                      jnp.where(paired, u // 2, u - short))
        from_left = on_short == left_short
        return from_left, jnp.where(from_left, home - 1 - k, home + pairs + k)

    def made(u):
        from_left, o = arrival(u)
        return jnp.where(from_left, 2 * o, 2 * o - 1)

    def ended(u):
        from_left, o = arrival(u)
        return jnp.where(from_left, o, o - 1)

    own((0,))
    for o in range(pairs - 1):
        @pl.when(jnp.logical_not(jnp.logical_and(gives, lax.rem(me, 2) == 1)))
        def _():
            hand(home + o, 0)

    power()

    def step(u, final):
        live = u < left_n + right_n
        from_left, o = arrival(u)
        per = PIECES // switch

        @pl.when(jnp.logical_and(takes, u < switch))
        def _():
            for i in range(per):
                p = jnp.minimum(u, switch - 1) * per + i
                remote(ab.at[pl.ds(0, piece), :], ab.at[pl.ds(0, piece), :], wave_sem.at[0],
                       wavein_sem.at[my_group, p], {"tm": partner}).wait_recv()
                for d in range(1, group_n):
                    pass_copy(p, d).start()

        @pl.when(jnp.logical_and(live, from_left))
        def _():
            for i in (1, 0):
                relay(2 * o + i, me, right_sem).wait_recv()

                @pl.when(me < high_end)
                def _():
                    relay(2 * o + i, me + 1, right_sem).start()

        @pl.when(jnp.logical_and(live, jnp.logical_not(from_left)))
        def _():
            for i in (0, 1):
                relay(2 * o + i, me, left_sem).wait_recv()

                @pl.when(me > low_end)
                def _():
                    relay(2 * o + i, me - 1, left_sem).start()

        @pl.when(jnp.logical_and(takes, u == switch + 1))
        def _():
            for d in range(1, group_n):
                who = lax.rem(my_group + d, group_n)
                for p in range(PIECES):
                    remote(ab.at[pl.ds(0, piece), :], ab.at[pl.ds(0, piece), :], wave_sem.at[0],
                           wavein_sem.at[who, p], {"groups": who}).wait_recv()

        both = jnp.logical_and(takes, u >= switch + pairs)
        if final:
            @pl.when(takes)
            def _():
                close(from_left, (0, 1))
                hand(ended(u), 0)
                hand_second(ended(u))
                hand(tm * pairs - 1, 0)
                hand_second(tm * pairs - 1)

            @pl.when(jnp.logical_not(moves))
            def _():
                close(from_left, (0,))
                hand(ended(u), 0)
                hand(tm * pairs - 1, 0)

            @pl.when(gives)
            def _():
                for o in range(2 * pairs):
                    at = low * pairs + o

                    @pl.when(jnp.logical_or(lax.rem(me, 2) == 1, o >= pairs - 1))
                    def _():
                        hand(at, 0)
                hand_extra(before_pair, 0)

            return

        @pl.when(jnp.logical_or(
            jnp.logical_and(gives, jnp.logical_and(live, o // pairs == partner)),
            jnp.logical_and(jnp.logical_not(gives), jnp.logical_not(jnp.logical_or(
                both, jnp.logical_and(takes, u == switch + 1))))))
        def _():
            process(made(u), pair, (0,))

        @pl.when(jnp.logical_and(takes, u == switch + 1))
        def _():
            process(made(u), pair, (0,))
            process(jnp.minimum(made(0), made(switch - 1)), switch * pair, (1,))
            for v in range(switch):
                hand_second(ended(v))

        @pl.when(both)
        def _():
            process(made(u), pair, (0, 1))
            hand_second(ended(u))

        hold = jnp.where(takes, switch, steps - 2)

        @pl.when(jnp.logical_and(jnp.logical_not(gives), u >= hold))
        def _():
            def hand_on(v, carry):
                hand(ended(v), 0)
                return carry

            lax.fori_loop(jnp.where(u == hold, 0, u), u + 1, hand_on, 0)

        @pl.when(u == jnp.where(moves, 0, 3))
        def _():
            template_sums()

        @pl.when(u == jnp.where(moves, 0, 2))
        def _():
            windows()

    def loop(u, carry):
        step(u, False)
        return carry

    lax.fori_loop(0, steps - 1, loop, 0)
    step(steps - 1, True)

    norms()

    def finish(c, carry):
        @pl.when(jnp.logical_or(jnp.logical_and(me < high_end, c // n < me),
                                jnp.logical_and(me < tm - 1, c // n == me)))
        def _():
            relay(c, me, right_sem).wait_send()

        @pl.when(jnp.logical_or(jnp.logical_and(me > low_end, c // n > me),
                                jnp.logical_and(me > 0, c // n == me)))
        def _():
            relay(c, me, left_sem).wait_send()

        return carry

    lax.fori_loop(0, n * tm, finish, 0)

    def finish_out(o, carry):
        in_pair = o // (2 * pairs) == me // 2

        @pl.when(jnp.logical_and(jnp.logical_or(jnp.logical_not(gives), in_pair),
                                 jnp.logical_not(is_local(o, 0))))
        def _():
            out_copy(o, 0).wait_send()

        @pl.when(jnp.logical_and(jnp.logical_and(takes, jnp.logical_not(in_pair)),
                                 jnp.logical_not(is_local(o, 1))))
        def _():
            out_copy(o, 1).wait_send()

        return carry

    lax.fori_loop(0, pairs * tm, finish_out, 0)

    @pl.when(jnp.logical_and(gives, jnp.logical_not(is_local(before_pair, 0))))
    def _():
        extra_copy(before_pair, 0).wait_send()

    @pl.when(jnp.logical_and(takes, jnp.logical_not(is_local(pair_last, 1))))
    def _():
        extra_copy(pair_last, 1).wait_send()
    for p in range(PIECES):
        @pl.when(gives)
        def _():
            wave_copy(p, partner).wait_send()

        @pl.when(takes)
        def _():
            for d in range(1, group_n):
                pass_copy(p, d).wait_send()

    for d in range(1, tm):
        mask_copy(d).wait_send()
    for d in range(1, cs_n):
        pow_copy(d).wait_send()

    @pl.when(my_cs != owner)
    def _():
        te_copy().wait_send()

    @pl.when(my_cs == owner)
    def _():
        for d in range(1, tm):
            fac_copy(d).wait_send()

    head_copy().wait_send()

    for q in range(blocks):
        b = my_cs * blocks + q
        b_outer = is_outer(b, half)
        for slot in range(cs_n):
            moved = slot % sub_n == 0
            inner = b + 1 - 2 * lax.rem(b, 2)
            apart = jnp.logical_and(b_outer, me // 2 != b // 2)
            source = jnp.where(apart, inner, b) if moved else b

            @pl.when(jnp.logical_not(jnp.logical_and(my_cs == slot, source == me)))
            def _():
                for k in range(pairs):
                    remote(acc.at[0, :, pl.ds(0, pair)],
                           rb.at[q, slot, :, pl.ds(k * pair, pair)], out_sem.at[0, 0],
                           in_sem.at[q, slot, k], {"tm": lax.rem(me + 1, tm)}).wait_recv()

        at = slice(q * rows, (q + 1) * rows)
        result = rb[q, 0]
        for c in range(1, cs_n):
            result = result + rb[q, c]
        b_low = b - lax.rem(b, 2)
        tail = jnp.logical_and(b_outer, me == b_low + 1)
        ahead = jnp.logical_and(b_outer, me == lax.rem(b_low + tm - 1, tm))
        for c in range(chan_n):
            source = jnp.where(me == b_low + 1, inner, b)
            near_me = jnp.logical_and(jnp.logical_and(my_sub == 0, my_chan == c), source == me)

            @pl.when(jnp.logical_and(jnp.logical_or(tail, ahead), jnp.logical_not(near_me)))
            def _():
                remote(acc.at[0, :, pl.ds(0, pair)], rx.at[q, c], out_sem.at[0, 0],
                       extrain_sem.at[q, c], {"tm": lax.rem(me + 1, tm)}).wait_recv()

        o_ref[at, :] = result * ew[1, at, :]

        @pl.when(jnp.logical_or(tail, ahead))
        def _():
            more = rx[q, 0]
            for c in range(1, chan_n):
                more = more + rx[q, c]
            whole = slice(tile - pair, tile)
            o_ref[at, whole] = (result[:, whole] + more) * ew[1, at, whole]


def solution(mesh):
    group_n, tm, chan_n, sub_n = (mesh.shape[a] for a in ("groups", "tm", "chan", "sub"))
    cs_n = chan_n * sub_n
    blocks = tm // cs_n

    def on_device(traces, templates, channel_mask):
        chans, tile = traces.shape
        rows, _, span = templates.shape
        coarse = span // FINE
        total = tm * tile
        n = tile // span
        out_rows = blocks * rows
        vmem = pl.BlockSpec(memory_space=pltpu.VMEM)
        f32, bf16 = jnp.float32, jnp.bfloat16
        dma = pltpu.SemaphoreType.DMA
        return pl.pallas_call(
            functools.partial(kernel, (group_n, tm, chan_n, sub_n)),
            out_shape=jax.ShapeDtypeStruct((out_rows, tile), f32),
            in_specs=[pl.BlockSpec(memory_space=pltpu.HBM)] * 3,
            out_specs=vmem,
            scratch_shapes=[
                pltpu.VMEM((chans, tile), bf16),
                pltpu.VMEM((rows, chans, span), bf16),
                pltpu.VMEM((rows, chans), jnp.int32),
                pltpu.VMEM((total + 3 * span, chans), bf16),
                pltpu.VMEM((coarse, FINE * rows, chans), f32),
                pltpu.VMEM((2 * FINE * rows, coarse * chans), bf16),
                pltpu.VMEM((2, rows, total), f32),
                pltpu.VMEM((blocks, cs_n, rows, tile), f32),
                pltpu.VMEM((blocks, chan_n, rows, 2 * span), f32),
                pltpu.VMEM((tm, rows, chans), f32),
                pltpu.VMEM((cs_n, out_rows, tile), f32),
                pltpu.VMEM((cs_n, rows, 2 * chans), f32),
                pltpu.VMEM((blocks, rows, LANES), f32),
                pltpu.VMEM((2, out_rows, span), f32),
                pltpu.VMEM((cs_n, out_rows, tile), f32),
                pltpu.VMEM((2, out_rows, tile), f32),
                dma((n * tm,)), dma((n * tm,)), dma((n * tm,)),
                dma((2, n * tm // 2)), dma((blocks, cs_n, n // 2)),
                dma(()), dma((blocks, chan_n)),
                dma((PIECES,)), dma((group_n, PIECES)), dma((group_n, PIECES)),
                dma((tm,)), dma((tm,)),
                dma((cs_n,)), dma((cs_n,)),
                dma(()), dma((cs_n,)),
                dma((tm,)), dma((blocks,)),
                dma((2,)),
                dma((3,)),
            ],
            compiler_params=pltpu.CompilerParams(collective_id=0, has_side_effects=True, vmem_limit_bytes=VMEM_LIMIT),
        )(*(pltpu.with_memory_space_constraint(a, pltpu.HBM)
            for a in (traces, templates, channel_mask)))

    placed = (
        P(("chan", "sub"), ("groups", "tm")),
        P("tm", ("chan", "sub"), None),
        P("tm", ("chan", "sub")),
    )
    return jax.shard_map(
        on_device,
        mesh=mesh,
        in_specs=placed,
        out_specs=P(("chan", "sub"), ("groups", "tm")),
        check_vma=False,
    )
```

```python
import functools

import jax
import jax.numpy as jnp
from jax import lax
from jax.experimental import pallas as pl
from jax.experimental.pallas import tpu as pltpu
from jax.sharding import PartitionSpec as P

EPSILON = 1e-06
MESH = pl.DeviceIdType.MESH
LANES = 128
FINE = 32
NT = (((1,), (1,)), ((), ()))
PIECES = 2
VMEM_LIMIT = 32 * 1024 * 1024


def is_outer(z, half):
    return (z % 2 == 0) == (z < half)


def kernel(sizes, x_hbm, w_hbm, m_hbm, o_ref, x_ref, w_ref, m_ref, xt, af, ab, acc, rb, rx, mk, pb, tp, fp, eh, es, ew,
           recv_sem, right_sem, left_sem, out_sem, in_sem, extra_sem,
           extrain_sem, wave_sem,
           wavein_sem, pass_sem, mask_sem, maskin_sem,
           pow_sem, powin_sem, te_sem, tein_sem, fac_sem, facin_sem, head_sem, load_sem):
    group_n, tm, chan_n, sub_n = sizes
    cs_n = chan_n * sub_n
    me = lax.axis_index("tm")
    my_chan = lax.axis_index("chan")
    my_sub = lax.axis_index("sub")
    my_cs = my_chan * sub_n + my_sub
    chans, tile = x_ref.shape
    rows, _, span = w_ref.shape
    blocks = tm // cs_n
    coarse = span // FINE
    total = tm * tile
    n = tile // span
    owner = me // blocks
    first = me * n
    my_group = lax.axis_index("groups")
    depth = FINE * rows
    piece = depth // (group_n * PIECES)
    half = tm // 2
    partner = me + 1 - 2 * lax.rem(me, 2)
    moves = my_sub == 0
    outer = is_outer(me, half)
    gives = jnp.logical_and(outer, moves)
    takes = jnp.logical_and(jnp.logical_not(outer), moves)
    low_end = jnp.where(moves, 1, 0)
    high_end = tm - 1 - low_end
    pair = 2 * span
    pairs = tile // pair
    switch = pairs

    def remote(src, dst, send, recv, to):
        return pltpu.make_async_remote_copy(
            src_ref=src, dst_ref=dst, send_sem=send, recv_sem=recv,
            device_id=to, device_id_type=MESH)

    def peer(d):
        return {"tm": lax.rem(me + d, tm)}

    def cs_place(c):
        return {"chan": c // sub_n, "sub": c % sub_n}

    loads = [pltpu.make_async_copy(src, dst, load_sem.at[i]) for i, (src, dst) in enumerate(
        ((m_hbm, m_ref), (x_hbm, x_ref), (w_hbm, w_ref)))]
    for load in loads:
        load.start()

    barrier = pltpu.get_barrier_semaphore()
    for d in range(1, tm):
        pl.semaphore_signal(barrier, inc=1, device_id=peer(d), device_id_type=MESH)
    for d in range(1, cs_n):
        pl.semaphore_signal(barrier, inc=1, device_id=cs_place(lax.rem(my_cs + d, cs_n)),
                            device_id_type=MESH)

    for d in range(1, group_n):
        pl.semaphore_signal(barrier, inc=1, device_id={"groups": lax.rem(my_group + d, group_n)},
                            device_id_type=MESH)

    loads[0].wait()
    mask = m_ref[...].astype(jnp.float32)
    mk[me] = mask
    loads[1].wait()
    xt[pl.ds(me * tile, tile), :] = jnp.transpose(x_ref[...])
    loads[2].wait()
    for k in range(rows):
        wave = jnp.transpose(w_ref[k].astype(jnp.float32)) * mask[k : k + 1, :]
        tp[my_cs, k : k + 1, 0:chans] = jnp.sum(wave * wave, axis=0, keepdims=True)
        for g in range(coarse):
            af[g, pl.ds(k, FINE, stride=rows), :] = wave[g * FINE : (g + 1) * FINE, :]
    for g in range(coarse):
        ab[0:depth, g * chans : (g + 1) * chans] = af[g].astype(jnp.bfloat16)
    tp[my_cs, :, chans : 2 * chans] = mask

    pl.semaphore_wait(barrier, tm - 1 + cs_n - 1 + group_n - 1)

    def mask_copy(d):
        return remote(mk.at[me], mk.at[me], mask_sem.at[d], maskin_sem.at[me], peer(d))

    for d in range(1, tm):
        mask_copy(d).start()

    def wave_copy(p, to):
        at = (my_group * PIECES + p) * piece
        return remote(ab.at[pl.ds(pl.multiple_of(at, piece), piece), :],
                      ab.at[pl.ds(pl.multiple_of(depth + at, piece), piece), :],
                      wave_sem.at[p], wavein_sem.at[my_group, p], {"tm": to})

    def pass_copy(p, d):
        at = pl.ds(pl.multiple_of(depth + (my_group * PIECES + p) * piece, piece), piece)
        return remote(ab.at[at, :], ab.at[at, :], pass_sem.at[d, p], wavein_sem.at[my_group, p],
                      {"groups": lax.rem(my_group + d, group_n)})

    @pl.when(gives)
    def _():
        for p in range(PIECES):
            wave_copy(p, partner).start()

    def relay(c, to, sem):
        part = pl.ds(pl.multiple_of(c * span, span), span)
        return remote(xt.at[part, :], xt.at[part, :], sem.at[c], recv_sem.at[c], {"tm": to})

    def send_own():
        for k in range(n):
            @pl.when(me < tm - 1)
            def _():
                relay(first + n - 1 - k, me + 1, right_sem).start()

            @pl.when(me > 0)
            def _():
                relay(first + k, me - 1, left_sem).start()

    send_own()

    def te_copy():
        return remote(tp.at[my_cs], tp.at[my_cs], te_sem, tein_sem.at[my_cs], cs_place(owner))

    @pl.when(my_cs != owner)
    def _():
        te_copy().start()

    acc[...] = jnp.zeros_like(acc)

    def spread(p):
        width = p.shape[1]
        pad = jnp.zeros((rows, LANES), jnp.float32)
        out = jnp.concatenate([pad, p[:rows]], 1)
        for b in range(1, FINE):
            one = jnp.concatenate([pad, p[b * rows : (b + 1) * rows]], 1)
            out = out + pltpu.roll(one, width + LANES - b, 1)
        return out

    def add_products(slots, right, start, before):
        for slot in slots:
            out = spread(lax.dot_general(ab[slot * depth : (slot + 1) * depth, :], right, NT,
                                         preferred_element_type=jnp.float32))
            acc[slot, :, pl.ds(before, LANES)] += out[:, :LANES]
            acc[slot, :, pl.ds(start, right.shape[0])] += out[:, LANES:]

    def process(c, width, slots):
        start = pl.multiple_of(c * span, span)
        before = pl.multiple_of(lax.rem(start + total - LANES, total), LANES)
        right = jnp.concatenate(
            [xt[pl.ds(pl.multiple_of(start + FINE * g, FINE), width), :] for g in range(coarse)],
            1)
        add_products(slots, right, start, before)

    def own(slots):
        process(first, tile - span, slots)

    def close(wide, slots):
        xt[total : total + span, :] = xt[0:span, :]
        start = total - wide
        right = jnp.concatenate(
            [xt[pl.ds(start + FINE * g, wide), :] for g in range(coarse)], 1)
        for slot in slots:
            out = spread(lax.dot_general(ab[slot * depth : (slot + 1) * depth, :], right, NT,
                                         preferred_element_type=jnp.float32))
            acc[slot, :, pl.ds(start - LANES, LANES)] += out[:, :LANES]
            for k in range(wide // span):
                at = start + k * span
                low = LANES + k * span
                acc[slot, :, pl.ds(at, span)] += out[:, low : low + span]

    def block_of(slot):
        return partner if slot else me

    def holder(slot):
        return block_of(slot) // blocks

    def columns(o):
        return pl.ds(pl.multiple_of(o * pair, pair), pair)

    def out_copy(o, slot):
        q = block_of(slot) % blocks
        return remote(acc.at[slot, :, columns(o)], rb.at[q, my_cs, :, columns(lax.rem(o, pairs))],
                      out_sem.at[slot, o], in_sem.at[q, my_cs, lax.rem(o, pairs)],
                      {"tm": o // pairs, **cs_place(holder(slot))})

    def extra_copy(o, slot):
        q = block_of(slot) % blocks
        return remote(acc.at[slot, :, columns(o)], rx.at[q, my_chan],
                      extra_sem, extrain_sem.at[q, my_chan],
                      {"tm": o // pairs, **cs_place(holder(slot))})

    def is_local(o, slot):
        return jnp.logical_and(o // pairs == me, my_cs == holder(slot))

    def hand(o, slot):
        @pl.when(is_local(o, slot))
        def _():
            rb[block_of(slot) % blocks, my_cs, :, columns(lax.rem(o, pairs))] = (
                acc[slot, :, columns(o)])

        @pl.when(jnp.logical_not(is_local(o, slot)))
        def _():
            out_copy(o, slot).start()

    def hand_extra(o, slot):
        @pl.when(is_local(o, slot))
        def _():
            rx[block_of(slot) % blocks, my_chan] = acc[slot, :, columns(o)]

        @pl.when(jnp.logical_not(is_local(o, slot)))
        def _():
            extra_copy(o, slot).start()

    home = me * pairs
    low = me - lax.rem(me, 2)
    pair_last = (low + 2) * pairs - 1
    before_pair = lax.rem(low * pairs + tm * pairs - 1, tm * pairs)

    def hand_first(o):
        hand(o, 0)

    def hand_second(o):
        @pl.when(o == pair_last)
        def _():
            hand_extra(o, 1)

        @pl.when(o != pair_last)
        def _():
            hand(o, 1)

    def pow_copy(d):
        to = lax.rem(my_cs + d, cs_n)
        return remote(es.at[to], pb.at[my_cs], pow_sem.at[d], powin_sem.at[my_cs], cs_place(to))

    def power():
        for d in range(1, tm):
            who = lax.rem(me + d, tm)
            remote(mk.at[who], mk.at[who], mask_sem.at[0], maskin_sem.at[who],
                   {"tm": who}).wait_recv()
        masks = jnp.concatenate([mk[i] for i in range(tm)], 0).astype(jnp.bfloat16)
        x32 = xt[pl.ds(me * tile, tile), :].astype(jnp.float32)
        square = x32 * x32
        high = square.astype(jnp.bfloat16)
        low = (square - high.astype(jnp.float32)).astype(jnp.bfloat16)
        p = lax.dot_general(jnp.concatenate([masks, masks], 1), jnp.concatenate([high, low], 1),
                            NT, preferred_element_type=jnp.float32)
        for c in range(cs_n):
            es[c] = p[c * blocks * rows : (c + 1) * blocks * rows, :]
        pb[my_cs] = es[my_cs]
        for d in range(1, cs_n):
            pow_copy(d).start()

    def fac_copy(d):
        return remote(fp.at[me % blocks], fp.at[me % blocks], fac_sem.at[d],
                      facin_sem.at[me % blocks], peer(d))

    def template_sums():
        @pl.when(my_cs == owner)
        def _():
            for d in range(1, cs_n):
                who = lax.rem(my_cs + d, cs_n)
                remote(tp.at[who], tp.at[who], te_sem, tein_sem.at[who], cs_place(who)).wait_recv()
            t = tp[0]
            for c in range(1, cs_n):
                t = t + tp[c]
            te = jnp.sum(t[:, :chans], axis=1, keepdims=True)
            active = jnp.sum(t[:, chans:], axis=1, keepdims=True)
            lane = lax.broadcasted_iota(jnp.int32, (rows, LANES), 1)
            fp[me % blocks] = jnp.where(lane < LANES // 2, te, active)
            for d in range(1, tm):
                fac_copy(d).start()

    def head_copy():
        return remote(eh.at[0], eh.at[1], head_sem.at[0], head_sem.at[1],
                      {"tm": lax.rem(me + tm - 1, tm)})

    def windows():
        for d in range(1, cs_n):
            who = lax.rem(my_cs + d, cs_n)
            remote(es.at[who], pb.at[who], pow_sem.at[0], powin_sem.at[who],
                   cs_place(who)).wait_recv()
        p = pb[0]
        for c in range(1, cs_n):
            p = p + pb[c]
        p = jnp.concatenate([jnp.zeros((blocks * rows, span), jnp.float32), p], 1)
        by = 1
        while by < span:
            p = p + pltpu.roll(p, tile + span - by, 1)
            by *= 2
        eh[0] = p[:, :span]
        head_copy().start()
        ew[0] = p[:, span:]

    def norms():
        head_copy().wait_recv()
        for q in range(blocks):
            j = my_cs * blocks + q

            @pl.when(me != j)
            def _():
                remote(fp.at[q], fp.at[q], fac_sem.at[0], facin_sem.at[q], {"tm": j}).wait_recv()

            at = slice(q * rows, (q + 1) * rows)
            factor = jnp.sqrt(span * fp[q, :, LANES - 1 : LANES])
            energy = jnp.concatenate(
                [ew[0, at, : tile - span], ew[0, at, tile - span :] + eh[1, at, :]], 1)
            ew[1, at, :] = factor / jnp.sqrt(energy * fp[q, :, 0:1] + EPSILON)

    left_n = pairs * jnp.where(jnp.logical_and(moves, me == tm - 1), 1, me)
    right_n = pairs * jnp.where(jnp.logical_and(moves, me == 0), 1, tm - 1 - me)
    short = jnp.minimum(left_n, right_n)
    left_short = left_n < right_n
    steps = pairs * (tm - 1)

    def arrival(u):
        v = u - switch
        paired = u < 2 * short
        on_short = jnp.where(takes, jnp.logical_and(v >= 0, v < short),
                             jnp.logical_and(paired, lax.rem(u, 2) == 0))
        k = jnp.where(takes, jnp.where(v < 0, u, jnp.where(on_short, v, u - short)),
                      jnp.where(paired, u // 2, u - short))
        from_left = on_short == left_short
        return from_left, jnp.where(from_left, home - 1 - k, home + pairs + k)

    def made(u):
        from_left, o = arrival(u)
        return jnp.where(from_left, 2 * o, 2 * o - 1)

    def ended(u):
        from_left, o = arrival(u)
        return jnp.where(from_left, o, o - 1)

    own((0,))
    for o in range(pairs - 1):
        @pl.when(jnp.logical_not(jnp.logical_and(gives, lax.rem(me, 2) == 1)))
        def _():
            hand(home + o, 0)

    power()

    def step(u, final):
        live = u < left_n + right_n
        from_left, o = arrival(u)
        per = PIECES // switch

        @pl.when(jnp.logical_and(takes, u < switch))
        def _():
            for i in range(per):
                p = jnp.minimum(u, switch - 1) * per + i
                remote(ab.at[pl.ds(0, piece), :], ab.at[pl.ds(0, piece), :], wave_sem.at[0],
                       wavein_sem.at[my_group, p], {"tm": partner}).wait_recv()
                for d in range(1, group_n):
                    pass_copy(p, d).start()

        @pl.when(jnp.logical_and(live, from_left))
        def _():
            for i in (1, 0):
                relay(2 * o + i, me, right_sem).wait_recv()

                @pl.when(me < high_end)
                def _():
                    relay(2 * o + i, me + 1, right_sem).start()

        @pl.when(jnp.logical_and(live, jnp.logical_not(from_left)))
        def _():
            for i in (0, 1):
                relay(2 * o + i, me, left_sem).wait_recv()

                @pl.when(me > low_end)
                def _():
                    relay(2 * o + i, me - 1, left_sem).start()

        @pl.when(jnp.logical_and(takes, u == switch + 1))
        def _():
            for d in range(1, group_n):
                who = lax.rem(my_group + d, group_n)
                for p in range(PIECES):
                    remote(ab.at[pl.ds(0, piece), :], ab.at[pl.ds(0, piece), :], wave_sem.at[0],
                           wavein_sem.at[who, p], {"groups": who}).wait_recv()

        both = jnp.logical_and(takes, u >= switch + pairs)
        if final:
            for slots, mine in (((0, 1), takes), ((0,), jnp.logical_not(moves))):
                @pl.when(jnp.logical_and(mine, from_left))
                def _():
                    process(made(u), pair, slots)
                    for slot in slots:
                        (hand_second if slot else hand_first)(ended(u))
                    close(span, slots)

                @pl.when(jnp.logical_and(mine, jnp.logical_not(from_left)))
                def _():
                    close(pair + span, slots)
                    for slot in slots:
                        (hand_second if slot else hand_first)(ended(u))

                @pl.when(mine)
                def _():
                    for slot in slots:
                        (hand_second if slot else hand_first)(tm * pairs - 1)

            @pl.when(gives)
            def _():
                for o in range(2 * pairs):
                    at = low * pairs + o

                    @pl.when(jnp.logical_or(lax.rem(me, 2) == 1, o >= pairs - 1))
                    def _():
                        hand(at, 0)
                hand_extra(before_pair, 0)

            return

        @pl.when(jnp.logical_or(
            jnp.logical_and(gives, jnp.logical_and(live, o // pairs == partner)),
            jnp.logical_and(jnp.logical_not(gives), jnp.logical_not(jnp.logical_or(
                both, jnp.logical_and(takes, u == switch + 1))))))
        def _():
            process(made(u), pair, (0,))

        @pl.when(jnp.logical_and(takes, u == switch + 1))
        def _():
            process(made(u), pair, (0,))
            process(jnp.minimum(made(0), made(switch - 1)), switch * pair, (1,))
            for v in range(switch):
                hand_second(ended(v))

        @pl.when(both)
        def _():
            process(made(u), pair, (0, 1))
            hand_second(ended(u))

        hold = jnp.where(takes, switch, steps - 2)

        @pl.when(jnp.logical_and(jnp.logical_not(gives), u >= hold))
        def _():
            def hand_on(v, carry):
                hand(ended(v), 0)
                return carry

            lax.fori_loop(jnp.where(u == hold, 0, u), u + 1, hand_on, 0)

        @pl.when(u == jnp.where(moves, 0, 3))
        def _():
            template_sums()

        @pl.when(u == jnp.where(moves, 0, 2))
        def _():
            windows()

    def loop(u, carry):
        step(u, False)
        return carry

    lax.fori_loop(0, steps - 1, loop, 0)
    step(steps - 1, True)

    norms()

    def finish(c, carry):
        @pl.when(jnp.logical_or(jnp.logical_and(me < high_end, c // n < me),
                                jnp.logical_and(me < tm - 1, c // n == me)))
        def _():
            relay(c, me, right_sem).wait_send()

        @pl.when(jnp.logical_or(jnp.logical_and(me > low_end, c // n > me),
                                jnp.logical_and(me > 0, c // n == me)))
        def _():
            relay(c, me, left_sem).wait_send()

        return carry

    lax.fori_loop(0, n * tm, finish, 0)

    def finish_out(o, carry):
        in_pair = o // (2 * pairs) == me // 2

        @pl.when(jnp.logical_and(jnp.logical_or(jnp.logical_not(gives), in_pair),
                                 jnp.logical_not(is_local(o, 0))))
        def _():
            out_copy(o, 0).wait_send()

        @pl.when(jnp.logical_and(jnp.logical_and(takes, jnp.logical_not(in_pair)),
                                 jnp.logical_not(is_local(o, 1))))
        def _():
            out_copy(o, 1).wait_send()

        return carry

    lax.fori_loop(0, pairs * tm, finish_out, 0)

    @pl.when(jnp.logical_and(gives, jnp.logical_not(is_local(before_pair, 0))))
    def _():
        extra_copy(before_pair, 0).wait_send()

    @pl.when(jnp.logical_and(takes, jnp.logical_not(is_local(pair_last, 1))))
    def _():
        extra_copy(pair_last, 1).wait_send()
    for p in range(PIECES):
        @pl.when(gives)
        def _():
            wave_copy(p, partner).wait_send()

        @pl.when(takes)
        def _():
            for d in range(1, group_n):
                pass_copy(p, d).wait_send()

    for d in range(1, tm):
        mask_copy(d).wait_send()
    for d in range(1, cs_n):
        pow_copy(d).wait_send()

    @pl.when(my_cs != owner)
    def _():
        te_copy().wait_send()

    @pl.when(my_cs == owner)
    def _():
        for d in range(1, tm):
            fac_copy(d).wait_send()

    head_copy().wait_send()

    for q in range(blocks):
        b = my_cs * blocks + q
        b_outer = is_outer(b, half)
        for slot in range(cs_n):
            moved = slot % sub_n == 0
            inner = b + 1 - 2 * lax.rem(b, 2)
            apart = jnp.logical_and(b_outer, me // 2 != b // 2)
            source = jnp.where(apart, inner, b) if moved else b

            @pl.when(jnp.logical_not(jnp.logical_and(my_cs == slot, source == me)))
            def _():
                for k in range(pairs):
                    remote(acc.at[0, :, pl.ds(0, pair)],
                           rb.at[q, slot, :, pl.ds(k * pair, pair)], out_sem.at[0, 0],
                           in_sem.at[q, slot, k], {"tm": lax.rem(me + 1, tm)}).wait_recv()

        at = slice(q * rows, (q + 1) * rows)
        result = rb[q, 0]
        for c in range(1, cs_n):
            result = result + rb[q, c]
        b_low = b - lax.rem(b, 2)
        tail = jnp.logical_and(b_outer, me == b_low + 1)
        ahead = jnp.logical_and(b_outer, me == lax.rem(b_low + tm - 1, tm))
        for c in range(chan_n):
            source = jnp.where(me == b_low + 1, inner, b)
            near_me = jnp.logical_and(jnp.logical_and(my_sub == 0, my_chan == c), source == me)

            @pl.when(jnp.logical_and(jnp.logical_or(tail, ahead), jnp.logical_not(near_me)))
            def _():
                remote(acc.at[0, :, pl.ds(0, pair)], rx.at[q, c], out_sem.at[0, 0],
                       extrain_sem.at[q, c], {"tm": lax.rem(me + 1, tm)}).wait_recv()

        o_ref[at, :] = result * ew[1, at, :]

        @pl.when(jnp.logical_or(tail, ahead))
        def _():
            more = rx[q, 0]
            for c in range(1, chan_n):
                more = more + rx[q, c]
            whole = slice(tile - pair, tile)
            o_ref[at, whole] = (result[:, whole] + more) * ew[1, at, whole]


def solution(mesh):
    group_n, tm, chan_n, sub_n = (mesh.shape[a] for a in ("groups", "tm", "chan", "sub"))
    cs_n = chan_n * sub_n
    blocks = tm // cs_n

    def on_device(traces, templates, channel_mask):
        chans, tile = traces.shape
        rows, _, span = templates.shape
        coarse = span // FINE
        total = tm * tile
        n = tile // span
        out_rows = blocks * rows
        vmem = pl.BlockSpec(memory_space=pltpu.VMEM)
        f32, bf16 = jnp.float32, jnp.bfloat16
        dma = pltpu.SemaphoreType.DMA
        return pl.pallas_call(
            functools.partial(kernel, (group_n, tm, chan_n, sub_n)),
            out_shape=jax.ShapeDtypeStruct((out_rows, tile), f32),
            in_specs=[pl.BlockSpec(memory_space=pltpu.HBM)] * 3,
            out_specs=vmem,
            scratch_shapes=[
                pltpu.VMEM((chans, tile), bf16),
                pltpu.VMEM((rows, chans, span), bf16),
                pltpu.VMEM((rows, chans), jnp.int32),
                pltpu.VMEM((total + span, chans), bf16),
                pltpu.VMEM((coarse, FINE * rows, chans), f32),
                pltpu.VMEM((2 * FINE * rows, coarse * chans), bf16),
                pltpu.VMEM((2, rows, total), f32),
                pltpu.VMEM((blocks, cs_n, rows, tile), f32),
                pltpu.VMEM((blocks, chan_n, rows, 2 * span), f32),
                pltpu.VMEM((tm, rows, chans), f32),
                pltpu.VMEM((cs_n, out_rows, tile), f32),
                pltpu.VMEM((cs_n, rows, 2 * chans), f32),
                pltpu.VMEM((blocks, rows, LANES), f32),
                pltpu.VMEM((2, out_rows, span), f32),
                pltpu.VMEM((cs_n, out_rows, tile), f32),
                pltpu.VMEM((2, out_rows, tile), f32),
                dma((n * tm,)), dma((n * tm,)), dma((n * tm,)),
                dma((2, n * tm // 2)), dma((blocks, cs_n, n // 2)),
                dma(()), dma((blocks, chan_n)),
                dma((PIECES,)), dma((group_n, PIECES)), dma((group_n, PIECES)),
                dma((tm,)), dma((tm,)),
                dma((cs_n,)), dma((cs_n,)),
                dma(()), dma((cs_n,)),
                dma((tm,)), dma((blocks,)),
                dma((2,)),
                dma((3,)),
            ],
            compiler_params=pltpu.CompilerParams(collective_id=0, has_side_effects=True, vmem_limit_bytes=VMEM_LIMIT),
        )(*(pltpu.with_memory_space_constraint(a, pltpu.HBM)
            for a in (traces, templates, channel_mask)))

    placed = (
        P(("chan", "sub"), ("groups", "tm")),
        P("tm", ("chan", "sub"), None),
        P("tm", ("chan", "sub")),
    )
    return jax.shard_map(
        on_device,
        mesh=mesh,
        in_specs=placed,
        out_specs=P(("chan", "sub"), ("groups", "tm")),
        check_vma=False,
    )
```

```python
import functools

import jax
import jax.numpy as jnp
from jax import lax
from jax.experimental import pallas as pl
from jax.experimental.pallas import tpu as pltpu
from jax.sharding import PartitionSpec as P

EPSILON = 1e-06
MESH = pl.DeviceIdType.MESH
LANES = 128
FINE = 32
NT = (((1,), (1,)), ((), ()))
PIECES = 2
VMEM_LIMIT = 32 * 1024 * 1024


def is_outer(z, half):
    return (z % 2 == 0) == (z < half)


def kernel(sizes, x_hbm, w_hbm, m_hbm, o_ref, x_ref, w_ref, m_ref, xt, af, ab, acc, rb, rx, mk, pb, tp, fp, eh, es, ew,
           recv_sem, right_sem, left_sem, out_sem, in_sem, extra_sem,
           extrain_sem, wave_sem,
           wavein_sem, pass_sem, mask_sem, maskin_sem,
           pow_sem, powin_sem, te_sem, tein_sem, fac_sem, facin_sem, head_sem, load_sem):
    group_n, tm, chan_n, sub_n = sizes
    cs_n = chan_n * sub_n
    me = lax.axis_index("tm")
    my_chan = lax.axis_index("chan")
    my_sub = lax.axis_index("sub")
    my_cs = my_chan * sub_n + my_sub
    chans, tile = x_ref.shape
    rows, _, span = w_ref.shape
    blocks = tm // cs_n
    coarse = span // FINE
    total = tm * tile
    n = tile // span
    owner = me // blocks
    first = me * n
    my_group = lax.axis_index("groups")
    depth = FINE * rows
    piece = depth // (group_n * PIECES)
    half = tm // 2
    partner = me + 1 - 2 * lax.rem(me, 2)
    moves = my_sub == 0
    outer = is_outer(me, half)
    gives = jnp.logical_and(outer, moves)
    takes = jnp.logical_and(jnp.logical_not(outer), moves)
    low_end = jnp.where(moves, 1, 0)
    high_end = tm - 1 - low_end
    pair = 2 * span
    pairs = tile // pair
    switch = pairs

    def remote(src, dst, send, recv, to):
        return pltpu.make_async_remote_copy(
            src_ref=src, dst_ref=dst, send_sem=send, recv_sem=recv,
            device_id=to, device_id_type=MESH)

    def peer(d):
        return {"tm": lax.rem(me + d, tm)}

    def cs_place(c):
        return {"chan": c // sub_n, "sub": c % sub_n}

    loads = [pltpu.make_async_copy(src, dst, load_sem.at[i]) for i, (src, dst) in enumerate(
        ((m_hbm, m_ref), (x_hbm, x_ref), (w_hbm, w_ref)))]
    for load in loads:
        load.start()

    barrier = pltpu.get_barrier_semaphore()
    for d in range(1, tm):
        pl.semaphore_signal(barrier, inc=1, device_id=peer(d), device_id_type=MESH)
    for d in range(1, cs_n):
        pl.semaphore_signal(barrier, inc=1, device_id=cs_place(lax.rem(my_cs + d, cs_n)),
                            device_id_type=MESH)

    for d in range(1, group_n):
        pl.semaphore_signal(barrier, inc=1, device_id={"groups": lax.rem(my_group + d, group_n)},
                            device_id_type=MESH)

    loads[0].wait()
    mask = m_ref[...].astype(jnp.float32)
    mk[me] = mask
    loads[1].wait()
    xt[pl.ds(me * tile, tile), :] = jnp.transpose(x_ref[...])
    loads[2].wait()
    for k in range(rows):
        wave = jnp.transpose(w_ref[k].astype(jnp.float32)) * mask[k : k + 1, :]
        tp[my_cs, k : k + 1, 0:chans] = jnp.sum(wave * wave, axis=0, keepdims=True)
        for g in range(coarse):
            af[g, pl.ds(k, FINE, stride=rows), :] = wave[g * FINE : (g + 1) * FINE, :]
    for g in range(coarse):
        ab[0:depth, g * chans : (g + 1) * chans] = af[g].astype(jnp.bfloat16)
    tp[my_cs, :, chans : 2 * chans] = mask

    pl.semaphore_wait(barrier, tm - 1 + cs_n - 1 + group_n - 1)

    def mask_copy(d):
        return remote(mk.at[me], mk.at[me], mask_sem.at[d], maskin_sem.at[me], peer(d))

    for d in range(1, tm):
        mask_copy(d).start()

    def wave_copy(p, to):
        at = (my_group * PIECES + p) * piece
        return remote(ab.at[pl.ds(pl.multiple_of(at, piece), piece), :],
                      ab.at[pl.ds(pl.multiple_of(depth + at, piece), piece), :],
                      wave_sem.at[p], wavein_sem.at[my_group, p], {"tm": to})

    def pass_copy(p, d):
        at = pl.ds(pl.multiple_of(depth + (my_group * PIECES + p) * piece, piece), piece)
        return remote(ab.at[at, :], ab.at[at, :], pass_sem.at[d, p], wavein_sem.at[my_group, p],
                      {"groups": lax.rem(my_group + d, group_n)})

    @pl.when(gives)
    def _():
        for p in range(PIECES):
            wave_copy(p, partner).start()

    def relay(c, to, sem):
        part = pl.ds(pl.multiple_of(c * span, span), span)
        return remote(xt.at[part, :], xt.at[part, :], sem.at[c], recv_sem.at[c], {"tm": to})

    def send_own():
        for k in range(n):
            @pl.when(me < tm - 1)
            def _():
                relay(first + n - 1 - k, me + 1, right_sem).start()

            @pl.when(me > 0)
            def _():
                relay(first + k, me - 1, left_sem).start()

    send_own()

    def te_copy():
        return remote(tp.at[my_cs], tp.at[my_cs], te_sem, tein_sem.at[my_cs], cs_place(owner))

    @pl.when(my_cs != owner)
    def _():
        te_copy().start()

    acc[...] = jnp.zeros_like(acc)

    def spread(p):
        width = p.shape[1]
        pad = jnp.zeros((rows, LANES), jnp.float32)
        out = jnp.concatenate([pad, p[:rows]], 1)
        for b in range(1, FINE):
            one = jnp.concatenate([pad, p[b * rows : (b + 1) * rows]], 1)
            out = out + pltpu.roll(one, width + LANES - b, 1)
        return out

    def add_products(slots, right, start, before):
        for slot in slots:
            out = spread(lax.dot_general(ab[slot * depth : (slot + 1) * depth, :], right, NT,
                                         preferred_element_type=jnp.float32))
            acc[slot, :, pl.ds(before, LANES)] += out[:, :LANES]
            acc[slot, :, pl.ds(start, right.shape[0])] += out[:, LANES:]

    def process(c, width, slots):
        start = pl.multiple_of(c * span, span)
        before = pl.multiple_of(lax.rem(start + total - LANES, total), LANES)
        right = jnp.concatenate(
            [xt[pl.ds(pl.multiple_of(start + FINE * g, FINE), width), :] for g in range(coarse)],
            1)
        add_products(slots, right, start, before)

    def own(slots):
        process(first, tile - span, slots)

    def close(wide, slots):
        xt[total : total + span, :] = xt[0:span, :]
        start = total - wide
        right = jnp.concatenate(
            [xt[pl.ds(start + FINE * g, wide), :] for g in range(coarse)], 1)
        for slot in slots:
            out = spread(lax.dot_general(ab[slot * depth : (slot + 1) * depth, :], right, NT,
                                         preferred_element_type=jnp.float32))
            acc[slot, :, pl.ds(start - LANES, LANES)] += out[:, :LANES]
            for k in range(wide // span):
                at = start + k * span
                low = LANES + k * span
                acc[slot, :, pl.ds(at, span)] += out[:, low : low + span]

    def block_of(slot):
        return partner if slot else me

    def holder(slot):
        return block_of(slot) // blocks

    def columns(o):
        return pl.ds(pl.multiple_of(o * pair, pair), pair)

    def out_copy(o, slot):
        q = block_of(slot) % blocks
        return remote(acc.at[slot, :, columns(o)], rb.at[q, my_cs, :, columns(lax.rem(o, pairs))],
                      out_sem.at[slot, o], in_sem.at[q, my_cs, lax.rem(o, pairs)],
                      {"tm": o // pairs, **cs_place(holder(slot))})

    def extra_copy(o, slot):
        q = block_of(slot) % blocks
        return remote(acc.at[slot, :, columns(o)], rx.at[q, my_chan],
                      extra_sem, extrain_sem.at[q, my_chan],
                      {"tm": o // pairs, **cs_place(holder(slot))})

    def is_local(o, slot):
        return jnp.logical_and(o // pairs == me, my_cs == holder(slot))

    def hand(o, slot):
        @pl.when(is_local(o, slot))
        def _():
            rb[block_of(slot) % blocks, my_cs, :, columns(lax.rem(o, pairs))] = (
                acc[slot, :, columns(o)])

        @pl.when(jnp.logical_not(is_local(o, slot)))
        def _():
            out_copy(o, slot).start()

    def hand_extra(o, slot):
        @pl.when(is_local(o, slot))
        def _():
            rx[block_of(slot) % blocks, my_chan] = acc[slot, :, columns(o)]

        @pl.when(jnp.logical_not(is_local(o, slot)))
        def _():
            extra_copy(o, slot).start()

    home = me * pairs
    low = me - lax.rem(me, 2)
    pair_last = (low + 2) * pairs - 1
    before_pair = lax.rem(low * pairs + tm * pairs - 1, tm * pairs)

    def hand_first(o):
        hand(o, 0)

    def hand_second(o):
        @pl.when(o == pair_last)
        def _():
            hand_extra(o, 1)

        @pl.when(o != pair_last)
        def _():
            hand(o, 1)

    def pow_copy(d):
        to = lax.rem(my_cs + d, cs_n)
        return remote(es.at[to], pb.at[my_cs], pow_sem.at[d], powin_sem.at[my_cs], cs_place(to))

    def power():
        for d in range(1, tm):
            who = lax.rem(me + d, tm)
            remote(mk.at[who], mk.at[who], mask_sem.at[0], maskin_sem.at[who],
                   {"tm": who}).wait_recv()
        masks = jnp.concatenate([mk[i] for i in range(tm)], 0).astype(jnp.bfloat16)
        x32 = xt[pl.ds(me * tile, tile), :].astype(jnp.float32)
        square = x32 * x32
        high = square.astype(jnp.bfloat16)
        low = (square - high.astype(jnp.float32)).astype(jnp.bfloat16)
        p = lax.dot_general(jnp.concatenate([masks, masks], 1), jnp.concatenate([high, low], 1),
                            NT, preferred_element_type=jnp.float32)
        for c in range(cs_n):
            es[c] = p[c * blocks * rows : (c + 1) * blocks * rows, :]
        pb[my_cs] = es[my_cs]
        for d in range(1, cs_n):
            pow_copy(d).start()

    def fac_copy(d):
        return remote(fp.at[me % blocks], fp.at[me % blocks], fac_sem.at[d],
                      facin_sem.at[me % blocks], peer(d))

    def template_sums():
        @pl.when(my_cs == owner)
        def _():
            for d in range(1, cs_n):
                who = lax.rem(my_cs + d, cs_n)
                remote(tp.at[who], tp.at[who], te_sem, tein_sem.at[who], cs_place(who)).wait_recv()
            t = tp[0]
            for c in range(1, cs_n):
                t = t + tp[c]
            te = jnp.sum(t[:, :chans], axis=1, keepdims=True)
            active = jnp.sum(t[:, chans:], axis=1, keepdims=True)
            lane = lax.broadcasted_iota(jnp.int32, (rows, LANES), 1)
            fp[me % blocks] = jnp.where(lane < LANES // 2, te, active)
            for d in range(1, tm):
                fac_copy(d).start()

    def head_copy():
        return remote(eh.at[0], eh.at[1], head_sem.at[0], head_sem.at[1],
                      {"tm": lax.rem(me + tm - 1, tm)})

    def windows():
        for d in range(1, cs_n):
            who = lax.rem(my_cs + d, cs_n)
            remote(es.at[who], pb.at[who], pow_sem.at[0], powin_sem.at[who],
                   cs_place(who)).wait_recv()
        p = pb[0]
        for c in range(1, cs_n):
            p = p + pb[c]
        p = jnp.concatenate([jnp.zeros((blocks * rows, span), jnp.float32), p], 1)
        by = 1
        while by < span:
            p = p + pltpu.roll(p, tile + span - by, 1)
            by *= 2
        eh[0] = p[:, :span]
        head_copy().start()
        ew[0] = p[:, span:]

    def norms():
        head_copy().wait_recv()
        for q in range(blocks):
            j = my_cs * blocks + q

            @pl.when(me != j)
            def _():
                remote(fp.at[q], fp.at[q], fac_sem.at[0], facin_sem.at[q], {"tm": j}).wait_recv()

            at = slice(q * rows, (q + 1) * rows)
            factor = jnp.sqrt(span * fp[q, :, LANES - 1 : LANES])
            energy = jnp.concatenate(
                [ew[0, at, : tile - span], ew[0, at, tile - span :] + eh[1, at, :]], 1)
            ew[1, at, :] = factor / jnp.sqrt(energy * fp[q, :, 0:1] + EPSILON)

    left_n = pairs * jnp.where(jnp.logical_and(moves, me == tm - 1), 1, me)
    right_n = pairs * jnp.where(jnp.logical_and(moves, me == 0), 1, tm - 1 - me)
    short = jnp.minimum(left_n, right_n)
    left_short = left_n < right_n
    steps = pairs * (tm - 1)

    def arrival(u):
        v = u - switch
        paired = u < 2 * short
        on_short = jnp.where(takes, jnp.logical_and(v >= 0, v < short),
                             jnp.logical_and(paired, lax.rem(u, 2) == 0))
        k = jnp.where(takes, jnp.where(v < 0, u, jnp.where(on_short, v, u - short)),
                      jnp.where(paired, u // 2, u - short))
        from_left = on_short == left_short
        return from_left, jnp.where(from_left, home - 1 - k, home + pairs + k)

    def made(u):
        from_left, o = arrival(u)
        return jnp.where(from_left, 2 * o, 2 * o - 1)

    def ended(u):
        from_left, o = arrival(u)
        return jnp.where(from_left, o, o - 1)

    own((0,))
    for o in range(pairs - 1):
        @pl.when(jnp.logical_not(jnp.logical_and(gives, lax.rem(me, 2) == 1)))
        def _():
            hand(home + o, 0)

    power()

    def step(u, final):
        live = u < left_n + right_n
        from_left, o = arrival(u)
        per = PIECES // switch

        @pl.when(jnp.logical_and(takes, u < switch))
        def _():
            for i in range(per):
                p = jnp.minimum(u, switch - 1) * per + i
                remote(ab.at[pl.ds(0, piece), :], ab.at[pl.ds(0, piece), :], wave_sem.at[0],
                       wavein_sem.at[my_group, p], {"tm": partner}).wait_recv()
                for d in range(1, group_n):
                    pass_copy(p, d).start()

        @pl.when(jnp.logical_and(live, from_left))
        def _():
            for i in (1, 0):
                relay(2 * o + i, me, right_sem).wait_recv()

                @pl.when(me < high_end)
                def _():
                    relay(2 * o + i, me + 1, right_sem).start()

        @pl.when(jnp.logical_and(live, jnp.logical_not(from_left)))
        def _():
            for i in (0, 1):
                relay(2 * o + i, me, left_sem).wait_recv()

                @pl.when(me > low_end)
                def _():
                    relay(2 * o + i, me - 1, left_sem).start()

        @pl.when(jnp.logical_and(takes, u == switch + 1))
        def _():
            for d in range(1, group_n):
                who = lax.rem(my_group + d, group_n)
                for p in range(PIECES):
                    remote(ab.at[pl.ds(0, piece), :], ab.at[pl.ds(0, piece), :], wave_sem.at[0],
                           wavein_sem.at[who, p], {"groups": who}).wait_recv()

        both = jnp.logical_and(takes, u >= switch + pairs)
        if final:
            for slots, mine in (((0, 1), takes), ((0,), jnp.logical_not(moves))):
                @pl.when(jnp.logical_and(mine, from_left))
                def _():
                    process(made(u), pair, slots)
                    for slot in slots:
                        (hand_second if slot else hand_first)(ended(u))
                    close(span, slots)

                @pl.when(jnp.logical_and(mine, jnp.logical_not(from_left)))
                def _():
                    close(pair + span, slots)
                    for slot in slots:
                        (hand_second if slot else hand_first)(ended(u))

                @pl.when(mine)
                def _():
                    for slot in slots:
                        (hand_second if slot else hand_first)(tm * pairs - 1)

            @pl.when(gives)
            def _():
                for o in range(2 * pairs):
                    at = low * pairs + o

                    @pl.when(jnp.logical_or(lax.rem(me, 2) == 1, o >= pairs - 1))
                    def _():
                        hand(at, 0)
                hand_extra(before_pair, 0)

            return

        @pl.when(jnp.logical_or(
            jnp.logical_and(gives, jnp.logical_and(live, o // pairs == partner)),
            jnp.logical_and(jnp.logical_not(gives), jnp.logical_not(jnp.logical_or(
                both, jnp.logical_and(takes, u == switch + 1))))))
        def _():
            process(made(u), pair, (0,))

        @pl.when(jnp.logical_and(takes, u == switch + 1))
        def _():
            process(made(u), pair, (0,))
            process(jnp.minimum(made(0), made(switch - 1)), switch * pair, (1,))
            for v in range(switch):
                hand_second(ended(v))

        @pl.when(both)
        def _():
            process(made(u), pair, (0, 1))
            hand_second(ended(u))

        edge = jnp.logical_and(outer, jnp.logical_not(moves))
        hold = jnp.where(takes, switch, jnp.where(edge, 0, steps - 2))

        @pl.when(jnp.logical_and(jnp.logical_not(gives), u >= hold))
        def _():
            def hand_on(v, carry):
                hand(ended(v), 0)
                return carry

            lax.fori_loop(jnp.where(u == hold, 0, u), u + 1, hand_on, 0)

        @pl.when(u == jnp.where(moves, 0, 3))
        def _():
            template_sums()

        @pl.when(u == jnp.where(moves, 0, 2))
        def _():
            windows()

    def loop(u, carry):
        step(u, False)
        return carry

    lax.fori_loop(0, steps - 1, loop, 0)
    step(steps - 1, True)

    norms()

    def finish(c, carry):
        @pl.when(jnp.logical_or(jnp.logical_and(me < high_end, c // n < me),
                                jnp.logical_and(me < tm - 1, c // n == me)))
        def _():
            relay(c, me, right_sem).wait_send()

        @pl.when(jnp.logical_or(jnp.logical_and(me > low_end, c // n > me),
                                jnp.logical_and(me > 0, c // n == me)))
        def _():
            relay(c, me, left_sem).wait_send()

        return carry

    lax.fori_loop(0, n * tm, finish, 0)

    def finish_out(o, carry):
        in_pair = o // (2 * pairs) == me // 2

        @pl.when(jnp.logical_and(jnp.logical_or(jnp.logical_not(gives), in_pair),
                                 jnp.logical_not(is_local(o, 0))))
        def _():
            out_copy(o, 0).wait_send()

        @pl.when(jnp.logical_and(jnp.logical_and(takes, jnp.logical_not(in_pair)),
                                 jnp.logical_not(is_local(o, 1))))
        def _():
            out_copy(o, 1).wait_send()

        return carry

    lax.fori_loop(0, pairs * tm, finish_out, 0)

    @pl.when(jnp.logical_and(gives, jnp.logical_not(is_local(before_pair, 0))))
    def _():
        extra_copy(before_pair, 0).wait_send()

    @pl.when(jnp.logical_and(takes, jnp.logical_not(is_local(pair_last, 1))))
    def _():
        extra_copy(pair_last, 1).wait_send()
    for p in range(PIECES):
        @pl.when(gives)
        def _():
            wave_copy(p, partner).wait_send()

        @pl.when(takes)
        def _():
            for d in range(1, group_n):
                pass_copy(p, d).wait_send()

    for d in range(1, tm):
        mask_copy(d).wait_send()
    for d in range(1, cs_n):
        pow_copy(d).wait_send()

    @pl.when(my_cs != owner)
    def _():
        te_copy().wait_send()

    @pl.when(my_cs == owner)
    def _():
        for d in range(1, tm):
            fac_copy(d).wait_send()

    head_copy().wait_send()

    for q in range(blocks):
        b = my_cs * blocks + q
        b_outer = is_outer(b, half)
        for slot in range(cs_n):
            moved = slot % sub_n == 0
            inner = b + 1 - 2 * lax.rem(b, 2)
            apart = jnp.logical_and(b_outer, me // 2 != b // 2)
            source = jnp.where(apart, inner, b) if moved else b

            @pl.when(jnp.logical_not(jnp.logical_and(my_cs == slot, source == me)))
            def _():
                for k in range(pairs):
                    remote(acc.at[0, :, pl.ds(0, pair)],
                           rb.at[q, slot, :, pl.ds(k * pair, pair)], out_sem.at[0, 0],
                           in_sem.at[q, slot, k], {"tm": lax.rem(me + 1, tm)}).wait_recv()

        at = slice(q * rows, (q + 1) * rows)
        result = rb[q, 0]
        for c in range(1, cs_n):
            result = result + rb[q, c]
        b_low = b - lax.rem(b, 2)
        tail = jnp.logical_and(b_outer, me == b_low + 1)
        ahead = jnp.logical_and(b_outer, me == lax.rem(b_low + tm - 1, tm))
        for c in range(chan_n):
            source = jnp.where(me == b_low + 1, inner, b)
            near_me = jnp.logical_and(jnp.logical_and(my_sub == 0, my_chan == c), source == me)

            @pl.when(jnp.logical_and(jnp.logical_or(tail, ahead), jnp.logical_not(near_me)))
            def _():
                remote(acc.at[0, :, pl.ds(0, pair)], rx.at[q, c], out_sem.at[0, 0],
                       extrain_sem.at[q, c], {"tm": lax.rem(me + 1, tm)}).wait_recv()

        o_ref[at, :] = result * ew[1, at, :]

        @pl.when(jnp.logical_or(tail, ahead))
        def _():
            more = rx[q, 0]
            for c in range(1, chan_n):
                more = more + rx[q, c]
            whole = slice(tile - pair, tile)
            o_ref[at, whole] = (result[:, whole] + more) * ew[1, at, whole]


def solution(mesh):
    group_n, tm, chan_n, sub_n = (mesh.shape[a] for a in ("groups", "tm", "chan", "sub"))
    cs_n = chan_n * sub_n
    blocks = tm // cs_n

    def on_device(traces, templates, channel_mask):
        chans, tile = traces.shape
        rows, _, span = templates.shape
        coarse = span // FINE
        total = tm * tile
        n = tile // span
        out_rows = blocks * rows
        vmem = pl.BlockSpec(memory_space=pltpu.VMEM)
        f32, bf16 = jnp.float32, jnp.bfloat16
        dma = pltpu.SemaphoreType.DMA
        return pl.pallas_call(
            functools.partial(kernel, (group_n, tm, chan_n, sub_n)),
            out_shape=jax.ShapeDtypeStruct((out_rows, tile), f32),
            in_specs=[pl.BlockSpec(memory_space=pltpu.HBM)] * 3,
            out_specs=vmem,
            scratch_shapes=[
                pltpu.VMEM((chans, tile), bf16),
                pltpu.VMEM((rows, chans, span), bf16),
                pltpu.VMEM((rows, chans), jnp.int32),
                pltpu.VMEM((total + span, chans), bf16),
                pltpu.VMEM((coarse, FINE * rows, chans), f32),
                pltpu.VMEM((2 * FINE * rows, coarse * chans), bf16),
                pltpu.VMEM((2, rows, total), f32),
                pltpu.VMEM((blocks, cs_n, rows, tile), f32),
                pltpu.VMEM((blocks, chan_n, rows, 2 * span), f32),
                pltpu.VMEM((tm, rows, chans), f32),
                pltpu.VMEM((cs_n, out_rows, tile), f32),
                pltpu.VMEM((cs_n, rows, 2 * chans), f32),
                pltpu.VMEM((blocks, rows, LANES), f32),
                pltpu.VMEM((2, out_rows, span), f32),
                pltpu.VMEM((cs_n, out_rows, tile), f32),
                pltpu.VMEM((2, out_rows, tile), f32),
                dma((n * tm,)), dma((n * tm,)), dma((n * tm,)),
                dma((2, n * tm // 2)), dma((blocks, cs_n, n // 2)),
                dma(()), dma((blocks, chan_n)),
                dma((PIECES,)), dma((group_n, PIECES)), dma((group_n, PIECES)),
                dma((tm,)), dma((tm,)),
                dma((cs_n,)), dma((cs_n,)),
                dma(()), dma((cs_n,)),
                dma((tm,)), dma((blocks,)),
                dma((2,)),
                dma((3,)),
            ],
            compiler_params=pltpu.CompilerParams(collective_id=0, has_side_effects=True, vmem_limit_bytes=VMEM_LIMIT),
        )(*(pltpu.with_memory_space_constraint(a, pltpu.HBM)
            for a in (traces, templates, channel_mask)))

    placed = (
        P(("chan", "sub"), ("groups", "tm")),
        P("tm", ("chan", "sub"), None),
        P("tm", ("chan", "sub")),
    )
    return jax.shard_map(
        on_device,
        mesh=mesh,
        in_specs=placed,
        out_specs=P(("chan", "sub"), ("groups", "tm")),
        check_vma=False,
    )
```

```python
import functools

import jax
import jax.numpy as jnp
from jax import lax
from jax.experimental import pallas as pl
from jax.experimental.pallas import tpu as pltpu
from jax.sharding import PartitionSpec as P

EPSILON = 1e-06
MESH = pl.DeviceIdType.MESH
LANES = 128
FINE = 32
NT = (((1,), (1,)), ((), ()))
PIECES = 2
VMEM_LIMIT = 32 * 1024 * 1024


def is_outer(z, half):
    return (z % 2 == 0) == (z < half)


def kernel(sizes, x_hbm, w_hbm, m_hbm, o_ref, x_ref, w_ref, m_ref, xt, af, ab, acc, rb, rx, mk, pb, tp, fp, eh, es, ew,
           recv_sem, right_sem, left_sem, out_sem, in_sem, extra_sem,
           extrain_sem, wave_sem,
           wavein_sem, pass_sem, mask_sem, maskin_sem,
           pow_sem, powin_sem, te_sem, tein_sem, fac_sem, facin_sem, head_sem, load_sem):
    group_n, tm, chan_n, sub_n = sizes
    cs_n = chan_n * sub_n
    me = lax.axis_index("tm")
    my_chan = lax.axis_index("chan")
    my_sub = lax.axis_index("sub")
    my_cs = my_chan * sub_n + my_sub
    chans, tile = x_ref.shape
    rows, _, span = w_ref.shape
    blocks = tm // cs_n
    coarse = span // FINE
    total = tm * tile
    n = tile // span
    owner = me // blocks
    first = me * n
    my_group = lax.axis_index("groups")
    depth = FINE * rows
    piece = depth // (group_n * PIECES)
    half = tm // 2
    partner = me + 1 - 2 * lax.rem(me, 2)
    moves = my_sub == 0
    outer = is_outer(me, half)
    gives = jnp.logical_and(outer, moves)
    takes = jnp.logical_and(jnp.logical_not(outer), moves)
    low_end = jnp.where(moves, 1, 0)
    high_end = tm - 1 - low_end
    pair = 2 * span
    pairs = tile // pair
    switch = pairs

    def remote(src, dst, send, recv, to):
        return pltpu.make_async_remote_copy(
            src_ref=src, dst_ref=dst, send_sem=send, recv_sem=recv,
            device_id=to, device_id_type=MESH)

    def peer(d):
        return {"tm": lax.rem(me + d, tm)}

    def cs_place(c):
        return {"chan": c // sub_n, "sub": c % sub_n}

    loads = [pltpu.make_async_copy(src, dst, load_sem.at[i]) for i, (src, dst) in enumerate(
        ((m_hbm, m_ref), (x_hbm, x_ref), (w_hbm, w_ref)))]
    for load in loads:
        load.start()

    barrier = pltpu.get_barrier_semaphore()
    for d in range(1, tm):
        pl.semaphore_signal(barrier, inc=1, device_id=peer(d), device_id_type=MESH)
    for d in range(1, cs_n):
        pl.semaphore_signal(barrier, inc=1, device_id=cs_place(lax.rem(my_cs + d, cs_n)),
                            device_id_type=MESH)

    for d in range(1, group_n):
        pl.semaphore_signal(barrier, inc=1, device_id={"groups": lax.rem(my_group + d, group_n)},
                            device_id_type=MESH)

    loads[0].wait()
    mask = m_ref[...].astype(jnp.float32)
    mk[me] = mask
    loads[1].wait()
    xt[pl.ds(me * tile, tile), :] = jnp.transpose(x_ref[...])
    loads[2].wait()
    for k in range(rows):
        wave = jnp.transpose(w_ref[k].astype(jnp.float32)) * mask[k : k + 1, :]
        tp[my_cs, k : k + 1, 0:chans] = jnp.sum(wave * wave, axis=0, keepdims=True)
        for g in range(coarse):
            af[g, pl.ds(k, FINE, stride=rows), :] = wave[g * FINE : (g + 1) * FINE, :]
    for g in range(coarse):
        ab[0:depth, g * chans : (g + 1) * chans] = af[g].astype(jnp.bfloat16)
    tp[my_cs, :, chans : 2 * chans] = mask

    pl.semaphore_wait(barrier, tm - 1 + cs_n - 1 + group_n - 1)

    def mask_copy(d):
        return remote(mk.at[me], mk.at[me], mask_sem.at[d], maskin_sem.at[me], peer(d))

    for d in range(1, tm):
        mask_copy(d).start()

    def wave_copy(p, to):
        at = (my_group * PIECES + p) * piece
        return remote(ab.at[pl.ds(pl.multiple_of(at, piece), piece), :],
                      ab.at[pl.ds(pl.multiple_of(depth + at, piece), piece), :],
                      wave_sem.at[p], wavein_sem.at[my_group, p], {"tm": to})

    def pass_copy(p, d):
        at = pl.ds(pl.multiple_of(depth + (my_group * PIECES + p) * piece, piece), piece)
        return remote(ab.at[at, :], ab.at[at, :], pass_sem.at[d, p], wavein_sem.at[my_group, p],
                      {"groups": lax.rem(my_group + d, group_n)})

    @pl.when(gives)
    def _():
        for p in range(PIECES):
            wave_copy(p, partner).start()

    def relay(c, to, sem):
        part = pl.ds(pl.multiple_of(c * span, span), span)
        return remote(xt.at[part, :], xt.at[part, :], sem.at[c], recv_sem.at[c], {"tm": to})

    def send_own():
        for k in range(n):
            @pl.when(me < tm - 1)
            def _():
                relay(first + n - 1 - k, me + 1, right_sem).start()

            @pl.when(me > 0)
            def _():
                relay(first + k, me - 1, left_sem).start()

    send_own()

    def te_copy():
        return remote(tp.at[my_cs], tp.at[my_cs], te_sem, tein_sem.at[my_cs], cs_place(owner))

    @pl.when(my_cs != owner)
    def _():
        te_copy().start()

    acc[...] = jnp.zeros_like(acc)

    def spread(p):
        width = p.shape[1]
        pad = jnp.zeros((rows, LANES), jnp.float32)
        out = jnp.concatenate([pad, p[:rows]], 1)
        for b in range(1, FINE):
            one = jnp.concatenate([pad, p[b * rows : (b + 1) * rows]], 1)
            out = out + pltpu.roll(one, width + LANES - b, 1)
        return out

    def add_products(slots, right, start, before):
        for slot in slots:
            out = spread(lax.dot_general(ab[slot * depth : (slot + 1) * depth, :], right, NT,
                                         preferred_element_type=jnp.float32))
            acc[slot, :, pl.ds(before, LANES)] += out[:, :LANES]
            acc[slot, :, pl.ds(start, right.shape[0])] += out[:, LANES:]

    def process(c, width, slots):
        start = pl.multiple_of(c * span, span)
        before = pl.multiple_of(lax.rem(start + total - LANES, total), LANES)
        right = jnp.concatenate(
            [xt[pl.ds(pl.multiple_of(start + FINE * g, FINE), width), :] for g in range(coarse)],
            1)
        add_products(slots, right, start, before)

    def own(slots):
        process(first, tile - span, slots)

    def close(wide, slots):
        xt[total : total + span, :] = xt[0:span, :]
        start = total - wide
        right = jnp.concatenate(
            [xt[pl.ds(start + FINE * g, wide), :] for g in range(coarse)], 1)
        for slot in slots:
            out = spread(lax.dot_general(ab[slot * depth : (slot + 1) * depth, :], right, NT,
                                         preferred_element_type=jnp.float32))
            acc[slot, :, pl.ds(start - LANES, LANES)] += out[:, :LANES]
            for k in range(wide // span):
                at = start + k * span
                low = LANES + k * span
                acc[slot, :, pl.ds(at, span)] += out[:, low : low + span]

    def block_of(slot):
        return partner if slot else me

    def holder(slot):
        return block_of(slot) // blocks

    def columns(o):
        return pl.ds(pl.multiple_of(o * pair, pair), pair)

    def out_copy(o, slot):
        q = block_of(slot) % blocks
        return remote(acc.at[slot, :, columns(o)], rb.at[q, my_cs, :, columns(lax.rem(o, pairs))],
                      out_sem.at[slot, o], in_sem.at[q, my_cs, lax.rem(o, pairs)],
                      {"tm": o // pairs, **cs_place(holder(slot))})

    def extra_copy(o, slot):
        q = block_of(slot) % blocks
        return remote(acc.at[slot, :, columns(o)], rx.at[q, my_chan],
                      extra_sem, extrain_sem.at[q, my_chan],
                      {"tm": o // pairs, **cs_place(holder(slot))})

    def is_local(o, slot):
        return jnp.logical_and(o // pairs == me, my_cs == holder(slot))

    def hand(o, slot):
        @pl.when(is_local(o, slot))
        def _():
            rb[block_of(slot) % blocks, my_cs, :, columns(lax.rem(o, pairs))] = (
                acc[slot, :, columns(o)])

        @pl.when(jnp.logical_not(is_local(o, slot)))
        def _():
            out_copy(o, slot).start()

    def hand_extra(o, slot):
        @pl.when(is_local(o, slot))
        def _():
            rx[block_of(slot) % blocks, my_chan] = acc[slot, :, columns(o)]

        @pl.when(jnp.logical_not(is_local(o, slot)))
        def _():
            extra_copy(o, slot).start()

    home = me * pairs
    low = me - lax.rem(me, 2)
    pair_last = (low + 2) * pairs - 1
    before_pair = lax.rem(low * pairs + tm * pairs - 1, tm * pairs)

    def hand_first(o):
        hand(o, 0)

    def hand_second(o):
        @pl.when(o == pair_last)
        def _():
            hand_extra(o, 1)

        @pl.when(o != pair_last)
        def _():
            hand(o, 1)

    def pow_copy(d):
        to = lax.rem(my_cs + d, cs_n)
        return remote(es.at[to], pb.at[my_cs], pow_sem.at[d], powin_sem.at[my_cs], cs_place(to))

    def power():
        for d in range(1, tm):
            who = lax.rem(me + d, tm)
            remote(mk.at[who], mk.at[who], mask_sem.at[0], maskin_sem.at[who],
                   {"tm": who}).wait_recv()
        masks = jnp.concatenate([mk[i] for i in range(tm)], 0).astype(jnp.bfloat16)
        x32 = xt[pl.ds(me * tile, tile), :].astype(jnp.float32)
        square = x32 * x32
        high = square.astype(jnp.bfloat16)
        low = (square - high.astype(jnp.float32)).astype(jnp.bfloat16)
        p = lax.dot_general(jnp.concatenate([masks, masks], 1), jnp.concatenate([high, low], 1),
                            NT, preferred_element_type=jnp.float32)
        for c in range(cs_n):
            es[c] = p[c * blocks * rows : (c + 1) * blocks * rows, :]
        pb[my_cs] = es[my_cs]
        for d in range(1, cs_n):
            pow_copy(d).start()

    def fac_copy(d):
        return remote(fp.at[me % blocks], fp.at[me % blocks], fac_sem.at[d],
                      facin_sem.at[me % blocks], peer(d))

    def template_sums():
        @pl.when(my_cs == owner)
        def _():
            for d in range(1, cs_n):
                who = lax.rem(my_cs + d, cs_n)
                remote(tp.at[who], tp.at[who], te_sem, tein_sem.at[who], cs_place(who)).wait_recv()
            t = tp[0]
            for c in range(1, cs_n):
                t = t + tp[c]
            te = jnp.sum(t[:, :chans], axis=1, keepdims=True)
            active = jnp.sum(t[:, chans:], axis=1, keepdims=True)
            lane = lax.broadcasted_iota(jnp.int32, (rows, LANES), 1)
            fp[me % blocks] = jnp.where(lane < LANES // 2, te, active)
            for d in range(1, tm):
                fac_copy(d).start()

    def head_copy():
        return remote(eh.at[0], eh.at[1], head_sem.at[0], head_sem.at[1],
                      {"tm": lax.rem(me + tm - 1, tm)})

    def windows():
        for d in range(1, cs_n):
            who = lax.rem(my_cs + d, cs_n)
            remote(es.at[who], pb.at[who], pow_sem.at[0], powin_sem.at[who],
                   cs_place(who)).wait_recv()
        p = pb[0]
        for c in range(1, cs_n):
            p = p + pb[c]
        p = jnp.concatenate([jnp.zeros((blocks * rows, span), jnp.float32), p], 1)
        by = 1
        while by < span:
            p = p + pltpu.roll(p, tile + span - by, 1)
            by *= 2
        eh[0] = p[:, :span]
        head_copy().start()
        ew[0] = p[:, span:]

    def norms():
        head_copy().wait_recv()
        for q in range(blocks):
            j = my_cs * blocks + q

            @pl.when(me != j)
            def _():
                remote(fp.at[q], fp.at[q], fac_sem.at[0], facin_sem.at[q], {"tm": j}).wait_recv()

            at = slice(q * rows, (q + 1) * rows)
            factor = jnp.sqrt(span * fp[q, :, LANES - 1 : LANES])
            energy = jnp.concatenate(
                [ew[0, at, : tile - span], ew[0, at, tile - span :] + eh[1, at, :]], 1)
            ew[1, at, :] = factor / jnp.sqrt(energy * fp[q, :, 0:1] + EPSILON)

    left_n = pairs * jnp.where(jnp.logical_and(moves, me == tm - 1), 1, me)
    right_n = pairs * jnp.where(jnp.logical_and(moves, me == 0), 1, tm - 1 - me)
    short = jnp.minimum(left_n, right_n)
    left_short = left_n < right_n
    steps = pairs * (tm - 1)

    def arrival(u):
        v = u - switch
        paired = u < 2 * short
        on_short = jnp.where(takes, jnp.logical_and(v >= 0, v < short),
                             jnp.logical_and(paired, lax.rem(u, 2) == 0))
        k = jnp.where(takes, jnp.where(v < 0, u, jnp.where(on_short, v, u - short)),
                      jnp.where(paired, u // 2, u - short))
        from_left = on_short == left_short
        return from_left, jnp.where(from_left, home - 1 - k, home + pairs + k)

    def made(u):
        from_left, o = arrival(u)
        return jnp.where(from_left, 2 * o, 2 * o - 1)

    def ended(u):
        from_left, o = arrival(u)
        return jnp.where(from_left, o, o - 1)

    own((0,))
    for o in range(pairs - 1):
        @pl.when(jnp.logical_not(jnp.logical_and(gives, lax.rem(me, 2) == 1)))
        def _():
            hand(home + o, 0)

    power()

    def step(u, final):
        live = u < left_n + right_n
        from_left, o = arrival(u)
        per = PIECES // switch

        @pl.when(jnp.logical_and(takes, u < switch))
        def _():
            for i in range(per):
                p = jnp.minimum(u, switch - 1) * per + i
                remote(ab.at[pl.ds(0, piece), :], ab.at[pl.ds(0, piece), :], wave_sem.at[0],
                       wavein_sem.at[my_group, p], {"tm": partner}).wait_recv()
                for d in range(1, group_n):
                    pass_copy(p, d).start()

        @pl.when(jnp.logical_and(live, from_left))
        def _():
            for i in (1, 0):
                relay(2 * o + i, me, right_sem).wait_recv()

                @pl.when(me < high_end)
                def _():
                    relay(2 * o + i, me + 1, right_sem).start()

        @pl.when(jnp.logical_and(live, jnp.logical_not(from_left)))
        def _():
            for i in (0, 1):
                relay(2 * o + i, me, left_sem).wait_recv()

                @pl.when(me > low_end)
                def _():
                    relay(2 * o + i, me - 1, left_sem).start()

        @pl.when(jnp.logical_and(takes, u == switch + 1))
        def _():
            for d in range(1, group_n):
                who = lax.rem(my_group + d, group_n)
                for p in range(PIECES):
                    remote(ab.at[pl.ds(0, piece), :], ab.at[pl.ds(0, piece), :], wave_sem.at[0],
                           wavein_sem.at[who, p], {"groups": who}).wait_recv()

        both = jnp.logical_and(takes, u >= switch + pairs)
        if final:
            for slots, mine in (((0, 1), takes), ((0,), jnp.logical_not(moves))):
                @pl.when(jnp.logical_and(mine, from_left))
                def _():
                    process(made(u), pair, slots)
                    for slot in slots:
                        (hand_second if slot else hand_first)(ended(u))
                    close(span, slots)

                @pl.when(jnp.logical_and(mine, jnp.logical_not(from_left)))
                def _():
                    close(pair + span, slots)
                    for slot in slots:
                        (hand_second if slot else hand_first)(ended(u))

                @pl.when(mine)
                def _():
                    for slot in slots:
                        (hand_second if slot else hand_first)(tm * pairs - 1)

            @pl.when(gives)
            def _():
                for o in range(2 * pairs):
                    at = low * pairs + o

                    @pl.when(jnp.logical_or(lax.rem(me, 2) == 1, o >= pairs - 1))
                    def _():
                        hand(at, 0)
                hand_extra(before_pair, 0)

            return

        @pl.when(jnp.logical_or(
            jnp.logical_and(gives, jnp.logical_and(live, o // pairs == partner)),
            jnp.logical_and(jnp.logical_not(gives), jnp.logical_not(jnp.logical_or(
                both, jnp.logical_and(takes, u == switch + 1))))))
        def _():
            process(made(u), pair, (0,))

        @pl.when(jnp.logical_and(takes, u == switch + 1))
        def _():
            process(made(u), pair, (0,))
            process(jnp.minimum(made(0), made(switch - 1)), switch * pair, (1,))
            for v in range(switch):
                hand_second(ended(v))

        @pl.when(both)
        def _():
            process(made(u), pair, (0, 1))
            hand_second(ended(u))

        hold = jnp.where(takes, switch, steps - 2)

        @pl.when(jnp.logical_and(jnp.logical_not(gives), u >= hold))
        def _():
            def hand_on(v, carry):
                hand(ended(v), 0)
                return carry

            lax.fori_loop(jnp.where(u == hold, 0, u), u + 1, hand_on, 0)

        @pl.when(u == jnp.where(moves, 0, 3))
        def _():
            template_sums()

        @pl.when(u == jnp.where(moves, 0, 3))
        def _():
            windows()

    def loop(u, carry):
        step(u, False)
        return carry

    lax.fori_loop(0, steps - 1, loop, 0)
    step(steps - 1, True)

    norms()

    def finish(c, carry):
        @pl.when(jnp.logical_or(jnp.logical_and(me < high_end, c // n < me),
                                jnp.logical_and(me < tm - 1, c // n == me)))
        def _():
            relay(c, me, right_sem).wait_send()

        @pl.when(jnp.logical_or(jnp.logical_and(me > low_end, c // n > me),
                                jnp.logical_and(me > 0, c // n == me)))
        def _():
            relay(c, me, left_sem).wait_send()

        return carry

    lax.fori_loop(0, n * tm, finish, 0)

    def finish_out(o, carry):
        in_pair = o // (2 * pairs) == me // 2

        @pl.when(jnp.logical_and(jnp.logical_or(jnp.logical_not(gives), in_pair),
                                 jnp.logical_not(is_local(o, 0))))
        def _():
            out_copy(o, 0).wait_send()

        @pl.when(jnp.logical_and(jnp.logical_and(takes, jnp.logical_not(in_pair)),
                                 jnp.logical_not(is_local(o, 1))))
        def _():
            out_copy(o, 1).wait_send()

        return carry

    lax.fori_loop(0, pairs * tm, finish_out, 0)

    @pl.when(jnp.logical_and(gives, jnp.logical_not(is_local(before_pair, 0))))
    def _():
        extra_copy(before_pair, 0).wait_send()

    @pl.when(jnp.logical_and(takes, jnp.logical_not(is_local(pair_last, 1))))
    def _():
        extra_copy(pair_last, 1).wait_send()
    for p in range(PIECES):
        @pl.when(gives)
        def _():
            wave_copy(p, partner).wait_send()

        @pl.when(takes)
        def _():
            for d in range(1, group_n):
                pass_copy(p, d).wait_send()

    for d in range(1, tm):
        mask_copy(d).wait_send()
    for d in range(1, cs_n):
        pow_copy(d).wait_send()

    @pl.when(my_cs != owner)
    def _():
        te_copy().wait_send()

    @pl.when(my_cs == owner)
    def _():
        for d in range(1, tm):
            fac_copy(d).wait_send()

    head_copy().wait_send()

    for q in range(blocks):
        b = my_cs * blocks + q
        b_outer = is_outer(b, half)
        for slot in range(cs_n):
            moved = slot % sub_n == 0
            inner = b + 1 - 2 * lax.rem(b, 2)
            apart = jnp.logical_and(b_outer, me // 2 != b // 2)
            source = jnp.where(apart, inner, b) if moved else b

            @pl.when(jnp.logical_not(jnp.logical_and(my_cs == slot, source == me)))
            def _():
                for k in range(pairs):
                    remote(acc.at[0, :, pl.ds(0, pair)],
                           rb.at[q, slot, :, pl.ds(k * pair, pair)], out_sem.at[0, 0],
                           in_sem.at[q, slot, k], {"tm": lax.rem(me + 1, tm)}).wait_recv()

        at = slice(q * rows, (q + 1) * rows)
        result = rb[q, 0]
        for c in range(1, cs_n):
            result = result + rb[q, c]
        b_low = b - lax.rem(b, 2)
        tail = jnp.logical_and(b_outer, me == b_low + 1)
        ahead = jnp.logical_and(b_outer, me == lax.rem(b_low + tm - 1, tm))
        for c in range(chan_n):
            source = jnp.where(me == b_low + 1, inner, b)
            near_me = jnp.logical_and(jnp.logical_and(my_sub == 0, my_chan == c), source == me)

            @pl.when(jnp.logical_and(jnp.logical_or(tail, ahead), jnp.logical_not(near_me)))
            def _():
                remote(acc.at[0, :, pl.ds(0, pair)], rx.at[q, c], out_sem.at[0, 0],
                       extrain_sem.at[q, c], {"tm": lax.rem(me + 1, tm)}).wait_recv()

        o_ref[at, :] = result * ew[1, at, :]

        @pl.when(jnp.logical_or(tail, ahead))
        def _():
            more = rx[q, 0]
            for c in range(1, chan_n):
                more = more + rx[q, c]
            whole = slice(tile - pair, tile)
            o_ref[at, whole] = (result[:, whole] + more) * ew[1, at, whole]


def solution(mesh):
    group_n, tm, chan_n, sub_n = (mesh.shape[a] for a in ("groups", "tm", "chan", "sub"))
    cs_n = chan_n * sub_n
    blocks = tm // cs_n

    def on_device(traces, templates, channel_mask):
        chans, tile = traces.shape
        rows, _, span = templates.shape
        coarse = span // FINE
        total = tm * tile
        n = tile // span
        out_rows = blocks * rows
        vmem = pl.BlockSpec(memory_space=pltpu.VMEM)
        f32, bf16 = jnp.float32, jnp.bfloat16
        dma = pltpu.SemaphoreType.DMA
        return pl.pallas_call(
            functools.partial(kernel, (group_n, tm, chan_n, sub_n)),
            out_shape=jax.ShapeDtypeStruct((out_rows, tile), f32),
            in_specs=[pl.BlockSpec(memory_space=pltpu.HBM)] * 3,
            out_specs=vmem,
            scratch_shapes=[
                pltpu.VMEM((chans, tile), bf16),
                pltpu.VMEM((rows, chans, span), bf16),
                pltpu.VMEM((rows, chans), jnp.int32),
                pltpu.VMEM((total + span, chans), bf16),
                pltpu.VMEM((coarse, FINE * rows, chans), f32),
                pltpu.VMEM((2 * FINE * rows, coarse * chans), bf16),
                pltpu.VMEM((2, rows, total), f32),
                pltpu.VMEM((blocks, cs_n, rows, tile), f32),
                pltpu.VMEM((blocks, chan_n, rows, 2 * span), f32),
                pltpu.VMEM((tm, rows, chans), f32),
                pltpu.VMEM((cs_n, out_rows, tile), f32),
                pltpu.VMEM((cs_n, rows, 2 * chans), f32),
                pltpu.VMEM((blocks, rows, LANES), f32),
                pltpu.VMEM((2, out_rows, span), f32),
                pltpu.VMEM((cs_n, out_rows, tile), f32),
                pltpu.VMEM((2, out_rows, tile), f32),
                dma((n * tm,)), dma((n * tm,)), dma((n * tm,)),
                dma((2, n * tm // 2)), dma((blocks, cs_n, n // 2)),
                dma(()), dma((blocks, chan_n)),
                dma((PIECES,)), dma((group_n, PIECES)), dma((group_n, PIECES)),
                dma((tm,)), dma((tm,)),
                dma((cs_n,)), dma((cs_n,)),
                dma(()), dma((cs_n,)),
                dma((tm,)), dma((blocks,)),
                dma((2,)),
                dma((3,)),
            ],
            compiler_params=pltpu.CompilerParams(collective_id=0, has_side_effects=True, vmem_limit_bytes=VMEM_LIMIT),
        )(*(pltpu.with_memory_space_constraint(a, pltpu.HBM)
            for a in (traces, templates, channel_mask)))

    placed = (
        P(("chan", "sub"), ("groups", "tm")),
        P("tm", ("chan", "sub"), None),
        P("tm", ("chan", "sub")),
    )
    return jax.shard_map(
        on_device,
        mesh=mesh,
        in_specs=placed,
        out_specs=P(("chan", "sub"), ("groups", "tm")),
        check_vma=False,
    )
```
